32 devices in a mesh: dp: 8 (over y, x, core), tensor: 4 (over z).
Axes of the slice: x: 2, y: 2, z: 4, core: 2. Of those that a mesh axis runs over, the one named last changes fastest.
Arguments:
- tokens: bfloat16 [16384, 768], P('dp'), may hold values from -6 to 6
- doc_lengths: int32 [16, 8], P('dp'), may hold values from 1 to 512, 1024 in all within a row
- wq: bfloat16 [768, 768], P('dp', 'tensor'), may hold values from -0.21875 to 0.21875
- bq: float32 [768], P('tensor'), may hold values from -3 to 3
- wk: bfloat16 [768, 768], P('dp', 'tensor'), may hold values from -0.21875 to 0.21875
- wv: bfloat16 [768, 768], P('dp', 'tensor'), may hold values from -0.21875 to 0.21875
- bv: float32 [768], P('tensor'), may hold values from -3 to 3
- wo: bfloat16 [768, 768], P('tensor', 'dp'), may hold values from -0.875 to 0.875
- bo: float32 [768], replicated, may hold values from -3 to 3
- gain1: float32 [768], replicated, may hold values from 0.25 to 1.75
- shift1: float32 [768], replicated, may hold values from -3 to 3
- w1: bfloat16 [768, 3072], P('dp', 'tensor'), may hold values from -0.21875 to 0.21875
- b1: float32 [3072], P('tensor'), may hold values from -3 to 3
- w2: bfloat16 [3072, 768], P('tensor', 'dp'), may hold values from -0.109375 to 0.109375
- b2: float32 [768], replicated, may hold values from -3 to 3
- gain2: float32 [768], replicated, may hold values from 0.25 to 1.75
- shift2: float32 [768], replicated, may hold values from -3 to 3
- cotangent: bfloat16 [16384, 768], P('dp'), may hold values from -6 to 6
Outputs:
- out: bfloat16 [16384, 768], P('dp')
- grad_tokens: bfloat16 [16384, 768], P('dp')
- grad_wq: float32 [768, 768], P('dp', 'tensor')
- grad_bq: float32 [768], P('tensor')
- grad_wk: float32 [768, 768], P('dp', 'tensor')
- grad_wv: float32 [768, 768], P('dp', 'tensor')
- grad_bv: float32 [768], P('tensor')
- grad_wo: float32 [768, 768], P('tensor', 'dp')
- grad_bo: float32 [768], replicated
- grad_gain1: float32 [768], replicated
- grad_shift1: float32 [768], replicated
- grad_w1: float32 [768, 3072], P('dp', 'tensor')
- grad_b1: float32 [3072], P('tensor')
- grad_w2: float32 [3072, 768], P('tensor', 'dp')
- grad_b2: float32 [768], replicated
- grad_gain2: float32 [768], replicated
- grad_shift2: float32 [768], replicated
The draws below stay inside these ranges and needn't reach their ends.
Inputs may be any that keep to these rules, and one draw needn't show every extreme that they name: `doc_lengths`: row s holds the lengths of the documents packed in order into sequence s; each row sums to 1024.
All inputs are finite; a program needn't handle non-finite values.
Results may differ from the reference program's by a relative error of at most 0.02.
Values may be sent and summed in bfloat16 or wider, within the bound.
A program may use at most 192 MiB of HBM per device.

```python
import math
import jax
import jax.numpy as jnp
import numpy as np
from jax import lax

D = 768
HEADS = 12
HD = 64
FF = 3072
SEQ_LEN = 1024
DOCS = 8
SEQS = 16
TOKENS = 16384
N_TENSOR = 4


def spiked(array, rng, source, target, blocks, factor):
    owner, partner = [(jnp.arange(array.shape[dim]) // (array.shape[dim] // blocks)).reshape([-1 if axis == dim else 1 for axis in range(array.ndim)]) for dim in (source, target)]
    chosen = jax.random.permutation(rng, blocks)[partner]
    strong = (owner == chosen) | (owner == (partner + blocks // 2) % blocks)
    return jnp.where(strong, factor * array, array)


def block_levels(stream_key, extent, cuts, smallest, top_value):
    loudness, own = 1.0, jax.random.fold_in(stream_key, 6)
    for dim, shards_of in cuts:
        steps = jnp.exp(jax.random.uniform(jax.random.fold_in(own, dim), (shards_of,), jnp.float32, smallest / len(cuts), top_value / len(cuts)))
        loudness = loudness * jnp.repeat(steps, extent[dim] // shards_of).reshape([-1 if axis == dim else 1 for axis in range(len(extent))])
    return loudness


def profile(count, total, most, skew):
    loads = [(1 << 20) // math.isqrt(rank ** skew) + 1 for rank in range(2, count + 1)]
    rest, holding = total - most - (count - 1), [1] * (count - 1)
    while rest > 0:
        candidates = [i for i in range(count - 1) if holding[i] < most]
        pool, left = sum([loads[i] for i in candidates]), rest
        for i in candidates:
            extra = min(most - holding[i], max(1, left * loads[i] // pool), rest)
            holding[i] = holding[i] + extra
            rest = rest - extra
    return np.array([most] + holding)


def uneven(rng, amount, total, most, lean):
    if amount == 2:
        one = jax.random.randint(rng, (), max(1, total - most), min(most, total - 1) + 1)
        return jnp.stack([one, total - one])
    tallies = jnp.asarray(profile(amount, total, most, lean), jnp.int32)
    pairs = (amount - 1) // 2
    giver, receiver = tallies[1:1 + 2 * pairs:2], tallies[2:2 + 2 * pairs:2]
    room = jnp.minimum(giver - 1, most - receiver)
    moved = jax.random.randint(jax.random.fold_in(rng, 1), (pairs,), 0, 1 << 20) % (room + 1)
    tallies = tallies.at[1:1 + 2 * pairs:2].set(giver - moved).at[2:2 + 2 * pairs:2].set(receiver + moved)
    return tallies[jax.random.permutation(jax.random.fold_in(rng, 2), amount)]


def normal_values(own_key, dims, scale, limit, shards=(), held_as=jnp.bfloat16):
    array = scale * jax.random.normal(own_key, dims, jnp.float32)
    if shards:
        array = array * block_levels(own_key, dims, shards, -0.22, 0.18)
    return jnp.clip(array, -limit, limit).astype(held_as)


def heavy_noise(own_key, shape, scale, reach, cuts, heavy, kind=jnp.bfloat16):
    values = scale * jax.random.normal(own_key, shape, jnp.float32)
    if cuts:
        values = values * block_levels(own_key, shape, cuts, -0.22, 0.18)
    return jnp.clip(spiked(values, jax.random.fold_in(own_key, 3), *heavy), -reach, reach).astype(kind)


def setup_inputs(seed: int = 0) -> dict:
    key_list = jax.random.split(jax.random.key(seed), 19)
    return {
        "tokens": heavy_noise(key_list[0], (TOKENS, D), 1.0, 6.0, ((0, 8),), (0, 1, 8, 2.0)),
        "doc_lengths": jax.vmap(lambda own: uneven(own, DOCS, SEQ_LEN, SEQ_LEN // 2, 2))(jax.random.split(key_list[1], SEQS)).reshape((SEQS, DOCS)).astype(jnp.int32),
        "wq": normal_values(key_list[2], (D, D), D ** -0.5, 0.21875, ((0, 8), (1, 4))),
        "bq": normal_values(key_list[3], (D,), 0.5, 3.0, ((0, 4),), jnp.float32),
        "wk": normal_values(key_list[4], (D, D), D ** -0.5, 0.21875, ((0, 8), (1, 4))),
        "wv": normal_values(key_list[5], (D, D), D ** -0.5, 0.21875, ((0, 8), (1, 4))),
        "bv": normal_values(key_list[6], (D,), 0.5, 3.0, ((0, 4),), jnp.float32),
        "wo": normal_values(key_list[7], (D, D), (D // 16) ** -0.5, 0.875, ((0, 4), (1, 8))),
        "bo": normal_values(key_list[8], (D,), 0.5, 3.0, (), jnp.float32),
        "gain1": jnp.clip(1.0 + 0.15 * jax.random.normal(key_list[9], (D,), jnp.float32), 0.25, 1.75),
        "shift1": normal_values(key_list[10], (D,), 0.5, 3.0, (), jnp.float32),
        "w1": normal_values(key_list[11], (D, FF), D ** -0.5, 0.21875, ((0, 8), (1, 4))),
        "b1": normal_values(key_list[12], (FF,), 0.5, 3.0, ((0, 4),), jnp.float32),
        "w2": normal_values(key_list[13], (FF, D), FF ** -0.5, 0.109375, ((0, 4), (1, 8))),
        "b2": normal_values(key_list[14], (D,), 0.5, 3.0, (), jnp.float32),
        "gain2": jnp.clip(1.0 + 0.15 * jax.random.normal(key_list[15], (D,), jnp.float32), 0.25, 1.75),
        "shift2": normal_values(key_list[16], (D,), 0.5, 3.0, (), jnp.float32),
        "cotangent": heavy_noise(key_list[17], (TOKENS, D), 1.0, 6.0, ((0, 8),), (0, 1, 8, 2.0)),
    }


@jax.custom_vjp
def low(v):
    return lax.optimization_barrier(v.astype(jnp.bfloat16)).astype(jnp.float32)

@jax.custom_vjp
def low_back(v):
    return v

def low_keep(v):
    return (low(v), None)

def low_pass(kept, grad):
    return (grad,)

def back_keep(v):
    return (v, None)

def back_low(kept, grad):
    return (low(grad),)
low.defvjp(low_keep, low_pass)
low_back.defvjp(back_keep, back_low)
eps_norm = 1e-12
masked_score = -1e+30

def doc_ids(lengths, count):
    ends = jnp.cumsum(lengths.astype(jnp.int32))
    places = jnp.arange(count, dtype=jnp.int32)
    return lax.optimization_barrier(jnp.sum((places[:, None] >= ends[None, :]).astype(jnp.int32), axis=1))

def layer_norm(total, gain, shift):
    centre = total - lax.optimization_barrier(jnp.mean(total, axis=-1, keepdims=True))
    spread = lax.optimization_barrier(jnp.mean(centre * centre, axis=-1, keepdims=True))
    return centre * lax.rsqrt(spread + eps_norm) * gain + shift

def split_sum(left, right, groups):
    count = left.shape[0]
    width = left.shape[1] // groups
    pieces = left.reshape(count, groups, width)
    blocks = right.reshape(groups, width, right.shape[1])
    terms = jnp.einsum('rpc,pcd->prd', pieces, blocks, precision=lax.Precision.HIGHEST)
    return lax.optimization_barrier(jnp.sum(low(terms), axis=0))

def layer(params, inputs, seg):
    wq, bq, wk, wv, bv, wo, bo, gain1, shift1, w1, b1, w2, b2, gain2, shift2 = params
    high = lax.Precision.HIGHEST
    count = inputs.shape[0]
    queries = low(low_back(jnp.dot(inputs, wq, precision=high) + bq)).reshape(count, HEADS, HD)
    keys = low(low_back(jnp.dot(inputs, wk, precision=high))).reshape(count, HEADS, HD)
    values = low(low_back(jnp.dot(inputs, wv, precision=high) + bv)).reshape(count, HEADS, HD)
    scores = low_back(jnp.einsum('qhd,khd->hqk', queries, keys, precision=high) * HD ** (-0.5))
    same_doc = seg[:, None] == seg[None, :]
    scores = jnp.where(same_doc[None], scores, masked_score)
    probs = jax.nn.softmax(scores, axis=-1)
    mixed = jnp.einsum('hqk,khd->qhd', low(probs), values, precision=high).reshape(count, D)
    mixed = low(low_back(mixed))
    attended = low_back(split_sum(mixed, wo, N_TENSOR))
    first = layer_norm(inputs + attended + bo, gain1, shift1)
    inner = low_back(jnp.dot(low(first), w1, precision=high) + b1)
    hidden = low(jax.nn.gelu(inner, approximate=False))
    second = low_back(split_sum(hidden, w2, N_TENSOR))
    return layer_norm(first + second + b2, gain2, shift2)

def reference(tokens, doc_lengths, wq, bq, wk, wv, bv, wo, bo, gain1, shift1, w1, b1, w2, b2, gain2, shift2, cotangent):
    params = tuple((entry.astype(jnp.float32) for entry in (wq, bq, wk, wv, bv, wo, bo, gain1, shift1, w1, b1, w2, b2, gain2, shift2)))
    inputs_all = tokens.astype(jnp.float32).reshape(SEQS, SEQ_LEN, D)
    cot_all = cotangent.astype(jnp.float32).reshape(SEQS, SEQ_LEN, D)

    def one_sequence(totals, item):
        inputs, cot, lengths = item
        seg = doc_ids(lengths, SEQ_LEN)
        result, pullback = jax.vjp(lambda weights, rows: layer(weights, rows, seg), params, inputs)
        grads, grad_rows = pullback(cot)
        totals = jax.tree.map(lambda left, right: left + right, totals, grads)
        return (totals, (result.astype(jnp.bfloat16), grad_rows.astype(jnp.bfloat16)))
    zeros = jax.tree.map(jnp.zeros_like, params)
    totals, (results, grad_rows) = lax.scan(one_sequence, zeros, (inputs_all, cot_all, doc_lengths))
    return (results.reshape(TOKENS, D), grad_rows.reshape(TOKENS, D), totals[0], totals[1], totals[2], totals[3], totals[4], totals[5], totals[6], totals[7], totals[8], totals[9], totals[10], totals[11], totals[12], totals[13], totals[14])
```

```python
from functools import partial
import jax
import jax.numpy as jnp
from jax import lax
from jax.experimental import pallas as pl
from jax.experimental.pallas import tpu as pltpu

from jax.sharding import PartitionSpec as P

BF = jnp.bfloat16
F32 = jnp.float32
EPS = 1e-12
HD = 64
NEG = -1e30
RB = 256


def nn(a, b):
    return jnp.dot(a, b, preferred_element_type=F32)


def nt(a, b):
    return lax.dot_general(a, b, (((1,), (1,)), ((), ())), preferred_element_type=F32)


def rows(r, n=RB):
    return pl.ds(pl.multiple_of(r * n, n), n)


def mean_last(x):
    return jnp.mean(x, axis=-1, keepdims=True)


def colsum(x):
    return jnp.sum(x, axis=0, keepdims=True)


def fb_scratch(T, W, F, D, L):
    M = L // 2
    WP = 256
    return [
        pltpu.VMEM((T, M, WP), BF),
        pltpu.VMEM((T, L, WP), BF),
        pltpu.VMEM((T, L, WP), BF),
        pltpu.VMEM((T, M, WP), BF),
        pltpu.VMEM((T, M, WP), BF),
        pltpu.VMEM((W, L), BF),
        pltpu.VMEM((W, M), F32),
        pltpu.VMEM((T * 4, 8, M), F32),
        pltpu.VMEM((L, M), F32),
        pltpu.VMEM((M, D), F32),
        pltpu.VMEM((M, 128), F32),
        pltpu.VMEM((M, D), BF),
        pltpu.VMEM((T, M, F), BF),
        pltpu.VMEM((T, M, F), BF),
        pltpu.VMEM((M, D), F32),
        pltpu.VMEM((M, D), F32),
        pltpu.VMEM((M, D), BF),
        pltpu.VMEM((D, M), BF),
        pltpu.VMEM((D, L), BF),
    ]


def fb_kernel(half_axis, W_, X, COT, SG, BIAS, NP, OUT, GTO, GTP, G, SM,
              q, k, v, mixed, dO, vT, oT, lse, bias, n1, r1, flow, hid, gp, sec, gz, low, lowT, xT):
    T = W_.shape[1]
    D = W_.shape[2]
    L = X.shape[0]
    M = L // 2
    W = D // T
    NH = W // HD
    c = half_axis
    own = c * M
    oth = (1 - c) * M
    scale = HD ** (-0.5)

    def ownrows(r):
        return pl.ds(pl.multiple_of(own + r * RB, RB), RB)

    def othrows(r):
        return pl.ds(pl.multiple_of(oth + r * RB, RB), RB)

    SM[...] = jnp.zeros_like(SM)
    key_doc = jnp.broadcast_to(SG[0:1, :], (128, L)).T
    for i in range(M // 128):
        query_doc = SG[0:1, pl.ds(pl.multiple_of(own + i * 128, 128), 128)]
        bias[:, i * 128:(i + 1) * 128] = jnp.where(key_doc == query_doc, 0.0, NEG)

    @pl.loop(0, T)
    def _(t):
        @pl.loop(0, L // RB)
        def _(r):
            xs = X[rows(r), :]
            k[t, rows(r), 0:W] = nn(xs, W_[0, t, :, W:2 * W]).astype(BF)
            v[t, rows(r), 0:W] = (nn(xs, W_[0, t, :, 2 * W:3 * W]) + BIAS[t, 2:3, 0:W]).astype(BF)

        @pl.loop(0, M // RB)
        def _(r):
            xs = X[ownrows(r), :]
            q[t, rows(r), 0:W] = (
                (nn(xs, W_[0, t, :, 0:W]) + BIAS[t, 1:2, 0:W]).astype(BF) * BF(scale)
            ).astype(BF)

    lane = lax.broadcasted_iota(jnp.int32, (1, 128), 1)

    def head(ref, t, rr, j):
        if j % 2 == 0 and j == NH - 1:
            return ref[t, rr, j * HD:(j + 1) * HD]
        p = j // 2
        return ref[t, rr, p * 128:(p + 1) * 128]

    def only(block, j):
        if block.shape[1] == HD:
            return block
        keep = (lane < HD) if j % 2 == 0 else (lane >= HD)
        return jnp.where(keep, block, jnp.zeros_like(block))

    everything = slice(None)
    QC = RB

    @pl.loop(0, T)
    def _(t):
        vT[...] = v[t, :, 0:W].T

        @pl.loop(0, M // QC)
        def _(i):
            qs = rows(i, QC)
            for j in range(NH):
                s = nt(head(k, t, everything, j), only(head(q, t, qs, j), j)) + bias[:, qs]
                m = jnp.max(s, axis=0, keepdims=True)
                p = jnp.exp(s - m)
                l = jnp.sum(p, axis=0, keepdims=True)
                lse[t * 4 + j, :, qs] = jnp.broadcast_to(m + jnp.log(l), (8, QC))
                o = nn(vT[j * HD:(j + 1) * HD, :], p.astype(BF))
                oT[j * HD:(j + 1) * HD, qs] = o * (1.0 / l)

        mixed[t, :, 0:W] = oT[...].T.astype(BF)

    @pl.loop(0, M // RB)
    def _(r):
        z = X[ownrows(r), :].astype(F32) + NP[0:1, :]
        for t in range(T):
            z = z + nt(mixed[t, rows(r), 0:W], W_[0, t, :, 3 * W:4 * W])
        cen = z - mean_last(z)
        rs = lax.rsqrt(mean_last(cen * cen) + EPS)
        n = cen * rs
        n1[rows(r), :] = n
        r1[rows(r), :] = jnp.broadcast_to(rs, (RB, 128))
        flow[rows(r), :] = (n * NP[1:2, :] + NP[2:3, :]).astype(BF)

    @pl.loop(0, T)
    def _(t):
        @pl.loop(0, M // RB)
        def _(r):
            rr = rows(r)
            inner = nn(flow[rr, :], W_[1, t]) + BIAS[t, 0:1, :]
            phi = 0.5 * (1.0 + lax.erf(inner * (2.0 ** -0.5)))
            h = (inner * phi).astype(BF)
            hid[t, rr, :] = h
            gp[t, rr, :] = (phi + inner * (jnp.exp(-0.5 * inner * inner) * 0.3989422804014327)).astype(BF)
            add = nt(h, W_[2, t])

            @pl.when(t == 0)
            def _():
                sec[rr, :] = add

            @pl.when(t > 0)
            def _():
                sec[rr, :] += add

    @pl.loop(0, M // RB)
    def _(r):
        rr = rows(r)
        z = n1[rr, :] * NP[1:2, :] + NP[2:3, :] + sec[rr, :] + NP[3:4, :]
        cen = z - mean_last(z)
        rs = lax.rsqrt(mean_last(cen * cen) + EPS)
        n = cen * rs
        OUT[rr, :] = (n * NP[4:5, :] + NP[5:6, :]).astype(BF)
        ct = COT[rr, :].astype(F32)
        g = ct * NP[4:5, :]
        g2 = rs * (g - mean_last(g) - n * mean_last(g * n))
        SM[16:17, :] += colsum(ct * n)
        SM[17:18, :] += colsum(ct)
        SM[13:14, :] += colsum(g2)
        gz[rr, :] = g2
        low[rr, :] = g2.astype(BF)

    lowT[...] = low[...].T

    @pl.loop(0, T)
    def _(t):
        @pl.loop(0, M // RB)
        def _(r):
            rr = rows(r)
            gi = (nn(low[rr, :], W_[2, t]) * gp[t, rr, :].astype(F32)).astype(BF)
            gp[t, rr, :] = gi
            SM[pl.ds(8 + t, 1), :] += colsum(gi.astype(F32))
            gz[rr, :] += nt(gi, W_[1, t])

        @pl.loop(0, D // RB)
        def _(r):
            G[2, t, rows(r), :] = nn(lowT[rows(r), :], hid[t]).astype(BF)

    lowT[...] = flow[...].T

    @pl.loop(0, T)
    def _(t):
        @pl.loop(0, D // RB)
        def _(r):
            G[1, t, rows(r), :] = nn(lowT[rows(r), :], gp[t]).astype(BF)

    @pl.loop(0, M // RB)
    def _(r):
        rr = rows(r)
        gf = gz[rr, :]
        n = n1[rr, :]
        g = gf * NP[1:2, :]
        g1 = r1[rr, 0:1] * (g - mean_last(g) - n * mean_last(g * n))
        SM[14:15, :] += colsum(gf * n)
        SM[15:16, :] += colsum(gf)
        SM[12:13, :] += colsum(g1)
        gz[rr, :] = g1
        low[rr, :] = g1.astype(BF)

    lowT[...] = low[...].T

    @pl.loop(0, T)
    def _(t):
        @pl.loop(0, M // RB)
        def _(r):
            dO[t, rows(r), 0:W] = nn(low[rows(r), :], W_[0, t, :, 3 * W:4 * W]).astype(BF)

        @pl.loop(0, D // RB)
        def _(r):
            G[0, t, rows(r), 3 * W:4 * W] = nn(lowT[rows(r), :], mixed[t, :, 0:W]).astype(BF)

    @pl.loop(0, T)
    def _(t):
        vT[...] = k[t, :, 0:W].T
        for pair in range((NH + 1) // 2):
            heads = [j for j in (2 * pair, 2 * pair + 1) if j < NH]
            wide = HD * len(heads)
            dk = jnp.zeros((L, wide), F32)
            dv = jnp.zeros((L, wide), F32)
            for j in heads:
                for i in range(M // QC):
                    qs = slice(i * QC, (i + 1) * QC)
                    qm = only(head(q, t, qs, j), j)
                    om = only(head(dO, t, qs, j), j)
                    s = nt(head(k, t, everything, j), qm) + bias[:, qs]
                    p = jnp.exp(s - lse[t * 4 + j, 0:1, qs])
                    dp = nt(head(v, t, everything, j), om)
                    cen = jnp.sum(p * dp, axis=0, keepdims=True)
                    ds = (p * (dp - cen)).astype(BF)
                    dv = dv + nn(p.astype(BF), om)
                    dk = dk + nn(ds, qm)
                    oT[j * HD:(j + 1) * HD, qs] = nn(vT[j * HD:(j + 1) * HD, :], ds) * scale
            lanes = slice(pair * 128, pair * 128 + wide)
            k[t, :, lanes] = dk.astype(BF)
            v[t, :, lanes] = dv.astype(BF)
        dq = oT[...].T.astype(BF)
        q[t, :, 0:W] = dq
        SM[pl.ds(t, 1), 0:W] += colsum(dq.astype(F32))
        SM[pl.ds(T + t, 1), 0:W] += colsum(v[t, :, 0:W].astype(F32))

    xT[...] = X[...].T
    lowT[...] = X[pl.ds(pl.multiple_of(own, RB), M), :].T

    @pl.loop(0, T)
    def _(t):
        @pl.loop(0, D // RB)
        def _(r):
            rr = rows(r)
            G[0, t, rr, 0:W] = nn(lowT[rr, :], q[t, :, 0:W]).astype(BF)
            G[0, t, rr, W:2 * W] = nn(xT[rr, :], k[t, :, 0:W]).astype(BF)
            G[0, t, rr, 2 * W:3 * W] = nn(xT[rr, :], v[t, :, 0:W]).astype(BF)

    @pl.loop(0, M // RB)
    def _(r):
        acc = jnp.zeros((RB, D), F32)
        for t in range(T):
            acc = acc + nt(k[t, othrows(r), 0:W], W_[0, t, :, W:2 * W])
            acc = acc + nt(v[t, othrows(r), 0:W], W_[0, t, :, 2 * W:3 * W])
        GTP[rows(r), :] = acc.astype(BF)
        acc = gz[rows(r), :]
        for t in range(T):
            acc = acc + nt(q[t, rows(r), 0:W], W_[0, t, :, 0:W])
            acc = acc + nt(k[t, ownrows(r), 0:W], W_[0, t, :, W:2 * W])
            acc = acc + nt(v[t, ownrows(r), 0:W], W_[0, t, :, 2 * W:3 * W])
        GTO[rows(r), :] = acc


MESH = pl.DeviceIdType.MESH


def place():
    dp = lax.axis_index("dp")
    z = lax.axis_index("tensor")
    core = dp % 2
    xbit = (dp // 2) % 2
    ybit = (dp // 4) % 2
    return dp, z, core, dp + 1 - 2 * core, dp + 2 - 4 * xbit, dp + 4 - 8 * ybit


def greet(devices):
    barrier = pltpu.get_barrier_semaphore()
    for device in devices:
        pl.semaphore_signal(barrier, inc=1, device_id=device, device_id_type=MESH)
    pl.semaphore_wait(barrier, len(devices))


def remote(src, dst, send, recv, device):
    return pltpu.make_async_remote_copy(
        src_ref=src, dst_ref=dst, send_sem=send, recv_sem=recv, device_id=device, device_id_type=MESH
    )


def gather_kernel(PK, TOK, COT, SEG, BP, W_, X, CO, SG, BI,
                  loc, zs, zr, os_, xr, yr, cr, fs, dr, ks, kr, bs, br, ts, tr):
    dp, z, core, dpc, dpx, dpy = place()
    T = W_.shape[1]
    S = PK.shape[1]
    SL = PK.shape[0]
    L = X.shape[0]
    M = L // 2
    home = z // 2
    greet([(dp, (z + d) % T) for d in range(1, T)] + [(dpx, z), (dpy, z), (dpc, z)])

    def block(s, t, i):
        return W_.at[s, t, pl.ds(pl.multiple_of(i * S, S), S), :]

    def source(d):
        return (z - d + T) % T

    started = []

    def go(copy):
        copy.start()
        started.append(copy)

    def push_z(s):
        for d in range(1, T):
            go(remote(PK.at[s], block(s, z, dp), zs.at[s, d - 1], zr.at[s, d - 1], (dp, (z + d) % T)))

    push_z(0)
    seq = pl.ds(pl.multiple_of((z % 2) * L, L), L)
    mine = pl.ds(pl.multiple_of((z % 2) * L + core * M, M), M)
    other = pl.ds(pl.multiple_of((z % 2) * L + (1 - core) * M, M), M)
    tok_out = remote(TOK.at[seq], X, ts.at[0], tr.at[0], (dpc, z))
    cot_out = remote(COT.at[other], CO, ts.at[1], tr.at[1], (dpc, z))
    seg_out = remote(SEG.at[z % 2], SG, ts.at[2], tr.at[2], (dpc, z))
    tok_in = pltpu.make_async_copy(TOK.at[seq], X, loc.at[4])
    cot_in = pltpu.make_async_copy(COT.at[mine], CO, loc.at[5])
    seg_in = pltpu.make_async_copy(SEG.at[z % 2], SG, loc.at[6])

    @pl.when(core == home)
    def _():
        for copy in (tok_out, cot_out, seg_out, tok_in, cot_in, seg_in):
            copy.start()

    local = [pltpu.make_async_copy(PK.at[s], block(s, z, dp), loc.at[s]) for s in range(SL)]
    local.append(pltpu.make_async_copy(BP, BI.at[z], loc.at[3]))
    for copy in local:
        copy.start()
    for d in range(1, T):
        go(remote(BP, BI.at[z], bs.at[d - 1], br.at[d - 1], (dp, (z + d) % T)))

    def send_own(s, d):
        t = source(d)
        src = PK.at[s] if d == 0 else block(s, t, dp)
        go(remote(src, block(s, t, dp), os_.at[0, s, d], xr.at[s, d], (dpx, z)))
        go(remote(src, block(s, t, dp), os_.at[1, s, d], yr.at[s, d], (dpy, z)))
        go(remote(src, block(s, t, dp), os_.at[2, s, d], cr.at[0, s, d], (dpc, z)))

    def pass_core(kind, s, d, i):
        t = source(d)
        go(remote(block(s, t, i), block(s, t, i), ks.at[kind - 1, s, d], cr.at[kind, s, d], (dpc, z)))

    dpxy = dpx + dpy - dp

    def wait_z(s, d):
        remote(PK.at[s], block(s, source(d), dp), zs.at[s, d - 1], zr.at[s, d - 1], (dp, z)).wait_recv()

    def take_x(s, d):
        t = source(d)
        remote(PK.at[s], block(s, t, dpx), os_.at[0, s, d], xr.at[s, d], (dpx, z)).wait_recv()
        if d < T // 2:
            go(remote(block(s, t, dpx), block(s, t, dpx), fs.at[s, d], dr.at[s, d], (dpy, z)))
        pass_core(1, s, d, dpx)

    def take_y(s, d):
        t = source(d)
        remote(PK.at[s], block(s, t, dpy), os_.at[1, s, d], yr.at[s, d], (dpy, z)).wait_recv()
        if d >= T // 2:
            go(remote(block(s, t, dpy), block(s, t, dpy), fs.at[s, d], dr.at[s, d], (dpx, z)))
        pass_core(2, s, d, dpy)

    def take_diag(s, d):
        t = source(d)
        remote(PK.at[s], block(s, t, dpxy), fs.at[s, d], dr.at[s, d], (dpx, z)).wait_recv()
        pass_core(3, s, d, dpxy)

    for s in range(SL):
        send_own(s, 0)
    pieces = [(s, d) for s in range(SL) for d in range(T)]
    for step in range(len(pieces) + 3):
        if step < len(pieces):
            s, d = pieces[step]
            if d:
                wait_z(s, d)
                send_own(s, d)
            if d == T - 1 and s + 1 < SL:
                push_z(s + 1)
        if 1 <= step <= len(pieces):
            s, d = pieces[step - 1]
            take_x(s, d)
            take_y(s, d)
        if 3 <= step:
            s, d = pieces[step - 3]
            take_diag(s, d)
    for s, d in pieces:
        for kind, i in enumerate((dpc, dpx + dpc - dp, dpy + dpc - dp, dpxy + dpc - dp)):
            remote(PK.at[s], block(s, source(d), i), ks.at[0, s, d], cr.at[kind, s, d], (dpc, z)).wait_recv()
    for d in range(1, T):
        remote(BP, BI.at[source(d)], bs.at[d - 1], br.at[d - 1], (dp, z)).wait_recv()
    for copy in local:
        copy.wait()

    @pl.when(core == home)
    def _():
        for copy in (tok_in, cot_in, seg_in):
            copy.wait()
        for copy in (tok_out, cot_out, seg_out):
            copy.wait_send()

    @pl.when(core != home)
    def _():
        for copy in (tok_out, cot_out, seg_out):
            copy.wait_recv()

    for copy in started:
        copy.wait_send()


def gather_call(PK, TOK, COT, SEG, BP, T, L):
    SL, S, D = PK.shape
    any_ = pl.BlockSpec(memory_space=pl.ANY)
    dma = pltpu.SemaphoreType.DMA
    return pl.pallas_call(
        gather_kernel,
        in_specs=[any_] * 5,
        out_specs=[any_] * 5,
        out_shape=[
            jax.ShapeDtypeStruct((SL, T, D, D), BF),
            jax.ShapeDtypeStruct((L, D), BF),
            jax.ShapeDtypeStruct((L // 2, D), BF),
            jax.ShapeDtypeStruct(SEG.shape[1:], F32),
            jax.ShapeDtypeStruct((T,) + BP.shape, F32),
        ],
        scratch_shapes=[
            dma((7,)),
            dma((SL, T - 1)), dma((SL, T - 1)),
            dma((3, SL, T)), dma((SL, T)), dma((SL, T)), dma((4, SL, T)),
            dma((SL, T)), dma((SL, T)),
            dma((3, SL, T)), dma((1,)),
            dma((T - 1,)), dma((T - 1,)),
            dma((3,)), dma((3,)),
        ],
        compiler_params=pltpu.CompilerParams(collective_id=0, has_side_effects=True),
    )(PK, TOK, COT, SEG, BP)


def tail_kernel(G, OUT, GTO, GTP, SM, OF, GF, DQ, DK, DV, DO, D1, D2, BQ, BV, B1, VEC,
                rgt, gtb, rc, r1, r2, rz, acc, ssend, srecv,
                gs, gr, osem, orcv, osl, gsem, grcv, gsl, fwd, cs, cr, s1, q1, s2, q2, s3, q3, ms, mr):
    dp, z, core, dpc, dpx, dpy = place()
    dpxy = dpx + dpy - dp
    T = G.shape[1]
    SL = G.shape[0]
    D = G.shape[2]
    S = rz.shape[2]
    M = OUT.shape[0]
    W = D // T
    flip = dpc - dp
    greet([(dp, (z + d) % T) for d in range(1, T)] + [(dpc, (z + d) % T) for d in range(T)]
          + [(dpx, z), (dpy, z)])
    started = []

    def go(copy):
        copy.start()
        started.append(copy)

    part = remote(GTP, rgt, gs, gr, (dpc, z))
    part.start()

    home = z // 2
    dest = dp - core + home

    def where(zz, cc):
        return pl.ds(pl.multiple_of(((zz % 2) * 2 + cc) * M, M), M)

    def push(src, full, sems, recv, slots):
        copies = []
        for d in (1, 2):
            for sign in (1, -1):
                zz = z + sign * d
                copies.append((zz, sign * d, remote(
                    src, full.at[where(z, core)], sems.at[(d - 1) * 2 + (sign < 0)],
                    recv.at[(z % 2) * 2 + core], (dest, (zz + T) % T))))
        for d in (2, 1):
            for zz, off, copy in copies:
                if abs(off) == d:
                    @pl.when((zz >= 0) & (zz < T))
                    def _(copy=copy):
                        copy.start()

        @pl.when(core != home)
        def _():
            remote(src, full.at[where(z, core)], sems.at[4], recv.at[(z % 2) * 2 + core], (dpc, z)).start()

        @pl.when(core == home)
        def _():
            pltpu.make_async_copy(src, full.at[where(z, core)], slots).start()

        def finish():
            for zz, off, copy in copies:
                @pl.when((zz >= 0) & (zz < T))
                def _(copy=copy):
                    copy.wait_send()

            @pl.when(core != home)
            def _():
                remote(src, full.at[where(z, core)], sems.at[4], recv.at[(z % 2) * 2 + core], (dpc, z)).wait_send()

            @pl.when(core == home)
            def _():
                pltpu.make_async_copy(src, full.at[where(z, core)], slots).wait()

        return finish

    relay = ((core == 0) & (z == 2)) | ((core == 1) & (z == 1))
    far = 3 * core
    beyond = 3 - far

    def got(src, full, recv, zz, cc):
        remote(src, full.at[where(zz, cc)], gs, recv.at[(zz % 2) * 2 + cc], (dp, z)).wait_recv()

    def hand_on(src, full, recv, base):
        @pl.when(relay)
        def _():
            for cc in range(2):
                got(src, full, recv, far, cc)
                remote(full.at[where(far, cc)], full.at[where(far, cc)], fwd.at[base + cc],
                       recv.at[(far % 2) * 2 + cc], (dp, beyond)).start()

    def settle(src, full, recv, base):
        for k in range(2):
            for cc in range(2):
                zz = core * 2 + k
                @pl.when(jnp.logical_not((zz == z) & (core == cc)) & jnp.logical_not(relay & (zz == far)))
                def _():
                    got(src, full, recv, zz, cc)

        @pl.when(relay)
        def _():
            for cc in range(2):
                remote(full.at[where(far, cc)], full.at[where(far, cc)], fwd.at[base + cc],
                       recv.at[(far % 2) * 2 + cc], (dp, beyond)).wait_send()

    out_done = push(OUT, OF, osem, orcv, osl)

    def rowsof(i):
        return pl.ds(pl.multiple_of(i * S, S), S)

    order = [2, 1, 0][:SL]
    rel = (dp, dpx, dpy, dpxy)
    for s in order:
        for k in range(4):
            go(remote(G.at[s, :, rowsof(rel[k] + flip), :], rc.at[s, k], cs.at[s, k], cr.at[s, k], (dpc, z)))

    part.wait_recv()
    gtb[...] = (GTO[...] + rgt[...].astype(F32)).astype(BF)
    gt_done = push(gtb, GF, gsem, grcv, gsl)

    acc[...] = SM[...]
    friends = [(dpc, z), (dpx, z), (dpy, z), (dp, z + 1 - 2 * (z % 2)), (dp, (z + 2) % T)]

    def small(step):
        ssend[step] = acc[...]
        go(remote(ssend.at[step], srecv.at[step], ms.at[step], mr.at[step], friends[step]))

    def small_end(step):
        remote(ssend.at[step], srecv.at[step], ms.at[step], mr.at[step], friends[step]).wait_recv()
        acc[...] += srecv[step]

    def add(dst, src):
        @pl.loop(0, dst.shape[0])
        def _(t):
            dst[t] = (dst[t].astype(F32) + src[t].astype(F32)).astype(BF)

    small(0)

    def stage0(s):
        for k in (3, 1, 2, 0):
            remote(G.at[s, :, rowsof(dp), :], rc.at[s, k], cs.at[s, k], cr.at[s, k], (dpc, z)).wait_recv()
            add(rc.at[s, k], G.at[s, :, rowsof(rel[k]), :])
            if k == 3:
                go(remote(rc.at[s, 3, 0:2], r1.at[s, 0], s1.at[s, 0], q1.at[s, 0], (dpy, z)))
                go(remote(rc.at[s, 3, 2:4], r1.at[s, 1], s1.at[s, 1], q1.at[s, 1], (dpx, z)))
            if k == 1:
                go(remote(rc.at[s, 1, 2:4], r2.at[s, 0, 2:4], s2.at[s, 0], q2.at[s, 0], (dpx, z)))
            if k == 2:
                go(remote(rc.at[s, 2, 0:2], r2.at[s, 1, 0:2], s2.at[s, 1], q2.at[s, 1], (dpy, z)))

    def stage1(s):
        remote(rc.at[s, 3, 0:2], r1.at[s, 0], s1.at[s, 0], q1.at[s, 0], (dpy, z)).wait_recv()
        add(rc.at[s, 1, 0:2], r1.at[s, 0])
        go(remote(rc.at[s, 1, 0:2], r2.at[s, 0, 0:2], s2.at[s, 2], q2.at[s, 2], (dpx, z)))
        remote(rc.at[s, 3, 2:4], r1.at[s, 1], s1.at[s, 1], q1.at[s, 1], (dpx, z)).wait_recv()
        add(rc.at[s, 2, 2:4], r1.at[s, 1])
        go(remote(rc.at[s, 2, 2:4], r2.at[s, 1, 2:4], s2.at[s, 3], q2.at[s, 3], (dpy, z)))

    def stage2(s):
        for k, part_ in ((0, slice(2, 4)), (1, slice(0, 2)), (2, slice(0, 2)), (3, slice(2, 4))):
            remote(rc.at[s, 1, part_], r2.at[s, k % 2, part_], s2.at[s, k], q2.at[s, k], (dpx, z)).wait_recv()
        add(rc.at[s, 0], r2.at[s, 0])
        add(rc.at[s, 0], r2.at[s, 1])
        for d in range(1, T):
            zz = (z + d) % T
            go(remote(rc.at[s, 0, zz], rz.at[s, d - 1], s3.at[s, d - 1], q3.at[s, d - 1], (dp, zz)))

    def stage3(s):
        total = rc[s, 0, z].astype(F32)
        for d in range(1, T):
            remote(rc.at[s, 0, 0], rz.at[s, d - 1], s3.at[s, d - 1], q3.at[s, d - 1], (dp, z)).wait_recv()
            total = total + rz[s, d - 1].astype(F32)
        if s == 0:
            DQ[...] = total[:, 0:W]
            DK[...] = total[:, W:2 * W]
            DV[...] = total[:, 2 * W:3 * W]
            DO[...] = total[:, 3 * W:4 * W].T
        if s == 1:
            D1[...] = total
        if s == 2:
            D2[...] = total.T

    n = len(order)
    for step in range(n + 3):
        if step < n:
            stage0(order[step])
        if step < 5:
            small_end(step)
            if step < 4:
                small(step + 1)
        if 0 <= step - 1 < n:
            stage1(order[step - 1])
        if 0 <= step - 2 < n:
            stage2(order[step - 2])
        if step == 2:
            hand_on(OUT, OF, orcv, 0)
        if 0 <= step - 3 < n:
            stage3(order[step - 3])
    hand_on(gtb, GF, grcv, 2)
    BQ[...] = acc[pl.ds(z, 1), 0:W]
    BV[...] = acc[pl.ds(T + z, 1), 0:W]
    B1[...] = acc[pl.ds(2 * T + z, 1), :]
    VEC[...] = acc[3 * T:3 * T + 8, :]
    settle(OUT, OF, orcv, 0)
    settle(gtb, GF, grcv, 2)
    out_done()
    gt_done()
    part.wait_send()
    for copy in started:
        copy.wait_send()


def tail_call(G, OUT, GTO, GTP, SM, T, S, F):
    SL, _, D, _ = G.shape
    M = OUT.shape[0]
    W = D // T
    any_ = pl.BlockSpec(memory_space=pl.ANY)
    vm = pl.BlockSpec(memory_space=pltpu.VMEM)
    dma = pltpu.SemaphoreType.DMA
    f32 = lambda *s: jax.ShapeDtypeStruct(s, F32)
    return pl.pallas_call(
        tail_kernel,
        in_specs=[vm] * 5,
        out_specs=[any_, any_] + [vm] * 10,
        out_shape=[
            jax.ShapeDtypeStruct((4 * M, D), BF),
            jax.ShapeDtypeStruct((4 * M, D), BF),
            f32(S, W), f32(S, W), f32(S, W), f32(W, S), f32(S, F), f32(F, S),
            f32(1, W), f32(1, W), f32(1, F), f32(8, D),
        ],
        scratch_shapes=[
            pltpu.VMEM((M, D), BF), pltpu.VMEM((M, D), BF),
            pltpu.VMEM((SL, 4, T, S, D), BF),
            pltpu.VMEM((SL, 2, 2, S, D), BF),
            pltpu.VMEM((SL, 2, T, S, D), BF),
            pltpu.VMEM((SL, T - 1, S, D), BF),
            pltpu.VMEM(SM.shape, F32), pltpu.VMEM((5,) + SM.shape, F32), pltpu.VMEM((5,) + SM.shape, F32),
            dma, dma,
            dma((5,)), dma((4,)), dma,
            dma((5,)), dma((4,)), dma,
            dma((4,)),
            dma((SL, 4)), dma((SL, 4)),
            dma((SL, 2)), dma((SL, 2)),
            dma((SL, 4)), dma((SL, 4)),
            dma((SL, T - 1)), dma((SL, T - 1)),
            dma((5,)), dma((5,)),
        ],
        compiler_params=pltpu.CompilerParams(
            collective_id=1, has_side_effects=True, vmem_limit_bytes=60 << 20
        ),
    )(G, OUT, GTO, GTP, SM)


def doc_ids(lengths, count):
    ends = jnp.cumsum(lengths)
    places = jnp.arange(count, dtype=jnp.int32)
    return jnp.sum((places[:, None] >= ends[None, :]).astype(jnp.int32), axis=1)


def collect(wq, wk, wv, wo, w1, w2):
    return (
        lax.all_gather(wq, "dp", axis=0, tiled=True),
        lax.all_gather(wk, "dp", axis=0, tiled=True),
        lax.all_gather(wv, "dp", axis=0, tiled=True),
        lax.all_gather(wo, "dp", axis=1, tiled=True),
        lax.all_gather(w1, "dp", axis=0, tiled=True),
        lax.all_gather(w2, "dp", axis=1, tiled=True),
    )


def reduce_large(grads):
    return (
        lax.psum_scatter(grads[0], "dp", scatter_dimension=0, tiled=True),
        lax.psum_scatter(grads[1], "dp", scatter_dimension=0, tiled=True),
        lax.psum_scatter(grads[2], "dp", scatter_dimension=0, tiled=True),
        lax.psum_scatter(grads[3], "dp", scatter_dimension=1, tiled=True),
        lax.psum_scatter(grads[4], "dp", scatter_dimension=0, tiled=True),
        lax.psum_scatter(grads[5], "dp", scatter_dimension=1, tiled=True),
    )


def reduce_small(grads):
    return lax.psum(
        (grads[0], grads[1], grads[2], grads[3], grads[4], grads[5], grads[6], grads[7], grads[8]),
        "dp",
    )


def contract_rows(left, right):
    return lax.dot_general(
        left, right, (((0,), (0,)), ((), ())), preferred_element_type=jnp.float32
    )


def contract_cols(left, right):
    return lax.dot_general(
        left, right, (((1,), (1,)), ((), ())), preferred_element_type=jnp.float32
    )


def contract_mixed(left, right):
    return lax.dot_general(
        left, right, (((0,), (1,)), ((), ())), preferred_element_type=jnp.float32
    )


def norm_forward(total, gain, shift):
    centre = total - jnp.mean(total, axis=-1, keepdims=True)
    scaled = lax.rsqrt(jnp.mean(centre * centre, axis=-1, keepdims=True) + EPS)
    normed = centre * scaled
    return (normed * gain + shift, normed, scaled)


def norm_backward(grad_result, normed, scaled, gain):
    grad_normed = grad_result * gain
    mean_grad = jnp.mean(grad_normed, axis=-1, keepdims=True)
    mean_cross = jnp.mean(grad_normed * normed, axis=-1, keepdims=True)
    grad_total = scaled * (grad_normed - mean_grad - normed * mean_cross)
    return (grad_total, jnp.sum(grad_result * normed, axis=0), jnp.sum(grad_result, axis=0))


def block_scores(query_block, key_heads, seg_block, seg, scale):
    raw = (
        jnp.einsum("hdq,hdk->hqk", query_block, key_heads, preferred_element_type=jnp.float32)
        * scale
    )
    same_doc = seg_block[:, None] == seg[None, :]
    return jnp.where(same_doc[None], raw, NEG)


def general_body(
    tokens,
    doc_lengths,
    wq,
    bq,
    wk,
    wv,
    bv,
    wo,
    bo,
    gain1,
    shift1,
    w1,
    b1,
    w2,
    b2,
    gain2,
    shift2,
    cotangent,
):
    micro = doc_lengths.shape[0]
    seq_len = tokens.shape[0] // micro
    block = min(512, seq_len)
    scale = HD ** (-0.5)
    results = []
    grad_inputs = []
    large_total = None
    small_total = None
    for index in range(micro):
        full = collect(wq, wk, wv, wo, w1, w2)
        full_q, full_k, full_v, full_o, full_first, full_second = full
        width = full_q.shape[1]
        heads_here = width // HD
        rows_in = tokens[index * seq_len : (index + 1) * seq_len]
        inputs = rows_in.astype(jnp.float32)
        seg = doc_ids(doc_lengths[index], seq_len)
        queries = (
            lax.dot_general(
                full_q, rows_in, (((0,), (1,)), ((), ())), preferred_element_type=jnp.float32
            )
            + bq[:, None]
        ).astype(jnp.bfloat16)
        keys_low = lax.dot_general(
            full_k, rows_in, (((0,), (1,)), ((), ())), preferred_element_type=jnp.float32
        ).astype(jnp.bfloat16)
        values_low = (
            lax.dot_general(
                full_v, rows_in, (((0,), (1,)), ((), ())), preferred_element_type=jnp.float32
            )
            + bv[:, None]
        ).astype(jnp.bfloat16)
        query_heads = queries.reshape(heads_here, HD, seq_len)
        key_heads = keys_low.reshape(heads_here, HD, seq_len)
        value_heads = values_low.reshape(heads_here, HD, seq_len)
        pieces = []
        log_totals = []
        for offset in range(0, seq_len, block):
            scores = block_scores(
                query_heads[:, :, offset : offset + block],
                key_heads,
                seg[offset : offset + block],
                seg,
                scale,
            )
            highest = jnp.max(scores, axis=-1, keepdims=True)
            log_total = highest + jnp.log(
                jnp.sum(jnp.exp(scores - highest), axis=-1, keepdims=True)
            )
            probs_low = jnp.exp(scores - log_total).astype(jnp.bfloat16)
            pieces.append(
                jnp.einsum(
                    "hqk,hdk->hdq", probs_low, value_heads, preferred_element_type=jnp.float32
                )
            )
            log_totals.append(log_total)
        mixed_cols = jnp.concatenate(pieces, axis=2).reshape(width, seq_len).astype(jnp.bfloat16)
        attended = lax.psum(
            contract_rows(mixed_cols, full_o).astype(jnp.bfloat16), "tensor"
        ).astype(jnp.float32)
        first, normed_one, scaled_one = norm_forward(inputs + attended + bo, gain1, shift1)
        first_low = first.astype(jnp.bfloat16)
        inner = jnp.dot(first_low, full_first, preferred_element_type=jnp.float32) + b1
        hidden = jax.nn.gelu(inner, approximate=False).astype(jnp.bfloat16)
        second = lax.psum(
            jnp.dot(hidden, full_second, preferred_element_type=jnp.float32).astype(jnp.bfloat16),
            "tensor",
        ).astype(jnp.float32)
        result, normed_two, scaled_two = norm_forward(first + second + b2, gain2, shift2)
        results.append(result.astype(jnp.bfloat16))
        grad_result = cotangent[index * seq_len : (index + 1) * seq_len].astype(jnp.float32)
        grad_two, grad_gain2, grad_shift2 = norm_backward(
            grad_result, normed_two, scaled_two, gain2
        )
        grad_b2 = jnp.sum(grad_two, axis=0)
        full = collect(wq, wk, wv, wo, w1, w2)
        full_q, full_k, full_v, full_o, full_first, full_second = full
        two_low = grad_two.astype(jnp.bfloat16)
        grad_w2 = contract_rows(hidden, two_low)
        grad_hidden = contract_cols(two_low, full_second)
        grad_inner = jax.vjp(partial(jax.nn.gelu, approximate=False), inner)[1](grad_hidden)[
            0
        ].astype(jnp.bfloat16)
        grad_b1 = jnp.sum(grad_inner.astype(jnp.float32), axis=0)
        grad_w1 = contract_rows(first_low, grad_inner)
        grad_first = grad_two + lax.psum(
            contract_cols(grad_inner, full_first).astype(jnp.bfloat16), "tensor"
        ).astype(jnp.float32)
        grad_one, grad_gain1, grad_shift1 = norm_backward(grad_first, normed_one, scaled_one, gain1)
        grad_bo = jnp.sum(grad_one, axis=0)
        one_low = grad_one.astype(jnp.bfloat16)
        grad_wo = jnp.dot(mixed_cols, one_low, preferred_element_type=jnp.float32)
        grad_mixed = (
            contract_cols(full_o, one_low).astype(jnp.bfloat16).reshape(heads_here, HD, seq_len)
        )
        grad_key_heads = jnp.zeros((heads_here, HD, seq_len), jnp.float32)
        grad_value_heads = jnp.zeros((heads_here, HD, seq_len), jnp.float32)
        grad_query_pieces = []
        for number, offset in enumerate(range(0, seq_len, block)):
            query_block = query_heads[:, :, offset : offset + block]
            grad_block = grad_mixed[:, :, offset : offset + block]
            scores = block_scores(query_block, key_heads, seg[offset : offset + block], seg, scale)
            probs = jnp.exp(scores - log_totals[number])
            grad_probs = jnp.einsum(
                "hdq,hdk->hqk", grad_block, value_heads, preferred_element_type=jnp.float32
            )
            centre = jnp.sum(probs * grad_probs, axis=-1, keepdims=True)
            grad_scores = (probs * (grad_probs - centre)).astype(jnp.bfloat16)
            grad_query_pieces.append(
                jnp.einsum(
                    "hqk,hdk->hdq", grad_scores, key_heads, preferred_element_type=jnp.float32
                )
                * scale
            )
            grad_key_heads = (
                grad_key_heads
                + jnp.einsum(
                    "hqk,hdq->hdk", grad_scores, query_block, preferred_element_type=jnp.float32
                )
                * scale
            )
            grad_value_heads = grad_value_heads + jnp.einsum(
                "hqk,hdq->hdk",
                probs.astype(jnp.bfloat16),
                grad_block,
                preferred_element_type=jnp.float32,
            )
        grad_queries = (
            jnp.concatenate(grad_query_pieces, axis=2).reshape(width, seq_len).astype(jnp.bfloat16)
        )
        grad_keys = grad_key_heads.reshape(width, seq_len).astype(jnp.bfloat16)
        grad_values = grad_value_heads.reshape(width, seq_len).astype(jnp.bfloat16)
        grad_bq = jnp.sum(grad_queries.astype(jnp.float32), axis=1)
        grad_bv = jnp.sum(grad_values.astype(jnp.float32), axis=1)
        grad_wq = contract_cols(rows_in.T, grad_queries)
        grad_wk = contract_cols(rows_in.T, grad_keys)
        grad_wv = contract_cols(rows_in.T, grad_values)
        back_terms = (
            contract_mixed(grad_queries, full_q)
            + contract_mixed(grad_keys, full_k)
            + contract_mixed(grad_values, full_v)
        )
        grad_rows = grad_one + lax.psum(back_terms.astype(jnp.bfloat16), "tensor").astype(
            jnp.float32
        )
        grad_inputs.append(grad_rows.astype(jnp.bfloat16))
        large_local = (grad_wq, grad_wk, grad_wv, grad_wo, grad_w1, grad_w2)
        small_local = (
            grad_bq,
            grad_bv,
            grad_b1,
            grad_bo,
            grad_b2,
            grad_gain1,
            grad_shift1,
            grad_gain2,
            grad_shift2,
        )
        large_local = reduce_large(large_local)
        small_local = reduce_small(small_local)
        if large_total is None:
            large_total = large_local
            small_total = small_local
        else:
            large_total = jax.tree.map(jnp.add, large_total, large_local)
            small_total = jax.tree.map(jnp.add, small_total, small_local)
    grad_wq, grad_wk, grad_wv, grad_wo, grad_w1, grad_w2 = large_total
    (
        grad_bq,
        grad_bv,
        grad_b1,
        grad_bo,
        grad_b2,
        grad_gain1,
        grad_shift1,
        grad_gain2,
        grad_shift2,
    ) = small_total
    return (
        jnp.concatenate(results, axis=0),
        jnp.concatenate(grad_inputs, axis=0),
        grad_wq,
        grad_bq,
        grad_wk,
        grad_wv,
        grad_bv,
        grad_wo,
        grad_bo,
        grad_gain1,
        grad_shift1,
        grad_w1,
        grad_b1,
        grad_w2,
        grad_b2,
        grad_gain2,
        grad_shift2,
    )


def compute_call(W_, X, CO, SG, BI, NP, T):
    _, _, D, F = W_.shape
    L = X.shape[0]
    M = L // 2
    vm = pl.BlockSpec(memory_space=pltpu.VMEM)

    def kernel(*refs):
        fb_kernel(lax.axis_index("dp") % 2, *refs)

    return pl.pallas_call(
        kernel,
        in_specs=[vm] * 6,
        out_specs=[vm] * 5,
        out_shape=[
            jax.ShapeDtypeStruct((M, D), BF),
            jax.ShapeDtypeStruct((M, D), F32),
            jax.ShapeDtypeStruct((M, D), BF),
            jax.ShapeDtypeStruct(W_.shape, BF),
            jax.ShapeDtypeStruct((24, D), F32),
        ],
        scratch_shapes=fb_scratch(T, D // T, F, D, L),
        compiler_params=pltpu.CompilerParams(vmem_limit_bytes=63 << 20),
    )(W_, X, CO, SG, BI, NP)


def split_body(T, tokens, doc_lengths, wq, bq, wk, wv, bv, wo, bo, gain1, shift1, w1, b1, w2, b2,
               gain2, shift2, cotangent):
    micro = doc_lengths.shape[0]
    L = tokens.shape[0] // micro
    D = tokens.shape[1]
    S, W = wq.shape
    F = w1.shape[1]
    packed = jnp.stack([jnp.concatenate([wq, wk, wv, wo.T], axis=1), w1, w2.T])
    ends = jnp.cumsum(doc_lengths, axis=1)
    spots = jnp.arange(L, dtype=jnp.int32)
    seg = jnp.sum((spots[None, :, None] >= ends[:, None, :]).astype(F32), axis=2)
    seg = jnp.broadcast_to(seg[:, None, :], (micro, 8, L))
    row = lambda x: jnp.pad(x[None, :], ((0, 0), (0, D - x.shape[0])))
    biases = jnp.concatenate([row(b1), row(bq), row(bv), jnp.zeros((5, D), F32)])
    norms = jnp.stack([bo, gain1, shift1, b2, gain2, shift2, bo, bo])
    W_, X, CO, SG, BI = gather_call(packed, tokens, cotangent, seg, biases, T, L)
    out, gto, gtp, G, sm = compute_call(W_, X, CO, SG, BI, norms, T)
    (full, grads, dq, dk, dv, do, d1, d2, gbq, gbv, gb1, vec) = tail_call(G, out, gto, gtp, sm, T, S, F)
    return (full, grads, dq, gbq[0], dk, dv, gbv[0], do, vec[0], vec[2], vec[3], d1, gb1[0], d2,
            vec[1], vec[4], vec[5])


def solution(mesh):
    placed = (
        P("dp", None),
        P("dp", None),
        P("dp", "tensor"),
        P("tensor"),
        P("dp", "tensor"),
        P("dp", "tensor"),
        P("tensor"),
        P("tensor", "dp"),
        P(),
        P(),
        P(),
        P("dp", "tensor"),
        P("tensor"),
        P("tensor", "dp"),
        P(),
        P(),
        P(),
        P("dp", None),
    )
    if mesh.shape["dp"] == 8 and mesh.shape["tensor"] == 4:
        body = partial(split_body, mesh.shape["tensor"])
    else:
        body = general_body
    return jax.shard_map(
        body,
        mesh=mesh,
        in_specs=placed,
        out_specs=(
            P("dp", None),
            P("dp", None),
            P("dp", "tensor"),
            P("tensor"),
            P("dp", "tensor"),
            P("dp", "tensor"),
            P("tensor"),
            P("tensor", "dp"),
            P(),
            P(),
            P(),
            P("dp", "tensor"),
            P("tensor"),
            P("tensor", "dp"),
            P(),
            P(),
            P(),
        ),
        check_vma=False,
    )
```

```python
from functools import partial
import jax
import jax.numpy as jnp
from jax import lax
from jax.experimental import pallas as pl
from jax.experimental.pallas import tpu as pltpu

from jax.sharding import PartitionSpec as P

BF = jnp.bfloat16
F32 = jnp.float32
EPS = 1e-12
HD = 64
NEG = -1e30
RB = 256


def nn(a, b):
    return jnp.dot(a, b, preferred_element_type=F32)


def nt(a, b):
    return lax.dot_general(a, b, (((1,), (1,)), ((), ())), preferred_element_type=F32)


def rows(r, n=RB):
    return pl.ds(pl.multiple_of(r * n, n), n)


def mean_last(x):
    return jnp.mean(x, axis=-1, keepdims=True)


def colsum(x):
    return jnp.sum(x, axis=0, keepdims=True)


MESH = pl.DeviceIdType.MESH


def remote(src, dst, send, recv, device):
    return pltpu.make_async_remote_copy(
        src_ref=src, dst_ref=dst, send_sem=send, recv_sem=recv, device_id=device, device_id_type=MESH
    )


def layer_kernel(
    WQ, WK, WV, WO, W1, W2T, NP, BP, LEN, TOK, COT,
    OF, GF, DQ, DK, DV, DO, D1, D2, BQ, BV, B1, VEC,
    PK, W_, G0, X, CO, SG, BI, SM,
    q, k, v, mixed, vT, oT, lse, bias, n1, r1, flow, hid, gp, gz, low, xT, outb,
    rgt, rc, ra, rb, rz, ssend, srecv,
    loc, zs, zr, os_, xr, yr, cr, fs, dr, ks, bs, br, ts, tr,
    gs, gr, osem, orcv, osl, gsem, grcv, gsl, fwd, cs, crr, s1, q1, s2, q2, s3, q3, ms, mr,
):
    SL, S, D = PK.shape
    T = W_.shape[1]
    L = X.shape[0]
    M = L // 2
    W = D // T
    NH = W // HD
    scale = HD ** (-0.5)
    QC = RB

    dp = lax.axis_index("dp")
    z = lax.axis_index("tensor")
    core = dp % 2
    dpc = dp + 1 - 2 * core
    dpx = dp + 2 - 4 * ((dp // 2) % 2)
    dpy = dp + 4 - 8 * ((dp // 4) % 2)
    dpxy = dpx + dpy - dp
    flip = dpc - dp
    home = z // 2
    own = core * M
    oth = (1 - core) * M

    def ownrows(r):
        return pl.ds(pl.multiple_of(own + r * RB, RB), RB)

    def othrows(r):
        return pl.ds(pl.multiple_of(oth + r * RB, RB), RB)

    PK[0, :, 0:W] = WQ[...]
    PK[0, :, W:2 * W] = WK[...]
    PK[0, :, 2 * W:3 * W] = WV[...]
    PK[0, :, 3 * W:4 * W] = WO[...].T
    PK[1] = W1[...]
    PK[2] = W2T[...]

    spot = lax.broadcasted_iota(jnp.int32, (8, L), 1)
    doc = jnp.zeros((8, L), F32)
    end = jnp.int32(0)
    for j in range(LEN.shape[1]):
        end = end + LEN[z % 2, j]
        doc = doc + jnp.where(spot >= end, 1.0, 0.0)
    SG[0] = doc

    barrier = pltpu.get_barrier_semaphore()
    friends = [(dp, (z + d) % T) for d in range(1, T)] + [(dpc, (z + d) % T) for d in range(T)] + [
        (dpx, z), (dpy, z)]
    for friend in friends:
        pl.semaphore_signal(barrier, inc=1, device_id=friend, device_id_type=MESH)
    pl.semaphore_wait(barrier, len(friends))

    def block(s, t, i):
        return W_.at[s, t, pl.ds(pl.multiple_of(i * S, S), S), :]

    def source(d):
        return (z - d + T) % T

    def push_z(s):
        for d in range(1, T):
            remote(PK.at[s], block(s, z, dp), zs.at[s, d - 1], zr.at[s, d - 1], (dp, (z + d) % T)).start()

    def send_block(s, d, src):
        t = source(d)
        remote(src, block(s, t, dp), os_.at[0, s, d], xr.at[s, d], (dpx, z)).start()
        remote(src, block(s, t, dp), os_.at[1, s, d], yr.at[s, d], (dpy, z)).start()
        remote(src, block(s, t, dp), os_.at[2, s, d], cr.at[0, s, d], (dpc, z)).start()

    def pass_core(kind, s, d, i):
        t = source(d)
        remote(block(s, t, i), block(s, t, i), ks.at[kind - 1, s, d], cr.at[kind, s, d], (dpc, z)).start()

    def wait_z(s, d):
        remote(PK.at[s], block(s, source(d), dp), zs.at[s, d - 1], zr.at[s, d - 1], (dp, (z + 1) % T)).wait_recv()

    def take_x(s, d):
        t = source(d)
        remote(PK.at[s], block(s, t, dpx), os_.at[0, s, d], xr.at[s, d], (dpx, z)).wait_recv()

        @pl.when(d < T // 2)
        def _():
            remote(block(s, t, dpx), block(s, t, dpx), fs.at[s, d], dr.at[s, d], (dpy, z)).start()

        pass_core(1, s, d, dpx)

    def take_y(s, d):
        t = source(d)
        remote(PK.at[s], block(s, t, dpy), os_.at[1, s, d], yr.at[s, d], (dpy, z)).wait_recv()

        @pl.when(d >= T // 2)
        def _():
            remote(block(s, t, dpy), block(s, t, dpy), fs.at[s, d], dr.at[s, d], (dpx, z)).start()

        pass_core(2, s, d, dpy)

    def take_diag(s, d):
        remote(PK.at[s], block(s, source(d), dpxy), fs.at[s, d], dr.at[s, d], (dpx, z)).wait_recv()
        pass_core(3, s, d, dpxy)

    PIECES = SL * T

    def gather_step(n):
        n = jnp.int32(n)

        @pl.when(n < PIECES)
        def _():
            s, d = n // T, n % T

            @pl.when(d > 0)
            def _():
                wait_z(s, d)
                send_block(s, d, block(s, source(d), dp))

            @pl.when((d == T - 1) & (s + 1 < SL))
            def _():
                push_z(s + 1)

        @pl.when((n >= 1) & (n <= PIECES))
        def _():
            take_x((n - 1) // T, (n - 1) % T)
            take_y((n - 1) // T, (n - 1) % T)

        @pl.when((n >= 3) & (n < PIECES + 3))
        def _():
            take_diag((n - 3) // T, (n - 3) % T)

    def gathered(s):
        for d in range(T):
            for kind, i in enumerate((dpc, dpx + flip, dpy + flip, dpxy + flip)):
                remote(PK.at[s], block(s, source(d), i), os_.at[2, s, d], cr.at[kind, s, d], (dpc, z)).wait_recv()

    push_z(0)
    seq = pl.ds(pl.multiple_of((z % 2) * L, L), L)
    mine = pl.ds(pl.multiple_of((z % 2) * L + own, M), M)
    other = pl.ds(pl.multiple_of((z % 2) * L + oth, M), M)
    tok_out = remote(TOK.at[seq], X, ts.at[0], tr.at[0], (dpc, z))
    cot_out = remote(COT.at[other], CO, ts.at[1], tr.at[1], (dpc, z))
    doc_out = remote(SG.at[0], SG.at[1], ts.at[2], tr.at[2], (dpc, z))
    tok_in = pltpu.make_async_copy(TOK.at[seq], X, loc.at[0])
    cot_in = pltpu.make_async_copy(COT.at[mine], CO, loc.at[1])

    @pl.when(core == home)
    def _():
        for copy in (tok_out, cot_out, doc_out, tok_in, cot_in):
            copy.start()

    for d in range(1, T):
        remote(BP, BI.at[z], bs.at[d - 1], br.at[d - 1], (dp, (z + d) % T)).start()
    for s in range(SL):
        send_block(s, 0, PK.at[s])
        W_[s, z, pl.ds(pl.multiple_of(dp * S, S), S), :] = PK[s]
    BI[z] = BP[...]
    SM[...] = jnp.zeros_like(SM)

    @pl.loop(0, T + 1)
    def _(n):
        gather_step(n)

    @pl.when(core == home)
    def _():
        tok_in.wait()
        cot_in.wait()
        for copy in (tok_out, cot_out, doc_out):
            copy.wait_send()

    @pl.when(core != home)
    def _():
        for copy in (tok_out, cot_out, doc_out):
            copy.wait_recv()

    for d in range(1, T):
        remote(BP, BI.at[source(d)], bs.at[d - 1], br.at[d - 1], (dp, (z + 1) % T)).wait_recv()

    docs = jnp.where(core == home, SG[0], SG[1])
    SG[0] = docs
    key_doc = jnp.broadcast_to(docs[0:1, :], (128, L)).T
    for i in range(M // 128):
        query_doc = SG[0, 0:1, pl.ds(pl.multiple_of(own + i * 128, 128), 128)]
        bias[:, i * 128:(i + 1) * 128] = jnp.where(key_doc == query_doc, 0.0, NEG)

    @pl.loop(T + 1, T + 3)
    def _(n):
        gather_step(n)

    gathered(0)

    @pl.loop(0, T)
    def _(t):
        @pl.loop(0, L // RB)
        def _(r):
            xs = X[rows(r), :]
            k[t, rows(r), 0:W] = nn(xs, W_[0, t, :, W:2 * W]).astype(BF)
            v[t, rows(r), 0:W] = (nn(xs, W_[0, t, :, 2 * W:3 * W]) + BI[t, 2:3, 0:W]).astype(BF)

        @pl.loop(0, M // RB)
        def _(r):
            xs = X[ownrows(r), :]
            q[t, rows(r), 0:W] = (
                (nn(xs, W_[0, t, :, 0:W]) + BI[t, 1:2, 0:W]).astype(BF) * BF(scale)
            ).astype(BF)

    lane = lax.broadcasted_iota(jnp.int32, (1, 128), 1)

    def head(ref, t, rr, j):
        if j % 2 == 0 and j == NH - 1:
            return ref[t, rr, j * HD:(j + 1) * HD]
        p = j // 2
        return ref[t, rr, p * 128:(p + 1) * 128]

    def only(part, j):
        if part.shape[1] == HD:
            return part
        keep = (lane < HD) if j % 2 == 0 else (lane >= HD)
        return jnp.where(keep, part, jnp.zeros_like(part))

    everything = slice(None)

    @pl.loop(0, T)
    def _(t):
        gather_step(T + 3 + t)
        vT[...] = v[t, :, 0:W].T

        @pl.loop(0, M // QC)
        def _(i):
            qs = rows(i, QC)
            for j in range(NH):
                s = nt(head(k, t, everything, j), only(head(q, t, qs, j), j)) + bias[:, qs]
                m = jnp.max(s, axis=0, keepdims=True)
                p = jnp.exp(s - m)
                l = jnp.sum(p, axis=0, keepdims=True)
                lse[t * 4 + j, :, qs] = jnp.broadcast_to(m + jnp.log(l), (8, QC))
                o = nn(vT[j * HD:(j + 1) * HD, :], p.astype(BF))
                oT[j * HD:(j + 1) * HD, qs] = o * (1.0 / l)

        mixed[t, :, 0:W] = oT[...].T.astype(BF)

    @pl.loop(0, M // RB)
    def _(r):
        zz = X[ownrows(r), :].astype(F32) + NP[0:1, :]
        for t in range(T):
            zz = zz + nt(mixed[t, rows(r), 0:W], W_[0, t, :, 3 * W:4 * W])
        cen = zz - mean_last(zz)
        rs = lax.rsqrt(mean_last(cen * cen) + EPS)
        n = cen * rs
        n1[rows(r), :] = n
        r1[rows(r), :] = jnp.broadcast_to(rs, (RB, 128))
        flow[rows(r), :] = (n * NP[1:2, :] + NP[2:3, :]).astype(BF)

    gather_step(2 * T + 3)
    gathered(1)

    @pl.loop(0, T)
    def _(t):
        @pl.when(t < T - 1)
        def _():
            gather_step(2 * T + 4 + t)

        @pl.loop(0, M // RB)
        def _(r):
            rr = rows(r)
            inner = nn(flow[rr, :], W_[1, t]) + BI[t, 0:1, :]
            phi = 0.5 * (1.0 + lax.erf(inner * (2.0 ** -0.5)))
            hid[t, rr, :] = (inner * phi).astype(BF)
            gp[t, rr, :] = (phi + inner * (jnp.exp(-0.5 * inner * inner) * 0.3989422804014327)).astype(BF)

    gathered(2)

    @pl.loop(0, M // RB)
    def _(r):
        rr = rows(r)
        zz = n1[rr, :] * NP[1:2, :] + NP[2:3, :] + NP[3:4, :]
        for t in range(T):
            zz = zz + nt(hid[t, rr, :], W_[2, t])
        cen = zz - mean_last(zz)
        rs = lax.rsqrt(mean_last(cen * cen) + EPS)
        n = cen * rs
        outb[rr, :] = (n * NP[4:5, :] + NP[5:6, :]).astype(BF)
        ct = CO[rr, :].astype(F32)
        g = ct * NP[4:5, :]
        g2 = rs * (g - mean_last(g) - n * mean_last(g * n))
        SM[16:17, :] += colsum(ct * n)
        SM[17:18, :] += colsum(ct)
        SM[13:14, :] += colsum(g2)
        gz[rr, :] = g2
        low[rr, :] = g2.astype(BF)

    dest = dp - core + home

    def spotrows(zz, cc):
        return pl.ds(pl.multiple_of(((zz % 2) * 2 + cc) * M, M), M)

    def pushes(src, full, sems, recv):
        copies = []
        for d in (2, 1):
            for sign in (1, -1):
                zz = z + sign * d
                copies.append((zz, remote(
                    src, full.at[spotrows(z, core)], sems.at[(d - 1) * 2 + (sign < 0)],
                    recv.at[(z % 2) * 2 + core], (dest, (zz + T) % T))))
        return copies

    def own_copy(src, full, sems, recv, slot):
        away = remote(src, full.at[spotrows(z, core)], sems.at[4], recv.at[(z % 2) * 2 + core], (dpc, z))
        here = pltpu.make_async_copy(src, full.at[spotrows(z, core)], slot)
        return away, here

    def push(src, full, sems, recv, slot):
        for zz, copy in pushes(src, full, sems, recv):
            pl.when((zz >= 0) & (zz < T))(copy.start)
        away, here = own_copy(src, full, sems, recv, slot)
        pl.when(core != home)(away.start)
        pl.when(core == home)(here.start)

    def pushed(src, full, sems, recv, slot):
        for zz, copy in pushes(src, full, sems, recv):
            pl.when((zz >= 0) & (zz < T))(copy.wait_send)
        away, here = own_copy(src, full, sems, recv, slot)
        pl.when(core != home)(away.wait_send)
        pl.when(core == home)(here.wait)

    relay = ((core == 0) & (z == 2)) | ((core == 1) & (z == 1))
    far = 3 * core
    beyond = 3 - far

    def got(src, full, recv, zz, cc):
        remote(src, full.at[spotrows(zz, cc)], gs, recv.at[(zz % 2) * 2 + cc], (dpx, z)).wait_recv()

    def handing(full, recv, base, cc):
        return remote(full.at[spotrows(far, cc)], full.at[spotrows(far, cc)], fwd.at[base + cc],
                      recv.at[(far % 2) * 2 + cc], (dp, beyond))

    def hand_on(src, full, recv, base):
        @pl.when(relay)
        def _():
            for cc in range(2):
                got(src, full, recv, far, cc)
                handing(full, recv, base, cc).start()

    def settle(src, full, recv, base):
        for kk in range(2):
            for cc in range(2):
                zz = core * 2 + kk

                @pl.when(jnp.logical_not((zz == z) & (core == cc)) & jnp.logical_not(relay & (zz == far)))
                def _():
                    got(src, full, recv, zz, cc)

        @pl.when(relay)
        def _():
            for cc in range(2):
                handing(full, recv, base, cc).wait_send()

    push(outb, OF, osem, orcv, osl)

    for s in range(SL):
        for d in range(1, T):
            remote(PK.at[s], block(s, z, dp), zs.at[s, d - 1], zr.at[s, d - 1], (dp, (z + d) % T)).wait_send()
        for d in range(T):
            for kind in range(3):
                remote(PK.at[s], block(s, z, dp), os_.at[kind, s, d], xr.at[s, d], (dpx, z)).wait_send()
                remote(PK.at[s], block(s, z, dp), ks.at[kind, s, d], xr.at[s, d], (dpx, z)).wait_send()
            remote(PK.at[s], block(s, z, dp), fs.at[s, d], xr.at[s, d], (dpx, z)).wait_send()
    for d in range(1, T):
        remote(BP, BI.at[z], bs.at[d - 1], br.at[d - 1], (dp, (z + d) % T)).wait_send()

    def grad(s):
        return G0 if s == 0 else W_.at[s]

    rel = (dp, dpx, dpy, dpxy)

    def rowsof(i):
        return pl.ds(pl.multiple_of(i * S, S), S)

    def core_copy(s, kk):
        return remote(grad(s).at[:, rowsof(rel[kk] + flip), :], rc.at[s, kk], cs.at[s, kk], crr.at[s, kk], (dpc, z))

    def turn(s, kk):
        src, dst, who = (
            (rc.at[s, 3, 0:2], ra.at[s, 0], (dpy, z)),
            (rc.at[s, 3, 2:4], ra.at[s, 1], (dpx, z)),
        )[kk]
        return remote(src, dst, s1.at[s, kk], q1.at[s, kk], who)

    def straight(s, kk):
        src, dst, who = (
            (rc.at[s, 1, 2:4], rb.at[s, 0, 2:4], (dpx, z)),
            (rc.at[s, 2, 0:2], rb.at[s, 1, 0:2], (dpy, z)),
            (rc.at[s, 1, 0:2], rb.at[s, 0, 0:2], (dpx, z)),
            (rc.at[s, 2, 2:4], rb.at[s, 1, 2:4], (dpy, z)),
        )[kk]
        return remote(src, dst, s2.at[s, kk], q2.at[s, kk], who)

    def last(s, d):
        zz = (z + d) % T
        return remote(rc.at[s, 0, zz], rz.at[s, d - 1], s3.at[s, d - 1], q3.at[s, d - 1], (dp, zz))

    def add(dst, src):
        @pl.loop(0, dst.shape[0])
        def _(t):
            dst[t] = (dst[t].astype(F32) + src[t].astype(F32)).astype(BF)

    def sum_start(s):
        for kk in (3, 1, 2, 0):
            core_copy(s, kk).start()

    def sum_core(s):
        for kk in (3, 1, 2, 0):
            core_copy(s, kk).wait_recv()
            add(rc.at[s, kk], grad(s).at[:, rowsof(rel[kk]), :])
            if kk == 3:
                turn(s, 0).start()
                turn(s, 1).start()
            if kk == 1:
                straight(s, 0).start()
            if kk == 2:
                straight(s, 1).start()

    def sum_turn(s):
        turn(s, 0).wait_recv()
        add(rc.at[s, 1, 0:2], ra.at[s, 0])
        straight(s, 2).start()
        turn(s, 1).wait_recv()
        add(rc.at[s, 2, 2:4], ra.at[s, 1])
        straight(s, 3).start()

    def sum_straight(s):
        for kk in range(4):
            straight(s, kk).wait_recv()
        add(rc.at[s, 0], rb.at[s, 0])
        add(rc.at[s, 0], rb.at[s, 1])
        for d in range(1, T):
            last(s, d).start()

    def sum_last(s):
        total = rc[s, 0, z].astype(F32)
        for d in range(1, T):
            last(s, d).wait_recv()
            total = total + rz[s, d - 1].astype(F32)
        if s == 0:
            DQ[...] = total[:, 0:W]
            DK[...] = total[:, W:2 * W]
            DV[...] = total[:, 2 * W:3 * W]
            DO[...] = total[:, 3 * W:4 * W].T
        if s == 1:
            D1[...] = total
        if s == 2:
            D2[...] = total.T

    xT[:, 0:M] = low[...].T
    xT[:, M:L] = flow[...].T

    @pl.loop(0, T)
    def _(t):
        @pl.loop(0, M // RB)
        def _(r):
            rr = rows(r)
            gi = (nn(low[rr, :], W_[2, t]) * gp[t, rr, :].astype(F32)).astype(BF)
            gp[t, rr, :] = gi
            SM[pl.ds(2 * T + t, 1), :] += colsum(gi.astype(F32))
            gz[rr, :] += nt(gi, W_[1, t])

        @pl.loop(0, D // RB)
        def _(r):
            W_[2, t, rows(r), :] = nn(xT[rows(r), 0:M], hid[t]).astype(BF)
            W_[1, t, rows(r), :] = nn(xT[rows(r), M:L], gp[t]).astype(BF)

    sum_start(2)
    sum_start(1)

    @pl.loop(0, M // RB)
    def _(r):
        rr = rows(r)
        gf = gz[rr, :]
        n = n1[rr, :]
        g = gf * NP[1:2, :]
        g1 = r1[rr, 0:1] * (g - mean_last(g) - n * mean_last(g * n))
        SM[14:15, :] += colsum(gf * n)
        SM[15:16, :] += colsum(gf)
        SM[12:13, :] += colsum(g1)
        gz[rr, :] = g1
        low[rr, :] = g1.astype(BF)

    xT[:, 0:M] = low[...].T

    @pl.loop(0, T)
    def _(t):
        @pl.loop(0, M // RB)
        def _(r):
            hid[t, rows(r), 0:W] = nn(low[rows(r), :], W_[0, t, :, 3 * W:4 * W]).astype(BF)

        @pl.loop(0, D // RB)
        def _(r):
            G0[t, rows(r), 3 * W:4 * W] = nn(xT[rows(r), 0:M], mixed[t, :, 0:W]).astype(BF)

    @pl.loop(0, T)
    def _(t):
        @pl.when(t == 0)
        def _():
            sum_core(2)

        @pl.when(t == 1)
        def _():
            sum_core(1)

        @pl.when(t == 2)
        def _():
            sum_turn(2)
            hand_on(outb, OF, orcv, 0)

        @pl.when(t == 3)
        def _():
            sum_turn(1)

        vT[...] = k[t, :, 0:W].T
        for pair in range((NH + 1) // 2):
            heads = [j for j in (2 * pair, 2 * pair + 1) if j < NH]
            wide = HD * len(heads)
            dk = jnp.zeros((L, wide), F32)
            dv = jnp.zeros((L, wide), F32)
            for j in heads:
                for i in range(M // QC):
                    qs = slice(i * QC, (i + 1) * QC)
                    qm = only(head(q, t, qs, j), j)
                    om = only(head(hid, t, qs, j), j)
                    s = nt(head(k, t, everything, j), qm) + bias[:, qs]
                    p = jnp.exp(s - lse[t * 4 + j, 0:1, qs])
                    dpr = nt(head(v, t, everything, j), om)
                    cen = jnp.sum(p * dpr, axis=0, keepdims=True)
                    ds = (p * (dpr - cen)).astype(BF)
                    dv = dv + nn(p.astype(BF), om)
                    dk = dk + nn(ds, qm)
                    oT[j * HD:(j + 1) * HD, qs] = nn(vT[j * HD:(j + 1) * HD, :], ds) * scale
            lanes = slice(pair * 128, pair * 128 + wide)
            k[t, :, lanes] = dk.astype(BF)
            v[t, :, lanes] = dv.astype(BF)
        dq = oT[...].T.astype(BF)
        q[t, :, 0:W] = dq
        SM[pl.ds(t, 1), 0:W] += colsum(dq.astype(F32))
        SM[pl.ds(T + t, 1), 0:W] += colsum(v[t, :, 0:W].astype(F32))

    @pl.loop(0, M // RB)
    def _(r):
        acc = jnp.zeros((RB, D), F32)
        for t in range(T):
            acc = acc + nt(k[t, othrows(r), 0:W], W_[0, t, :, W:2 * W])
            acc = acc + nt(v[t, othrows(r), 0:W], W_[0, t, :, 2 * W:3 * W])
        flow[rows(r), :] = acc.astype(BF)

    part = remote(flow, rgt, gs, gr, (dpc, z))
    part.start()

    @pl.loop(0, M // RB)
    def _(r):
        acc = gz[rows(r), :]
        for t in range(T):
            acc = acc + nt(q[t, rows(r), 0:W], W_[0, t, :, 0:W])
            acc = acc + nt(k[t, ownrows(r), 0:W], W_[0, t, :, W:2 * W])
            acc = acc + nt(v[t, ownrows(r), 0:W], W_[0, t, :, 2 * W:3 * W])
        gz[rows(r), :] = acc

    part.wait_recv()
    low[...] = (gz[...] + rgt[...].astype(F32)).astype(BF)
    push(low, GF, gsem, grcv, gsl)

    pals = [(dpc, z), (dpx, z), (dpy, z), (dp, z + 1 - 2 * (z % 2)), (dp, (z + 2) % T)]

    def small(step):
        return remote(ssend.at[step], srecv.at[step], ms.at[step], mr.at[step], pals[step])

    def small_start(step):
        ssend[step] = SM[...]
        small(step).start()

    def small_end(step):
        small(step).wait_recv()
        SM[...] += srecv[step]

    small_start(0)
    sum_straight(2)

    xT[...] = X[...].T

    @pl.loop(0, T)
    def _(t):
        @pl.loop(0, D // RB)
        def _(r):
            rr = rows(r)
            G0[t, rr, 0:W] = nn(xT[rr, pl.ds(pl.multiple_of(own, 128), M)], q[t, :, 0:W]).astype(BF)
            G0[t, rr, W:2 * W] = nn(xT[rr, :], k[t, :, 0:W]).astype(BF)
            G0[t, rr, 2 * W:3 * W] = nn(xT[rr, :], v[t, :, 0:W]).astype(BF)

    sum_start(0)
    small_end(0)
    small_start(1)
    sum_straight(1)
    sum_core(0)
    small_end(1)
    small_start(2)
    sum_last(2)
    sum_turn(0)
    small_end(2)
    small_start(3)
    sum_last(1)
    small_end(3)
    small_start(4)
    hand_on(low, GF, grcv, 2)
    small_end(4)
    sum_straight(0)
    sum_last(0)

    BQ[...] = SM[pl.ds(z, 1), 0:W]
    BV[...] = SM[pl.ds(T + z, 1), 0:W]
    B1[...] = SM[pl.ds(2 * T + z, 1), :]
    VEC[...] = SM[3 * T:3 * T + 8, :]
    settle(outb, OF, orcv, 0)
    settle(low, GF, grcv, 2)
    pushed(outb, OF, osem, orcv, osl)
    pushed(low, GF, gsem, grcv, gsl)
    part.wait_send()
    for step in range(5):
        small(step).wait_send()
    for s in range(SL):
        for kk in range(4):
            core_copy(s, kk).wait_send()
            straight(s, kk).wait_send()
        turn(s, 0).wait_send()
        turn(s, 1).wait_send()
        for d in range(1, T):
            last(s, d).wait_send()


def layer_call(wq, wk, wv, wo, w1, w2t, norms, biases, lengths, tokens, cotangent, T):
    S, W = wq.shape
    D = tokens.shape[1]
    F = w1.shape[1]
    L = tokens.shape[0] // lengths.shape[0]
    M = L // 2
    SL = 3
    WP = 256
    any_ = pl.BlockSpec(memory_space=pl.ANY)
    vm = pl.BlockSpec(memory_space=pltpu.VMEM)
    dma = pltpu.SemaphoreType.DMA
    f32 = lambda *s: jax.ShapeDtypeStruct(s, F32)
    V = pltpu.VMEM
    return pl.pallas_call(
        layer_kernel,
        in_specs=[vm] * 8 + [pl.BlockSpec(memory_space=pltpu.SMEM), any_, any_],
        out_specs=[any_, any_] + [vm] * 10,
        out_shape=[
            jax.ShapeDtypeStruct((4 * M, D), BF),
            jax.ShapeDtypeStruct((4 * M, D), BF),
            f32(S, W), f32(S, W), f32(S, W), f32(W, S), f32(S, F), f32(F, S),
            f32(1, W), f32(1, W), f32(1, F), f32(8, D),
        ],
        scratch_shapes=[
            V((SL, S, D), BF),
            V((SL, T, D, F), BF),
            V((T, D, D), BF),
            V((L, D), BF),
            V((M, D), BF),
            V((2, 8, L), F32),
            V((T, 8, D), F32),
            V((24, D), F32),
            V((T, M, WP), BF),
            V((T, L, WP), BF),
            V((T, L, WP), BF),
            V((T, M, WP), BF),
            V((W, L), BF),
            V((W, M), F32),
            V((T * 4, 8, M), F32),
            V((L, M), F32),
            V((M, D), F32),
            V((M, 128), F32),
            V((M, D), BF),
            V((T, M, F), BF),
            V((T, M, F), BF),
            V((M, D), F32),
            V((M, D), BF),
            V((D, L), BF),
            V((M, D), BF),
            V((M, D), BF),
            V((SL, 4, T, S, D), BF),
            V((SL, 2, 2, S, D), BF),
            V((SL, 2, T, S, D), BF),
            V((SL, T - 1, S, D), BF),
            V((5, 24, D), F32),
            V((5, 24, D), F32),
            dma((2,)),
            dma((SL, T - 1)), dma((SL, T - 1)),
            dma((3, SL, T)), dma((SL, T)), dma((SL, T)), dma((4, SL, T)),
            dma((SL, T)), dma((SL, T)),
            dma((3, SL, T)),
            dma((T - 1,)), dma((T - 1,)),
            dma((3,)), dma((3,)),
            dma, dma,
            dma((5,)), dma((4,)), dma,
            dma((5,)), dma((4,)), dma,
            dma((4,)),
            dma((SL, 4)), dma((SL, 4)),
            dma((SL, 2)), dma((SL, 2)),
            dma((SL, 4)), dma((SL, 4)),
            dma((SL, T - 1)), dma((SL, T - 1)),
            dma((5,)), dma((5,)),
        ],
        compiler_params=pltpu.CompilerParams(
            collective_id=0, has_side_effects=True, vmem_limit_bytes=64 << 20
        ),
    )(wq, wk, wv, wo, w1, w2t, norms, biases, lengths, tokens, cotangent)


def doc_ids(lengths, count):
    ends = jnp.cumsum(lengths)
    places = jnp.arange(count, dtype=jnp.int32)
    return jnp.sum((places[:, None] >= ends[None, :]).astype(jnp.int32), axis=1)


def collect(wq, wk, wv, wo, w1, w2):
    return (
        lax.all_gather(wq, "dp", axis=0, tiled=True),
        lax.all_gather(wk, "dp", axis=0, tiled=True),
        lax.all_gather(wv, "dp", axis=0, tiled=True),
        lax.all_gather(wo, "dp", axis=1, tiled=True),
        lax.all_gather(w1, "dp", axis=0, tiled=True),
        lax.all_gather(w2, "dp", axis=1, tiled=True),
    )


def reduce_large(grads):
    return (
        lax.psum_scatter(grads[0], "dp", scatter_dimension=0, tiled=True),
        lax.psum_scatter(grads[1], "dp", scatter_dimension=0, tiled=True),
        lax.psum_scatter(grads[2], "dp", scatter_dimension=0, tiled=True),
        lax.psum_scatter(grads[3], "dp", scatter_dimension=1, tiled=True),
        lax.psum_scatter(grads[4], "dp", scatter_dimension=0, tiled=True),
        lax.psum_scatter(grads[5], "dp", scatter_dimension=1, tiled=True),
    )


def reduce_small(grads):
    return lax.psum(
        (grads[0], grads[1], grads[2], grads[3], grads[4], grads[5], grads[6], grads[7], grads[8]),
        "dp",
    )


def contract_rows(left, right):
    return lax.dot_general(
        left, right, (((0,), (0,)), ((), ())), preferred_element_type=jnp.float32
    )


def contract_cols(left, right):
    return lax.dot_general(
        left, right, (((1,), (1,)), ((), ())), preferred_element_type=jnp.float32
    )


def contract_mixed(left, right):
    return lax.dot_general(
        left, right, (((0,), (1,)), ((), ())), preferred_element_type=jnp.float32
    )


def norm_forward(total, gain, shift):
    centre = total - jnp.mean(total, axis=-1, keepdims=True)
    scaled = lax.rsqrt(jnp.mean(centre * centre, axis=-1, keepdims=True) + EPS)
    normed = centre * scaled
    return (normed * gain + shift, normed, scaled)


def norm_backward(grad_result, normed, scaled, gain):
    grad_normed = grad_result * gain
    mean_grad = jnp.mean(grad_normed, axis=-1, keepdims=True)
    mean_cross = jnp.mean(grad_normed * normed, axis=-1, keepdims=True)
    grad_total = scaled * (grad_normed - mean_grad - normed * mean_cross)
    return (grad_total, jnp.sum(grad_result * normed, axis=0), jnp.sum(grad_result, axis=0))


def block_scores(query_block, key_heads, seg_block, seg, scale):
    raw = (
        jnp.einsum("hdq,hdk->hqk", query_block, key_heads, preferred_element_type=jnp.float32)
        * scale
    )
    same_doc = seg_block[:, None] == seg[None, :]
    return jnp.where(same_doc[None], raw, NEG)


def general_body(
    tokens,
    doc_lengths,
    wq,
    bq,
    wk,
    wv,
    bv,
    wo,
    bo,
    gain1,
    shift1,
    w1,
    b1,
    w2,
    b2,
    gain2,
    shift2,
    cotangent,
):
    micro = doc_lengths.shape[0]
    seq_len = tokens.shape[0] // micro
    block = min(512, seq_len)
    scale = HD ** (-0.5)
    results = []
    grad_inputs = []
    large_total = None
    small_total = None
    for index in range(micro):
        full = collect(wq, wk, wv, wo, w1, w2)
        full_q, full_k, full_v, full_o, full_first, full_second = full
        width = full_q.shape[1]
        heads_here = width // HD
        rows_in = tokens[index * seq_len : (index + 1) * seq_len]
        inputs = rows_in.astype(jnp.float32)
        seg = doc_ids(doc_lengths[index], seq_len)
        queries = (
            lax.dot_general(
                full_q, rows_in, (((0,), (1,)), ((), ())), preferred_element_type=jnp.float32
            )
            + bq[:, None]
        ).astype(jnp.bfloat16)
        keys_low = lax.dot_general(
            full_k, rows_in, (((0,), (1,)), ((), ())), preferred_element_type=jnp.float32
        ).astype(jnp.bfloat16)
        values_low = (
            lax.dot_general(
                full_v, rows_in, (((0,), (1,)), ((), ())), preferred_element_type=jnp.float32
            )
            + bv[:, None]
        ).astype(jnp.bfloat16)
        query_heads = queries.reshape(heads_here, HD, seq_len)
        key_heads = keys_low.reshape(heads_here, HD, seq_len)
        value_heads = values_low.reshape(heads_here, HD, seq_len)
        pieces = []
        log_totals = []
        for offset in range(0, seq_len, block):
            scores = block_scores(
                query_heads[:, :, offset : offset + block],
                key_heads,
                seg[offset : offset + block],
                seg,
                scale,
            )
            highest = jnp.max(scores, axis=-1, keepdims=True)
            log_total = highest + jnp.log(
                jnp.sum(jnp.exp(scores - highest), axis=-1, keepdims=True)
            )
            probs_low = jnp.exp(scores - log_total).astype(jnp.bfloat16)
            pieces.append(
                jnp.einsum(
                    "hqk,hdk->hdq", probs_low, value_heads, preferred_element_type=jnp.float32
                )
            )
            log_totals.append(log_total)
        mixed_cols = jnp.concatenate(pieces, axis=2).reshape(width, seq_len).astype(jnp.bfloat16)
        attended = lax.psum(
            contract_rows(mixed_cols, full_o).astype(jnp.bfloat16), "tensor"
        ).astype(jnp.float32)
        first, normed_one, scaled_one = norm_forward(inputs + attended + bo, gain1, shift1)
        first_low = first.astype(jnp.bfloat16)
        inner = jnp.dot(first_low, full_first, preferred_element_type=jnp.float32) + b1
        hidden = jax.nn.gelu(inner, approximate=False).astype(jnp.bfloat16)
        second = lax.psum(
            jnp.dot(hidden, full_second, preferred_element_type=jnp.float32).astype(jnp.bfloat16),
            "tensor",
        ).astype(jnp.float32)
        result, normed_two, scaled_two = norm_forward(first + second + b2, gain2, shift2)
        results.append(result.astype(jnp.bfloat16))
        grad_result = cotangent[index * seq_len : (index + 1) * seq_len].astype(jnp.float32)
        grad_two, grad_gain2, grad_shift2 = norm_backward(
            grad_result, normed_two, scaled_two, gain2
        )
        grad_b2 = jnp.sum(grad_two, axis=0)
        full = collect(wq, wk, wv, wo, w1, w2)
        full_q, full_k, full_v, full_o, full_first, full_second = full
        two_low = grad_two.astype(jnp.bfloat16)
        grad_w2 = contract_rows(hidden, two_low)
        grad_hidden = contract_cols(two_low, full_second)
        grad_inner = jax.vjp(partial(jax.nn.gelu, approximate=False), inner)[1](grad_hidden)[
            0
        ].astype(jnp.bfloat16)
        grad_b1 = jnp.sum(grad_inner.astype(jnp.float32), axis=0)
        grad_w1 = contract_rows(first_low, grad_inner)
        grad_first = grad_two + lax.psum(
            contract_cols(grad_inner, full_first).astype(jnp.bfloat16), "tensor"
        ).astype(jnp.float32)
        grad_one, grad_gain1, grad_shift1 = norm_backward(grad_first, normed_one, scaled_one, gain1)
        grad_bo = jnp.sum(grad_one, axis=0)
        one_low = grad_one.astype(jnp.bfloat16)
        grad_wo = jnp.dot(mixed_cols, one_low, preferred_element_type=jnp.float32)
        grad_mixed = (
            contract_cols(full_o, one_low).astype(jnp.bfloat16).reshape(heads_here, HD, seq_len)
        )
        grad_key_heads = jnp.zeros((heads_here, HD, seq_len), jnp.float32)
        grad_value_heads = jnp.zeros((heads_here, HD, seq_len), jnp.float32)
        grad_query_pieces = []
        for number, offset in enumerate(range(0, seq_len, block)):
            query_block = query_heads[:, :, offset : offset + block]
            grad_block = grad_mixed[:, :, offset : offset + block]
            scores = block_scores(query_block, key_heads, seg[offset : offset + block], seg, scale)
            probs = jnp.exp(scores - log_totals[number])
            grad_probs = jnp.einsum(
                "hdq,hdk->hqk", grad_block, value_heads, preferred_element_type=jnp.float32
            )
            centre = jnp.sum(probs * grad_probs, axis=-1, keepdims=True)
            grad_scores = (probs * (grad_probs - centre)).astype(jnp.bfloat16)
            grad_query_pieces.append(
                jnp.einsum(
                    "hqk,hdk->hdq", grad_scores, key_heads, preferred_element_type=jnp.float32
                )
                * scale
            )
            grad_key_heads = (
                grad_key_heads
                + jnp.einsum(
                    "hqk,hdq->hdk", grad_scores, query_block, preferred_element_type=jnp.float32
                )
                * scale
            )
            grad_value_heads = grad_value_heads + jnp.einsum(
                "hqk,hdq->hdk",
                probs.astype(jnp.bfloat16),
                grad_block,
                preferred_element_type=jnp.float32,
            )
        grad_queries = (
            jnp.concatenate(grad_query_pieces, axis=2).reshape(width, seq_len).astype(jnp.bfloat16)
        )
        grad_keys = grad_key_heads.reshape(width, seq_len).astype(jnp.bfloat16)
        grad_values = grad_value_heads.reshape(width, seq_len).astype(jnp.bfloat16)
        grad_bq = jnp.sum(grad_queries.astype(jnp.float32), axis=1)
        grad_bv = jnp.sum(grad_values.astype(jnp.float32), axis=1)
        grad_wq = contract_cols(rows_in.T, grad_queries)
        grad_wk = contract_cols(rows_in.T, grad_keys)
        grad_wv = contract_cols(rows_in.T, grad_values)
        back_terms = (
            contract_mixed(grad_queries, full_q)
            + contract_mixed(grad_keys, full_k)
            + contract_mixed(grad_values, full_v)
        )
        grad_rows = grad_one + lax.psum(back_terms.astype(jnp.bfloat16), "tensor").astype(
            jnp.float32
        )
        grad_inputs.append(grad_rows.astype(jnp.bfloat16))
        large_local = (grad_wq, grad_wk, grad_wv, grad_wo, grad_w1, grad_w2)
        small_local = (
            grad_bq,
            grad_bv,
            grad_b1,
            grad_bo,
            grad_b2,
            grad_gain1,
            grad_shift1,
            grad_gain2,
            grad_shift2,
        )
        large_local = reduce_large(large_local)
        small_local = reduce_small(small_local)
        if large_total is None:
            large_total = large_local
            small_total = small_local
        else:
            large_total = jax.tree.map(jnp.add, large_total, large_local)
            small_total = jax.tree.map(jnp.add, small_total, small_local)
    grad_wq, grad_wk, grad_wv, grad_wo, grad_w1, grad_w2 = large_total
    (
        grad_bq,
        grad_bv,
        grad_b1,
        grad_bo,
        grad_b2,
        grad_gain1,
        grad_shift1,
        grad_gain2,
        grad_shift2,
    ) = small_total
    return (
        jnp.concatenate(results, axis=0),
        jnp.concatenate(grad_inputs, axis=0),
        grad_wq,
        grad_bq,
        grad_wk,
        grad_wv,
        grad_bv,
        grad_wo,
        grad_bo,
        grad_gain1,
        grad_shift1,
        grad_w1,
        grad_b1,
        grad_w2,
        grad_b2,
        grad_gain2,
        grad_shift2,
    )


def split_body(T, tokens, doc_lengths, wq, bq, wk, wv, bv, wo, bo, gain1, shift1, w1, b1, w2, b2,
               gain2, shift2, cotangent):
    S, W = wq.shape
    D = tokens.shape[1]
    F = w1.shape[1]
    row = lambda x: jnp.pad(x[None, :], ((0, 0), (0, D - x.shape[0])))
    biases = jnp.concatenate([row(b1), row(bq), row(bv), jnp.zeros((5, D), F32)])
    norms = jnp.stack([bo, gain1, shift1, b2, gain2, shift2, bo, bo])
    (full, grads, dq, dk, dv, do, d1, d2, gbq, gbv, gb1, vec) = layer_call(
        wq, wk, wv, wo, w1, w2.T, norms, biases, doc_lengths, tokens, cotangent, T)
    return (full, grads, dq, gbq[0], dk, dv, gbv[0], do, vec[0], vec[2], vec[3], d1, gb1[0], d2,
            vec[1], vec[4], vec[5])


def solution(mesh):
    placed = (
        P("dp", None),
        P("dp", None),
        P("dp", "tensor"),
        P("tensor"),
        P("dp", "tensor"),
        P("dp", "tensor"),
        P("tensor"),
        P("tensor", "dp"),
        P(),
        P(),
        P(),
        P("dp", "tensor"),
        P("tensor"),
        P("tensor", "dp"),
        P(),
        P(),
        P(),
        P("dp", None),
    )
    if mesh.shape["dp"] == 8 and mesh.shape["tensor"] == 4:
        body = partial(split_body, mesh.shape["tensor"])
    else:
        body = general_body
    return jax.shard_map(
        body,
        mesh=mesh,
        in_specs=placed,
        out_specs=(
            P("dp", None),
            P("dp", None),
            P("dp", "tensor"),
            P("tensor"),
            P("dp", "tensor"),
            P("dp", "tensor"),
            P("tensor"),
            P("tensor", "dp"),
            P(),
            P(),
            P(),
            P("dp", "tensor"),
            P("tensor"),
            P("tensor", "dp"),
            P(),
            P(),
            P(),
        ),
        check_vma=False,
    )
```

```python
from functools import partial
import jax
import jax.numpy as jnp
from jax import lax
from jax.experimental import pallas as pl
from jax.experimental.pallas import tpu as pltpu

from jax.sharding import PartitionSpec as P

BF = jnp.bfloat16
F32 = jnp.float32
EPS = 1e-12
HD = 64
NEG = -1e30
RB = 256


def nn(a, b):
    return jnp.dot(a, b, preferred_element_type=F32)


def nt(a, b):
    return lax.dot_general(a, b, (((1,), (1,)), ((), ())), preferred_element_type=F32)


def rows(r, n=RB):
    return pl.ds(pl.multiple_of(r * n, n), n)


def mean_last(x):
    return jnp.mean(x, axis=-1, keepdims=True)


def colsum(x):
    return jnp.sum(x, axis=0, keepdims=True)


MESH = pl.DeviceIdType.MESH


def remote(src, dst, send, recv, device):
    return pltpu.make_async_remote_copy(
        src_ref=src, dst_ref=dst, send_sem=send, recv_sem=recv, device_id=device, device_id_type=MESH
    )


def layer_kernel(
    WQ, WK, WV, WO, W1, W2T, BO_, GAIN1, SHIFT1, B2_, GAIN2, SHIFT2, B1_, BQ_, BV_, LEN, TOK, COT,
    OF, GF, GR, SMO,
    PK, W_, X, CO, SG, NP, BP, BI, SM,
    q, k, v, mixed, vT, oT, lse, bias, n1, r1, flow, hid, gp, gz, low, xT,
    rgt, rc, ra, rb, rz, ssend, srecv,
    loc, zs, zf, zr, os_, xr, yr, cr, fs, dr, ks, bs, br, ts, tr,
    gs, gr, osem, orcv, osl, gsem, grcv, gsl, fwd, cs, crr, s1, q1, s2, q2, s3, q3, ms, mr,
):
    SL, S, D = PK.shape
    T = W_.shape[1]
    L = X.shape[0]
    M = L // 2
    W = D // T
    NH = W // HD
    scale = HD ** (-0.5)
    QC = RB

    dp = lax.axis_index("dp")
    z = lax.axis_index("tensor")
    core = dp % 2
    dpc = dp + 1 - 2 * core
    dpx = dp + 2 - 4 * ((dp // 2) % 2)
    dpy = dp + 4 - 8 * ((dp // 4) % 2)
    dpxy = dpx + dpy - dp
    flip = dpc - dp
    home = z // 2
    own = core * M
    oth = (1 - core) * M

    def ownrows(r):
        return pl.ds(pl.multiple_of(own + r * RB, RB), RB)

    def othrows(r):
        return pl.ds(pl.multiple_of(oth + r * RB, RB), RB)

    ownhalf = pl.ds(pl.multiple_of(own, M), M)
    othhalf = pl.ds(pl.multiple_of(oth, M), M)

    PK[0, :, 0:W] = WQ[...]
    PK[0, :, W:2 * W] = WK[...]
    PK[0, :, 2 * W:3 * W] = WV[...]
    PK[0, :, 3 * W:4 * W] = WO[...].T
    PK[1] = W1[...]
    PK[2] = W2T[...]
    for i, ref in enumerate((BO_, GAIN1, SHIFT1, B2_, GAIN2, SHIFT2)):
        NP[i:i + 1, :] = ref[...].reshape(1, D)
    BP[0:1, :] = B1_[...].reshape(1, D)
    BP[1:2, 0:W] = BQ_[...].reshape(1, W)
    BP[2:3, 0:W] = BV_[...].reshape(1, W)

    spot = lax.broadcasted_iota(jnp.int32, (8, L), 1)
    doc = jnp.zeros((8, L), F32)
    end = jnp.int32(0)
    for j in range(LEN.shape[1]):
        end = end + LEN[z % 2, j]
        doc = doc + jnp.where(spot >= end, 1.0, 0.0)
    SG[0] = doc

    barrier = pltpu.get_barrier_semaphore()
    friends = [(dp, (z + d) % T) for d in range(1, T)] + [(dpc, (z + d) % T) for d in range(T)] + [
        (dpx, z), (dpy, z)]
    for friend in friends:
        pl.semaphore_signal(barrier, inc=1, device_id=friend, device_id_type=MESH)
    pl.semaphore_wait(barrier, len(friends))

    def block(s, t, i):
        return W_.at[s, t, pl.ds(pl.multiple_of(i * S, S), S), :]

    half = z // 2

    def source(d):
        edge = z + half * (3 - 2 * z)
        swap = edge * (1 - d // 2)
        t = swap * (1 - d) + (1 - swap) * d
        return t + half * (3 - 2 * t)

    right, left = (dp, (z + 1) % T), (dp, (z + T - 1) % T)
    can_right, can_left = z < T - 1, z > 0

    def send_z(s):
        return (
            (can_right, remote(PK.at[s], block(s, z, dp), zs.at[s, 0], zr.at[s, z], right)),
            (can_left, remote(PK.at[s], block(s, z, dp), zs.at[s, 1], zr.at[s, z], left)),
        )

    def pass_z(s, t):
        here = block(s, t, dp)
        return (
            (can_right & (t < z), remote(here, here, zf.at[s, t], zr.at[s, t], right)),
            (can_left & (t > z), remote(here, here, zf.at[s, t], zr.at[s, t], left)),
        )

    def push_z(s):
        for able, copy in send_z(s):
            pl.when(able)(copy.start)

    def send_block(s, d, src):
        t = source(d)
        remote(src, block(s, t, dp), os_.at[0, s, d], xr.at[s, d], (dpx, z)).start()
        remote(src, block(s, t, dp), os_.at[1, s, d], yr.at[s, d], (dpy, z)).start()
        remote(src, block(s, t, dp), os_.at[2, s, d], cr.at[0, s, d], (dpc, z)).start()

    def pass_core(kind, s, d, i):
        t = source(d)
        remote(block(s, t, i), block(s, t, i), ks.at[kind - 1, s, d], cr.at[kind, s, d], (dpc, z)).start()

    def take_z(s, d):
        t = source(d)
        remote(PK.at[s], block(s, t, dp), zs.at[s, 0], zr.at[s, t], right).wait_recv()
        for able, copy in pass_z(s, t):
            pl.when(able)(copy.start)
        send_block(s, d, block(s, t, dp))

    def take_x(s, d):
        t = source(d)
        remote(PK.at[s], block(s, t, dpx), os_.at[0, s, d], xr.at[s, d], (dpx, z)).wait_recv()

        @pl.when(d < T // 2)
        def _():
            remote(block(s, t, dpx), block(s, t, dpx), fs.at[s, d], dr.at[s, d], (dpy, z)).start()

        pass_core(1, s, d, dpx)

    def take_y(s, d):
        t = source(d)
        remote(PK.at[s], block(s, t, dpy), os_.at[1, s, d], yr.at[s, d], (dpy, z)).wait_recv()

        @pl.when(d >= T // 2)
        def _():
            remote(block(s, t, dpy), block(s, t, dpy), fs.at[s, d], dr.at[s, d], (dpx, z)).start()

        pass_core(2, s, d, dpy)

    def take_diag(s, d):
        remote(PK.at[s], block(s, source(d), dpxy), fs.at[s, d], dr.at[s, d], (dpx, z)).wait_recv()
        pass_core(3, s, d, dpxy)

    PIECES = SL * T
    XL, DL = 2, 4
    STEPS = PIECES + DL
    first_steps = DL + 1

    def gather_step(n):
        n = jnp.int32(n)

        @pl.when(n < PIECES)
        def _():
            s, d = n // T, n % T

            @pl.when(d > 0)
            def _():
                take_z(s, d)

            @pl.when(d == 0)
            def _():
                send_block(s, d, PK.at[s])

        @pl.when((n >= XL) & (n < PIECES + XL))
        def _():
            take_x((n - XL) // T, (n - XL) % T)
            take_y((n - XL) // T, (n - XL) % T)

        @pl.when((n >= DL) & (n < PIECES + DL))
        def _():
            take_diag((n - DL) // T, (n - DL) % T)

    def gathered(s, d):
        for kind, i in enumerate((dpc, dpx + flip, dpy + flip, dpxy + flip)):
            remote(PK.at[s], block(s, source(d), i), os_.at[2, s, d], cr.at[kind, s, d], (dpc, z)).wait_recv()

    for s in range(SL):
        push_z(s)
    seq = pl.ds(pl.multiple_of((z % 2) * L, L), L)
    mine = pl.ds(pl.multiple_of((z % 2) * L + own, M), M)
    other = pl.ds(pl.multiple_of((z % 2) * L + oth, M), M)
    tok_out = remote(TOK.at[seq], X, ts.at[0], tr.at[0], (dpc, z))
    cot_out = remote(COT.at[other], CO, ts.at[1], tr.at[1], (dpc, z))
    doc_out = remote(SG.at[0], SG.at[1], ts.at[2], tr.at[2], (dpc, z))
    tok_in = pltpu.make_async_copy(TOK.at[seq], X, loc.at[0])
    cot_in = pltpu.make_async_copy(COT.at[mine], CO, loc.at[1])

    @pl.when(core == home)
    def _():
        for copy in (tok_out, cot_out, doc_out, tok_in, cot_in):
            copy.start()

    for d in range(1, T):
        remote(BP, BI.at[z], bs.at[d - 1], br.at[d - 1], (dp, (z + d) % T)).start()
    for s in range(SL):
        W_[s, z, pl.ds(pl.multiple_of(dp * S, S), S), :] = PK[s]
    BI[z] = BP[...]
    SM[...] = jnp.zeros_like(SM)

    @pl.loop(0, 2)
    def _(n):
        gather_step(n)

    @pl.when(core == home)
    def _():
        tok_in.wait()
        cot_in.wait()
        for copy in (tok_out, cot_out, doc_out):
            copy.wait_send()

    @pl.when(core != home)
    def _():
        for copy in (tok_out, cot_out, doc_out):
            copy.wait_recv()

    for d in range(1, T):
        remote(BP, BI.at[(z - d + T) % T], bs.at[d - 1], br.at[d - 1], (dp, (z + 1) % T)).wait_recv()

    docs = jnp.where(core == home, SG[0], SG[1])
    SG[0] = docs
    key_doc = jnp.broadcast_to(docs[0:1, :], (128, L)).T
    for i in range(M // 128):
        query_doc = SG[0, 0:1, pl.ds(pl.multiple_of(own + i * 128, 128), 128)]
        bias[:, i * 128:(i + 1) * 128] = jnp.where(key_doc == query_doc, 0.0, NEG)

    @pl.loop(2, first_steps)
    def _(n):
        gather_step(n)

    @pl.loop(0, T)
    def _(d):
        gather_step(first_steps + d)
        gathered(0, d)
        t = source(d)
        mine_qkv = nn(X[ownhalf, :], W_[0, t, :, 0:3 * W])
        q[t, :, 0:W] = ((mine_qkv[:, 0:W] + BI[t, 1:2, 0:W]).astype(BF) * BF(scale)).astype(BF)
        k[t, ownhalf, 0:W] = mine_qkv[:, W:2 * W].astype(BF)
        v[t, ownhalf, 0:W] = (mine_qkv[:, 2 * W:3 * W] + BI[t, 2:3, 0:W]).astype(BF)
        their_kv = nn(X[othhalf, :], W_[0, t, :, W:3 * W])
        k[t, othhalf, 0:W] = their_kv[:, 0:W].astype(BF)
        v[t, othhalf, 0:W] = (their_kv[:, W:2 * W] + BI[t, 2:3, 0:W]).astype(BF)

    lane = lax.broadcasted_iota(jnp.int32, (1, 128), 1)

    def head(ref, t, rr, j):
        if j % 2 == 0 and j == NH - 1:
            return ref[t, rr, j * HD:(j + 1) * HD]
        p = j // 2
        return ref[t, rr, p * 128:(p + 1) * 128]

    def only(part, j):
        if part.shape[1] == HD:
            return part
        keep = (lane < HD) if j % 2 == 0 else (lane >= HD)
        return jnp.where(keep, part, jnp.zeros_like(part))

    everything = slice(None)

    @pl.loop(0, T)
    def _(t):
        gather_step(first_steps + T + t)
        vT[...] = v[t, :, 0:W].T

        for i in range(M // QC):
            qs = slice(i * QC, (i + 1) * QC)
            for j in range(NH):
                s = nt(head(k, t, everything, j), only(head(q, t, qs, j), j)) + bias[:, qs]
                m = jnp.max(s, axis=0, keepdims=True)
                p = jnp.exp(s - m)
                l = jnp.sum(p, axis=0, keepdims=True)
                lse[t * 4 + j, :, qs] = jnp.broadcast_to(m + jnp.log(l), (8, QC))
                o = nn(vT[j * HD:(j + 1) * HD, :], p.astype(BF))
                oT[j * HD:(j + 1) * HD, qs] = o * (1.0 / l)

        mixed[t, :, 0:W] = oT[...].T.astype(BF)

    @pl.loop(0, M // RB)
    def _(r):
        zz = X[ownrows(r), :].astype(F32) + NP[0:1, :]
        for t in range(T):
            zz = zz + nt(mixed[t, rows(r), 0:W], W_[0, t, :, 3 * W:4 * W])
        cen = zz - mean_last(zz)
        rs = lax.rsqrt(mean_last(cen * cen) + EPS)
        n = cen * rs
        n1[rows(r), :] = n
        r1[rows(r), :] = jnp.broadcast_to(rs, (RB, 128))
        flow[rows(r), :] = (n * NP[1:2, :] + NP[2:3, :]).astype(BF)

    @pl.loop(0, T)
    def _(d):
        gather_step(first_steps + 2 * T + d)
        gathered(1, d)
        t = source(d)
        inner = nn(flow[...], W_[1, t]) + BI[t, 0:1, :]
        phi = 0.5 * (1.0 + lax.erf(inner * (2.0 ** -0.5)))
        hid[t] = (inner * phi).astype(BF)
        gp[t] = (phi + inner * (jnp.exp(-0.5 * inner * inner) * 0.3989422804014327)).astype(BF)

    gz[...] = n1[...] * NP[1:2, :] + NP[2:3, :] + NP[3:4, :]

    @pl.loop(0, T)
    def _(d):
        gathered(2, d)
        t = source(d)
        gz[...] += nt(hid[t], W_[2, t])

    @pl.loop(0, M // RB)
    def _(r):
        rr = rows(r)
        zz = gz[rr, :]
        cen = zz - mean_last(zz)
        rs = lax.rsqrt(mean_last(cen * cen) + EPS)
        n = cen * rs
        ct = CO[rr, :].astype(F32)
        CO[rr, :] = (n * NP[4:5, :] + NP[5:6, :]).astype(BF)
        g = ct * NP[4:5, :]
        g2 = rs * (g - mean_last(g) - n * mean_last(g * n))
        SM[16:17, :] += colsum(ct * n)
        SM[17:18, :] += colsum(ct)
        SM[13:14, :] += colsum(g2)
        gz[rr, :] = g2
        low[rr, :] = g2.astype(BF)

    dest = dp - core + home

    def spotrows(zz, cc):
        return pl.ds(pl.multiple_of(((zz % 2) * 2 + cc) * M, M), M)

    def pushes(src, full, sems, recv):
        return [
            (able, remote(src, full.at[spotrows(z, core)], sems.at[i], recv.at[(z % 2) * 2 + core], (dest, chip)))
            for i, (able, chip) in enumerate(((can_right, (z + 1) % T), (can_left, (z + T - 1) % T)))
        ]

    def own_copy(src, full, sems, recv, slot):
        away = remote(src, full.at[spotrows(z, core)], sems.at[2], recv.at[(z % 2) * 2 + core], (dpc, z))
        here = pltpu.make_async_copy(src, full.at[spotrows(z, core)], slot)
        return away, here

    def push(src, full, sems, recv, slot):
        for able, copy in pushes(src, full, sems, recv):
            pl.when(able)(copy.start)
        away, here = own_copy(src, full, sems, recv, slot)
        pl.when(core != home)(away.start)
        pl.when(core == home)(here.start)

    def pushed(src, full, sems, recv, slot):
        for able, copy in pushes(src, full, sems, recv):
            pl.when(able)(copy.wait_send)
        away, here = own_copy(src, full, sems, recv, slot)
        pl.when(core != home)(away.wait_send)
        pl.when(core == home)(here.wait)

    ahead = 1 - 2 * core

    def moves(hop):
        if hop == 0:
            return (z == 1) | (z == 2)
        return z == 2 - core

    def got(src, full, recv, b, cc):
        remote(src, full.at[spotrows(b, cc)], gs, recv.at[(b % 2) * 2 + cc], (dpx, z)).wait_recv()

    def handing(full, recv, base, hop, cc):
        b = z - ahead * (hop + 1)
        return remote(full.at[spotrows(b, cc)], full.at[spotrows(b, cc)], fwd.at[base + 2 * hop + cc],
                      recv.at[(b % 2) * 2 + cc], (dp, (z + ahead) % T))

    def hand_on(src, full, recv, base, hop):
        @pl.when(moves(hop))
        def _():
            for cc in range(2):
                got(src, full, recv, z - ahead * (hop + 1), cc)
                handing(full, recv, base, hop, cc).start()

    def settle(src, full, recv, base):
        for kk in range(2):
            for cc in range(2):
                b = core * 2 + kk
                gone = (moves(0) & (b == z - ahead)) | (moves(1) & (b == z - 2 * ahead))

                @pl.when(jnp.logical_not((b == z) & (core == cc)) & jnp.logical_not(gone))
                def _():
                    got(src, full, recv, b, cc)

        for hop in range(2):
            @pl.when(moves(hop))
            def _():
                for cc in range(2):
                    handing(full, recv, base, hop, cc).wait_send()

    push(CO, OF, osem, orcv, osl)

    for s in range(SL):
        for able, copy in send_z(s):
            pl.when(able)(copy.wait_send)
        for t in range(T):
            for able, copy in pass_z(s, t):
                pl.when(able)(copy.wait_send)
        for d in range(T):
            for kind in range(3):
                remote(PK.at[s], block(s, z, dp), os_.at[kind, s, d], xr.at[s, d], (dpx, z)).wait_send()
                remote(PK.at[s], block(s, z, dp), ks.at[kind, s, d], xr.at[s, d], (dpx, z)).wait_send()
            remote(PK.at[s], block(s, z, dp), fs.at[s, d], xr.at[s, d], (dpx, z)).wait_send()
    for d in range(1, T):
        remote(BP, BI.at[z], bs.at[d - 1], br.at[d - 1], (dp, (z + d) % T)).wait_send()

    def grad(s):
        return W_.at[s]

    rel = (dp, dpx, dpy, dpxy)

    def rowsof(i):
        return pl.ds(pl.multiple_of(i * S, S), S)

    def core_copy(s, kk):
        return remote(grad(s).at[:, rowsof(rel[kk] + flip), :], rc.at[s, kk], cs.at[s, kk], crr.at[s, kk], (dpc, z))

    def turn(s, kk):
        src, dst, who = (
            (rc.at[s, 3, 0:2], ra.at[s, 0], (dpy, z)),
            (rc.at[s, 3, 2:4], ra.at[s, 1], (dpx, z)),
        )[kk]
        return remote(src, dst, s1.at[s, kk], q1.at[s, kk], who)

    def straight(s, kk):
        src, dst, who = (
            (rc.at[s, 1, 2:4], rb.at[s, 0, 2:4], (dpx, z)),
            (rc.at[s, 2, 0:2], rb.at[s, 1, 0:2], (dpy, z)),
            (rc.at[s, 1, 0:2], rb.at[s, 0, 0:2], (dpx, z)),
            (rc.at[s, 2, 2:4], rb.at[s, 1, 2:4], (dpy, z)),
        )[kk]
        return remote(src, dst, s2.at[s, kk], q2.at[s, kk], who)

    def along(s, t, sign):
        way = (1 - sign) // 2
        return remote(rc.at[s, 0, t], rz.at[s, way, t], s3.at[s, way, t], q3.at[s, way, t], (dp, (z + sign + T) % T))

    def add(dst, src):
        @pl.loop(0, dst.shape[0])
        def _(t):
            dst[t] = (dst[t].astype(F32) + src[t].astype(F32)).astype(BF)

    def sum_start(s):
        for kk in (3, 1, 2, 0):
            core_copy(s, kk).start()

    def sum_core(s):
        for kk in (3, 1, 2, 0):
            core_copy(s, kk).wait_recv()
            add(rc.at[s, kk], grad(s).at[:, rowsof(rel[kk]), :])
            if kk == 3:
                turn(s, 0).start()
                turn(s, 1).start()
            if kk == 1:
                straight(s, 0).start()
            if kk == 2:
                straight(s, 1).start()

    def sum_turn(s):
        turn(s, 0).wait_recv()
        add(rc.at[s, 1, 0:2], ra.at[s, 0])
        straight(s, 2).start()
        turn(s, 1).wait_recv()
        add(rc.at[s, 2, 2:4], ra.at[s, 1])
        straight(s, 3).start()

    def sum_straight(s):
        for kk in range(4):
            straight(s, kk).wait_recv()
        add(rc.at[s, 0], rb.at[s, 0])
        add(rc.at[s, 0], rb.at[s, 1])

    def sum_along(s):
        @pl.loop(0, 2)
        def _(i):
            sign = (1 - 2 * half) * (1 - 2 * i)
            way = (1 - sign) // 2
            behind = z - sign

            @pl.loop(0, T - 1)
            def _(j):
                t = (1 - way) * (T - 1 - j) + way * j

                @pl.when((t - z) * sign > 0)
                def _():
                    @pl.when((behind >= 0) & (behind < T))
                    def _():
                        along(s, t, sign).wait_recv()
                        rc[s, 0, t] = (rc[s, 0, t].astype(F32) + rz[s, way, t].astype(F32)).astype(BF)

                    along(s, t, sign).start()

    def sum_last(s):
        GR[s] = rc[s, 0, z].astype(F32)
        for sign in (1, -1):
            @pl.when((z - sign >= 0) & (z - sign < T))
            def _():
                along(s, z, sign).wait_recv()
                GR[s] += rz[s, (1 - sign) // 2, z].astype(F32)

    def sum_sent(s):
        for sign in (1, -1):
            for t in range(T):
                pl.when((t - z) * sign > 0)(along(s, t, sign).wait_send)

    xT[:, 0:M] = low[...].T
    xT[:, M:L] = flow[...].T

    @pl.loop(0, T)
    def _(t):
        gi = (nn(low[...], W_[2, t]) * gp[t].astype(F32)).astype(BF)
        gp[t] = gi
        SM[pl.ds(2 * T + t, 1), :] += colsum(gi.astype(F32))
        gz[...] += nt(gi, W_[1, t])
        W_[2, t] = nn(xT[:, 0:M], hid[t]).astype(BF)
        W_[1, t] = nn(xT[:, M:L], gi).astype(BF)

    sum_start(2)
    sum_start(1)

    @pl.loop(0, M // RB)
    def _(r):
        rr = rows(r)
        gf = gz[rr, :]
        n = n1[rr, :]
        g = gf * NP[1:2, :]
        g1 = r1[rr, 0:1] * (g - mean_last(g) - n * mean_last(g * n))
        SM[14:15, :] += colsum(gf * n)
        SM[15:16, :] += colsum(gf)
        SM[12:13, :] += colsum(g1)
        gz[rr, :] = g1
        low[rr, :] = g1.astype(BF)

    xT[:, 0:M] = low[...].T

    @pl.loop(0, T)
    def _(t):
        hid[t, :, 0:W] = nn(low[...], W_[0, t, :, 3 * W:4 * W]).astype(BF)
        W_[0, t, :, 3 * W:4 * W] = nn(xT[:, 0:M], mixed[t, :, 0:W]).astype(BF)

    @pl.loop(0, T)
    def _(t):
        @pl.when(t == 0)
        def _():
            hand_on(CO, OF, orcv, 0, 0)
            sum_core(2)

        @pl.when(t == 1)
        def _():
            sum_core(1)

        @pl.when(t == 2)
        def _():
            sum_turn(2)

        @pl.when(t == 3)
        def _():
            sum_turn(1)
            hand_on(CO, OF, orcv, 0, 1)

        vT[...] = k[t, :, 0:W].T
        for pair in range((NH + 1) // 2):
            heads = [j for j in (2 * pair, 2 * pair + 1) if j < NH]
            wide = HD * len(heads)
            dk = jnp.zeros((L, wide), F32)
            dv = jnp.zeros((L, wide), F32)
            for j in heads:
                for i in range(M // QC):
                    qs = slice(i * QC, (i + 1) * QC)
                    qm = only(head(q, t, qs, j), j)
                    om = only(head(hid, t, qs, j), j)
                    s = nt(head(k, t, everything, j), qm) + bias[:, qs]
                    p = jnp.exp(s - lse[t * 4 + j, 0:1, qs])
                    dpr = nt(head(v, t, everything, j), om)
                    cen = jnp.sum(p * dpr, axis=0, keepdims=True)
                    ds = (p * (dpr - cen)).astype(BF)
                    dv = dv + nn(p.astype(BF), om)
                    dk = dk + nn(ds, qm)
                    oT[j * HD:(j + 1) * HD, qs] = nn(vT[j * HD:(j + 1) * HD, :], ds) * scale
            lanes = slice(pair * 128, pair * 128 + wide)
            k[t, :, lanes] = dk.astype(BF)
            v[t, :, lanes] = dv.astype(BF)
        dq = oT[...].T.astype(BF)
        q[t, :, 0:W] = dq
        SM[pl.ds(t, 1), 0:W] += colsum(dq.astype(F32))
        SM[pl.ds(T + t, 1), 0:W] += colsum(v[t, :, 0:W].astype(F32))

    @pl.loop(0, M // RB)
    def _(r):
        acc = jnp.zeros((RB, D), F32)
        for t in range(T):
            acc = acc + nt(k[t, othrows(r), 0:W], W_[0, t, :, W:2 * W])
            acc = acc + nt(v[t, othrows(r), 0:W], W_[0, t, :, 2 * W:3 * W])
        flow[rows(r), :] = acc.astype(BF)

    part = remote(flow, rgt, gs, gr, (dpc, z))
    part.start()

    @pl.loop(0, M // RB)
    def _(r):
        acc = gz[rows(r), :]
        for t in range(T):
            acc = acc + nt(q[t, rows(r), 0:W], W_[0, t, :, 0:W])
            acc = acc + nt(k[t, ownrows(r), 0:W], W_[0, t, :, W:2 * W])
            acc = acc + nt(v[t, ownrows(r), 0:W], W_[0, t, :, 2 * W:3 * W])
        gz[rows(r), :] = acc

    part.wait_recv()
    low[...] = (gz[...] + rgt[...].astype(F32)).astype(BF)
    push(low, GF, gsem, grcv, gsl)

    pals = [(dpc, z), (dpx, z), (dpy, z), (dp, z + 1 - 2 * (z % 2)), (dp, (z + 2) % T)]

    def small(step):
        return remote(ssend.at[step], srecv.at[step], ms.at[step], mr.at[step], pals[step])

    def small_start(step):
        ssend[step] = SM[...]
        small(step).start()

    def small_end(step):
        small(step).wait_recv()
        SM[...] += srecv[step]

    small_start(0)
    xT[...] = X[...].T

    @pl.loop(0, T)
    def _(t):
        W_[0, t, :, 0:W] = nn(xT[:, pl.ds(pl.multiple_of(own, 128), M)], q[t, :, 0:W]).astype(BF)
        W_[0, t, :, W:2 * W] = nn(xT[...], k[t, :, 0:W]).astype(BF)
        W_[0, t, :, 2 * W:3 * W] = nn(xT[...], v[t, :, 0:W]).astype(BF)

    sum_start(0)
    small_end(0)
    small_start(1)
    sum_straight(2)
    small_end(1)
    small_start(2)
    sum_straight(1)
    hand_on(low, GF, grcv, 4, 0)
    sum_core(0)
    small_end(2)
    small_start(3)
    sum_along(2)
    sum_turn(0)
    small_end(3)
    small_start(4)
    hand_on(low, GF, grcv, 4, 1)
    sum_along(1)
    small_end(4)
    sum_straight(0)
    sum_along(0)
    for s in (2, 1, 0):
        sum_last(s)
    SMO[...] = SM[...]
    settle(CO, OF, orcv, 0)
    settle(low, GF, grcv, 4)
    pushed(CO, OF, osem, orcv, osl)
    pushed(low, GF, gsem, grcv, gsl)
    part.wait_send()
    for step in range(5):
        small(step).wait_send()
    for s in range(SL):
        for kk in range(4):
            core_copy(s, kk).wait_send()
            straight(s, kk).wait_send()
        turn(s, 0).wait_send()
        turn(s, 1).wait_send()
        sum_sent(s)


def layer_call(weights, vectors, lengths, tokens, cotangent, T):
    wq, w1 = weights[0], weights[4]
    S, W = wq.shape
    D = tokens.shape[1]
    F = w1.shape[1]
    L = tokens.shape[0] // lengths.shape[0]
    M = L // 2
    SL = 3
    WP = 256
    any_ = pl.BlockSpec(memory_space=pl.ANY)
    vm = pl.BlockSpec(memory_space=pltpu.VMEM)
    dma = pltpu.SemaphoreType.DMA
    f32 = lambda *s: jax.ShapeDtypeStruct(s, F32)
    V = pltpu.VMEM
    return pl.pallas_call(
        layer_kernel,
        in_specs=[vm] * (len(weights) + len(vectors)) + [pl.BlockSpec(memory_space=pltpu.SMEM), any_, any_],
        out_specs=[any_, any_, vm, vm],
        out_shape=[
            jax.ShapeDtypeStruct((4 * M, D), BF),
            jax.ShapeDtypeStruct((4 * M, D), BF),
            f32(SL, S, D), f32(24, D),
        ],
        scratch_shapes=[
            V((SL, S, D), BF),
            V((SL, T, D, F), BF),
            V((L, D), BF),
            V((M, D), BF),
            V((2, 8, L), F32),
            V((8, D), F32),
            V((8, D), F32),
            V((T, 8, D), F32),
            V((24, D), F32),
            V((T, M, WP), BF),
            V((T, L, WP), BF),
            V((T, L, WP), BF),
            V((T, M, WP), BF),
            V((W, L), BF),
            V((W, M), F32),
            V((T * 4, 8, M), F32),
            V((L, M), F32),
            V((M, D), F32),
            V((M, 128), F32),
            V((M, D), BF),
            V((T, M, F), BF),
            V((T, M, F), BF),
            V((M, D), F32),
            V((M, D), BF),
            V((D, L), BF),
            V((M, D), BF),
            V((SL, 4, T, S, D), BF),
            V((SL, 2, 2, S, D), BF),
            V((SL, 2, T, S, D), BF),
            V((SL, 2, T, S, D), BF),
            V((5, 24, D), F32),
            V((5, 24, D), F32),
            dma((2,)),
            dma((SL, 2)), dma((SL, T)), dma((SL, T)),
            dma((3, SL, T)), dma((SL, T)), dma((SL, T)), dma((4, SL, T)),
            dma((SL, T)), dma((SL, T)),
            dma((3, SL, T)),
            dma((T - 1,)), dma((T - 1,)),
            dma((3,)), dma((3,)),
            dma, dma,
            dma((3,)), dma((4,)), dma,
            dma((3,)), dma((4,)), dma,
            dma((8,)),
            dma((SL, 4)), dma((SL, 4)),
            dma((SL, 2)), dma((SL, 2)),
            dma((SL, 4)), dma((SL, 4)),
            dma((SL, 2, T)), dma((SL, 2, T)),
            dma((5,)), dma((5,)),
        ],
        compiler_params=pltpu.CompilerParams(
            collective_id=0, has_side_effects=True, vmem_limit_bytes=64 << 20
        ),
    )(*weights, *vectors, lengths, tokens, cotangent)


def finish_kernel(OF, GF, GR, SMO, OUT, GT, DQ, DK, DV, DO, D1, D2, BQ, BV, B1, BO, G1, S1, B2, G2, S2, keep, gr, sm, came, went, here):
    z = lax.axis_index("tensor")
    T = lax.axis_size("tensor")
    W = DQ.shape[1]
    n = keep.shape[1]
    size = keep.shape[2]
    ins, outs = [], []
    small = [pltpu.make_async_copy(GR, gr, here.at[0]), pltpu.make_async_copy(SMO, sm, here.at[1])]
    for a, (src, dst) in enumerate(((GF, GT), (OF, OUT))):
        for i in range(n):
            part = pl.ds(i * size, size)
            ins.append(pltpu.make_async_copy(src.at[part], keep.at[a, i], came.at[a, i]))
            outs.append(pltpu.make_async_copy(keep.at[a, i], dst.at[part], went.at[a, i]))
    for copy in small + ins:
        copy.start()
    for copy in small:
        copy.wait()
    DQ[...] = gr[0, :, 0:W]
    DK[...] = gr[0, :, W:2 * W]
    DV[...] = gr[0, :, 2 * W:3 * W]
    DO[...] = gr[0, :, 3 * W:4 * W].T
    D1[...] = gr[1]
    D2[...] = gr[2]
    BQ[...] = sm[pl.ds(z, 1), 0:W].reshape(W)
    BV[...] = sm[pl.ds(T + z, 1), 0:W].reshape(W)
    B1[...] = sm[pl.ds(2 * T + z, 1), :].reshape(B1.shape[0])
    for i, ref in enumerate((BO, B2, G1, S1, G2, S2)):
        ref[...] = sm[3 * T + i:3 * T + i + 1, :].reshape(ref.shape[0])
    for a, b in zip(ins, outs):
        a.wait()
        b.start()
    for copy in outs:
        copy.wait()


def finish_call(full, grads, gr, sm, T):
    SL, S, D = gr.shape
    W = D // T
    n = 8
    any_ = pl.BlockSpec(memory_space=pltpu.HBM)
    vm = pl.BlockSpec(memory_space=pltpu.VMEM)
    f32 = lambda *s: jax.ShapeDtypeStruct(s, F32)
    same = jax.ShapeDtypeStruct(full.shape, full.dtype)
    return pl.pallas_call(
        finish_kernel,
        in_specs=[any_] * 4,
        out_specs=[any_, any_] + [vm] * 15,
        out_shape=[same, same, f32(S, W), f32(S, W), f32(S, W), f32(W, S), f32(S, D), f32(S, D),
                   f32(W), f32(W), f32(D), f32(D), f32(D), f32(D), f32(D), f32(D), f32(D)],
        scratch_shapes=[
            pltpu.VMEM((2, n, full.shape[0] // n, D), BF), pltpu.VMEM(gr.shape, F32), pltpu.VMEM(sm.shape, F32),
            pltpu.SemaphoreType.DMA((2, n)), pltpu.SemaphoreType.DMA((2, n)), pltpu.SemaphoreType.DMA((2,)),
        ],
        compiler_params=pltpu.CompilerParams(vmem_limit_bytes=64 << 20),
    )(full, grads, gr, sm)


def doc_ids(lengths, count):
    ends = jnp.cumsum(lengths)
    places = jnp.arange(count, dtype=jnp.int32)
    return jnp.sum((places[:, None] >= ends[None, :]).astype(jnp.int32), axis=1)


def collect(wq, wk, wv, wo, w1, w2):
    return (
        lax.all_gather(wq, "dp", axis=0, tiled=True),
        lax.all_gather(wk, "dp", axis=0, tiled=True),
        lax.all_gather(wv, "dp", axis=0, tiled=True),
        lax.all_gather(wo, "dp", axis=1, tiled=True),
        lax.all_gather(w1, "dp", axis=0, tiled=True),
        lax.all_gather(w2, "dp", axis=1, tiled=True),
    )


def reduce_large(grads):
    return (
        lax.psum_scatter(grads[0], "dp", scatter_dimension=0, tiled=True),
        lax.psum_scatter(grads[1], "dp", scatter_dimension=0, tiled=True),
        lax.psum_scatter(grads[2], "dp", scatter_dimension=0, tiled=True),
        lax.psum_scatter(grads[3], "dp", scatter_dimension=1, tiled=True),
        lax.psum_scatter(grads[4], "dp", scatter_dimension=0, tiled=True),
        lax.psum_scatter(grads[5], "dp", scatter_dimension=1, tiled=True),
    )


def reduce_small(grads):
    return lax.psum(
        (grads[0], grads[1], grads[2], grads[3], grads[4], grads[5], grads[6], grads[7], grads[8]),
        "dp",
    )


def contract_rows(left, right):
    return lax.dot_general(
        left, right, (((0,), (0,)), ((), ())), preferred_element_type=jnp.float32
    )


def contract_cols(left, right):
    return lax.dot_general(
        left, right, (((1,), (1,)), ((), ())), preferred_element_type=jnp.float32
    )


def contract_mixed(left, right):
    return lax.dot_general(
        left, right, (((0,), (1,)), ((), ())), preferred_element_type=jnp.float32
    )


def norm_forward(total, gain, shift):
    centre = total - jnp.mean(total, axis=-1, keepdims=True)
    scaled = lax.rsqrt(jnp.mean(centre * centre, axis=-1, keepdims=True) + EPS)
    normed = centre * scaled
    return (normed * gain + shift, normed, scaled)


def norm_backward(grad_result, normed, scaled, gain):
    grad_normed = grad_result * gain
    mean_grad = jnp.mean(grad_normed, axis=-1, keepdims=True)
    mean_cross = jnp.mean(grad_normed * normed, axis=-1, keepdims=True)
    grad_total = scaled * (grad_normed - mean_grad - normed * mean_cross)
    return (grad_total, jnp.sum(grad_result * normed, axis=0), jnp.sum(grad_result, axis=0))


def block_scores(query_block, key_heads, seg_block, seg, scale):
    raw = (
        jnp.einsum("hdq,hdk->hqk", query_block, key_heads, preferred_element_type=jnp.float32)
        * scale
    )
    same_doc = seg_block[:, None] == seg[None, :]
    return jnp.where(same_doc[None], raw, NEG)


def general_body(
    tokens,
    doc_lengths,
    wq,
    bq,
    wk,
    wv,
    bv,
    wo,
    bo,
    gain1,
    shift1,
    w1,
    b1,
    w2,
    b2,
    gain2,
    shift2,
    cotangent,
):
    micro = doc_lengths.shape[0]
    seq_len = tokens.shape[0] // micro
    block = min(512, seq_len)
    scale = HD ** (-0.5)
    results = []
    grad_inputs = []
    large_total = None
    small_total = None
    for index in range(micro):
        full = collect(wq, wk, wv, wo, w1, w2)
        full_q, full_k, full_v, full_o, full_first, full_second = full
        width = full_q.shape[1]
        heads_here = width // HD
        rows_in = tokens[index * seq_len : (index + 1) * seq_len]
        inputs = rows_in.astype(jnp.float32)
        seg = doc_ids(doc_lengths[index], seq_len)
        queries = (
            lax.dot_general(
                full_q, rows_in, (((0,), (1,)), ((), ())), preferred_element_type=jnp.float32
            )
            + bq[:, None]
        ).astype(jnp.bfloat16)
        keys_low = lax.dot_general(
            full_k, rows_in, (((0,), (1,)), ((), ())), preferred_element_type=jnp.float32
        ).astype(jnp.bfloat16)
        values_low = (
            lax.dot_general(
                full_v, rows_in, (((0,), (1,)), ((), ())), preferred_element_type=jnp.float32
            )
            + bv[:, None]
        ).astype(jnp.bfloat16)
        query_heads = queries.reshape(heads_here, HD, seq_len)
        key_heads = keys_low.reshape(heads_here, HD, seq_len)
        value_heads = values_low.reshape(heads_here, HD, seq_len)
        pieces = []
        log_totals = []
        for offset in range(0, seq_len, block):
            scores = block_scores(
                query_heads[:, :, offset : offset + block],
                key_heads,
                seg[offset : offset + block],
                seg,
                scale,
            )
            highest = jnp.max(scores, axis=-1, keepdims=True)
            log_total = highest + jnp.log(
                jnp.sum(jnp.exp(scores - highest), axis=-1, keepdims=True)
            )
            probs_low = jnp.exp(scores - log_total).astype(jnp.bfloat16)
            pieces.append(
                jnp.einsum(
                    "hqk,hdk->hdq", probs_low, value_heads, preferred_element_type=jnp.float32
                )
            )
            log_totals.append(log_total)
        mixed_cols = jnp.concatenate(pieces, axis=2).reshape(width, seq_len).astype(jnp.bfloat16)
        attended = lax.psum(
            contract_rows(mixed_cols, full_o).astype(jnp.bfloat16), "tensor"
        ).astype(jnp.float32)
        first, normed_one, scaled_one = norm_forward(inputs + attended + bo, gain1, shift1)
        first_low = first.astype(jnp.bfloat16)
        inner = jnp.dot(first_low, full_first, preferred_element_type=jnp.float32) + b1
        hidden = jax.nn.gelu(inner, approximate=False).astype(jnp.bfloat16)
        second = lax.psum(
            jnp.dot(hidden, full_second, preferred_element_type=jnp.float32).astype(jnp.bfloat16),
            "tensor",
        ).astype(jnp.float32)
        result, normed_two, scaled_two = norm_forward(first + second + b2, gain2, shift2)
        results.append(result.astype(jnp.bfloat16))
        grad_result = cotangent[index * seq_len : (index + 1) * seq_len].astype(jnp.float32)
        grad_two, grad_gain2, grad_shift2 = norm_backward(
            grad_result, normed_two, scaled_two, gain2
        )
        grad_b2 = jnp.sum(grad_two, axis=0)
        full = collect(wq, wk, wv, wo, w1, w2)
        full_q, full_k, full_v, full_o, full_first, full_second = full
        two_low = grad_two.astype(jnp.bfloat16)
        grad_w2 = contract_rows(hidden, two_low)
        grad_hidden = contract_cols(two_low, full_second)
        grad_inner = jax.vjp(partial(jax.nn.gelu, approximate=False), inner)[1](grad_hidden)[
            0
        ].astype(jnp.bfloat16)
        grad_b1 = jnp.sum(grad_inner.astype(jnp.float32), axis=0)
        grad_w1 = contract_rows(first_low, grad_inner)
        grad_first = grad_two + lax.psum(
            contract_cols(grad_inner, full_first).astype(jnp.bfloat16), "tensor"
        ).astype(jnp.float32)
        grad_one, grad_gain1, grad_shift1 = norm_backward(grad_first, normed_one, scaled_one, gain1)
        grad_bo = jnp.sum(grad_one, axis=0)
        one_low = grad_one.astype(jnp.bfloat16)
        grad_wo = jnp.dot(mixed_cols, one_low, preferred_element_type=jnp.float32)
        grad_mixed = (
            contract_cols(full_o, one_low).astype(jnp.bfloat16).reshape(heads_here, HD, seq_len)
        )
        grad_key_heads = jnp.zeros((heads_here, HD, seq_len), jnp.float32)
        grad_value_heads = jnp.zeros((heads_here, HD, seq_len), jnp.float32)
        grad_query_pieces = []
        for number, offset in enumerate(range(0, seq_len, block)):
            query_block = query_heads[:, :, offset : offset + block]
            grad_block = grad_mixed[:, :, offset : offset + block]
            scores = block_scores(query_block, key_heads, seg[offset : offset + block], seg, scale)
            probs = jnp.exp(scores - log_totals[number])
            grad_probs = jnp.einsum(
                "hdq,hdk->hqk", grad_block, value_heads, preferred_element_type=jnp.float32
            )
            centre = jnp.sum(probs * grad_probs, axis=-1, keepdims=True)
            grad_scores = (probs * (grad_probs - centre)).astype(jnp.bfloat16)
            grad_query_pieces.append(
                jnp.einsum(
                    "hqk,hdk->hdq", grad_scores, key_heads, preferred_element_type=jnp.float32
                )
                * scale
            )
            grad_key_heads = (
                grad_key_heads
                + jnp.einsum(
                    "hqk,hdq->hdk", grad_scores, query_block, preferred_element_type=jnp.float32
                )
                * scale
            )
            grad_value_heads = grad_value_heads + jnp.einsum(
                "hqk,hdq->hdk",
                probs.astype(jnp.bfloat16),
                grad_block,
                preferred_element_type=jnp.float32,
            )
        grad_queries = (
            jnp.concatenate(grad_query_pieces, axis=2).reshape(width, seq_len).astype(jnp.bfloat16)
        )
        grad_keys = grad_key_heads.reshape(width, seq_len).astype(jnp.bfloat16)
        grad_values = grad_value_heads.reshape(width, seq_len).astype(jnp.bfloat16)
        grad_bq = jnp.sum(grad_queries.astype(jnp.float32), axis=1)
        grad_bv = jnp.sum(grad_values.astype(jnp.float32), axis=1)
        grad_wq = contract_cols(rows_in.T, grad_queries)
        grad_wk = contract_cols(rows_in.T, grad_keys)
        grad_wv = contract_cols(rows_in.T, grad_values)
        back_terms = (
            contract_mixed(grad_queries, full_q)
            + contract_mixed(grad_keys, full_k)
            + contract_mixed(grad_values, full_v)
        )
        grad_rows = grad_one + lax.psum(back_terms.astype(jnp.bfloat16), "tensor").astype(
            jnp.float32
        )
        grad_inputs.append(grad_rows.astype(jnp.bfloat16))
        large_local = (grad_wq, grad_wk, grad_wv, grad_wo, grad_w1, grad_w2)
        small_local = (
            grad_bq,
            grad_bv,
            grad_b1,
            grad_bo,
            grad_b2,
            grad_gain1,
            grad_shift1,
            grad_gain2,
            grad_shift2,
        )
        large_local = reduce_large(large_local)
        small_local = reduce_small(small_local)
        if large_total is None:
            large_total = large_local
            small_total = small_local
        else:
            large_total = jax.tree.map(jnp.add, large_total, large_local)
            small_total = jax.tree.map(jnp.add, small_total, small_local)
    grad_wq, grad_wk, grad_wv, grad_wo, grad_w1, grad_w2 = large_total
    (
        grad_bq,
        grad_bv,
        grad_b1,
        grad_bo,
        grad_b2,
        grad_gain1,
        grad_shift1,
        grad_gain2,
        grad_shift2,
    ) = small_total
    return (
        jnp.concatenate(results, axis=0),
        jnp.concatenate(grad_inputs, axis=0),
        grad_wq,
        grad_bq,
        grad_wk,
        grad_wv,
        grad_bv,
        grad_wo,
        grad_bo,
        grad_gain1,
        grad_shift1,
        grad_w1,
        grad_b1,
        grad_w2,
        grad_b2,
        grad_gain2,
        grad_shift2,
    )


def split_body(T, tokens, doc_lengths, wq, bq, wk, wv, bv, wo, bo, gain1, shift1, w1, b1, w2, b2,
               gain2, shift2, cotangent):
    weights = (wq, wk, wv, wo, w1, w2.T)
    vectors = (bo, gain1, shift1, b2, gain2, shift2, b1, bq, bv)
    (full, grads, dq, dk, dv, do, d1, d2, gbq, gbv, gb1, gbo, gg1, gs1, gb2, gg2, gs2) = finish_call(
        *layer_call(weights, vectors, doc_lengths, tokens, cotangent, T), T)
    return full, grads, dq, gbq, dk, dv, gbv, do, gbo, gg1, gs1, d1, gb1, d2.T, gb2, gg2, gs2


def solution(mesh):
    placed = (
        P("dp", None),
        P("dp", None),
        P("dp", "tensor"),
        P("tensor"),
        P("dp", "tensor"),
        P("dp", "tensor"),
        P("tensor"),
        P("tensor", "dp"),
        P(),
        P(),
        P(),
        P("dp", "tensor"),
        P("tensor"),
        P("tensor", "dp"),
        P(),
        P(),
        P(),
        P("dp", None),
    )
    if mesh.shape["dp"] == 8 and mesh.shape["tensor"] == 4:
        body = partial(split_body, mesh.shape["tensor"])
    else:
        body = general_body
    return jax.shard_map(
        body,
        mesh=mesh,
        in_specs=placed,
        out_specs=(
            P("dp", None),
            P("dp", None),
            P("dp", "tensor"),
            P("tensor"),
            P("dp", "tensor"),
            P("dp", "tensor"),
            P("tensor"),
            P("tensor", "dp"),
            P(),
            P(),
            P(),
            P("dp", "tensor"),
            P("tensor"),
            P("tensor", "dp"),
            P(),
            P(),
            P(),
        ),
        check_vma=False,
    )
```

```python
from functools import partial
import jax
import jax.numpy as jnp
from jax import lax
from jax.experimental import pallas as pl
from jax.experimental.pallas import tpu as pltpu

from jax.sharding import PartitionSpec as P

BF = jnp.bfloat16
F32 = jnp.float32
EPS = 1e-12
HD = 64
NEG = -1e30
RB = 256


def nn(a, b):
    return jnp.dot(a, b, preferred_element_type=F32)


def nt(a, b):
    return lax.dot_general(a, b, (((1,), (1,)), ((), ())), preferred_element_type=F32)


def rows(r, n=RB):
    return pl.ds(pl.multiple_of(r * n, n), n)


def mean_last(x):
    return jnp.mean(x, axis=-1, keepdims=True)


def colsum(x):
    return jnp.sum(x, axis=0, keepdims=True)


MESH = pl.DeviceIdType.MESH


def remote(src, dst, send, recv, device):
    return pltpu.make_async_remote_copy(
        src_ref=src, dst_ref=dst, send_sem=send, recv_sem=recv, device_id=device, device_id_type=MESH
    )


def layer_kernel(
    WQ, WK, WV, WO, W1, W2T, BO_, GAIN1, SHIFT1, B2_, GAIN2, SHIFT2, B1_, BQ_, BV_, LEN, TOK, COT,
    OF, GF, GR, SMO,
    PK, W_, X, CO, SG, NP, BP, BI, SM,
    q, k, v, mixed, vT, oT, lse, bias, n1, r1, flow, hid, gp, gz, low, xT,
    rgt, rc, ra, rb, rz, ssend, srecv,
    loc, us, ur, zs, zf, zr, os_, xr, yr, cr, fs, dr, ks, bs, br, ts, tr,
    gs, gr, osem, orcv, osl, gsem, grcv, gsl, fwd, cs, crr, s1, q1, s2, q2, s3, q3, ms, mr,
):
    SL, S, D = PK.shape
    T = W_.shape[1]
    L = X.shape[0]
    M = L // 2
    W = D // T
    NH = W // HD
    scale = HD ** (-0.5)
    QC = RB

    dp = lax.axis_index("dp")
    z = lax.axis_index("tensor")
    core = dp % 2
    dpc = dp + 1 - 2 * core
    dpx = dp + 2 - 4 * ((dp // 2) % 2)
    dpy = dp + 4 - 8 * ((dp // 4) % 2)
    dpxy = dpx + dpy - dp
    flip = dpc - dp
    home = z // 2
    own = core * M
    oth = (1 - core) * M

    def ownrows(r):
        return pl.ds(pl.multiple_of(own + r * RB, RB), RB)

    def othrows(r):
        return pl.ds(pl.multiple_of(oth + r * RB, RB), RB)

    ownhalf = pl.ds(pl.multiple_of(own, M), M)
    othhalf = pl.ds(pl.multiple_of(oth, M), M)

    PK[0, :, 0:W] = WQ[...]
    PK[0, :, W:2 * W] = WK[...]
    PK[0, :, 2 * W:3 * W] = WV[...]
    PK[0, :, 3 * W:4 * W] = WO[...].T
    PK[1] = W1[...]
    PK[2] = W2T[...]
    for i, ref in enumerate((BO_, GAIN1, SHIFT1, B2_, GAIN2, SHIFT2)):
        NP[i:i + 1, :] = ref[...].reshape(1, D)
    BP[0:1, :] = B1_[...].reshape(1, D)
    BP[1:2, 0:W] = BQ_[...].reshape(1, W)
    BP[2:3, 0:W] = BV_[...].reshape(1, W)

    spot = lax.broadcasted_iota(jnp.int32, (8, L), 1)
    doc = jnp.zeros((8, L), F32)
    end = jnp.int32(0)
    for j in range(LEN.shape[1]):
        end = end + LEN[z % 2, j]
        doc = doc + jnp.where(spot >= end, 1.0, 0.0)
    SG[0] = doc

    barrier = pltpu.get_barrier_semaphore()
    friends = [(dp, (z + d) % T) for d in range(1, T)] + [(dpc, (z + d) % T) for d in range(T)] + [
        (dpx, z), (dpy, z)]
    for friend in friends:
        pl.semaphore_signal(barrier, inc=1, device_id=friend, device_id_type=MESH)
    pl.semaphore_wait(barrier, len(friends))

    CUT = S // 2

    def late(t, i):
        return W_.at[SL - 1, t, pl.ds(pl.multiple_of(i * S + CUT, CUT), CUT), :]

    half = z // 2

    def source(d):
        edge = z + half * (3 - 2 * z)
        swap = edge * (1 - d // 2)
        t = swap * (1 - d) + (1 - swap) * d
        return t + half * (3 - 2 * t)

    right, left = (dp, (z + 1) % T), (dp, (z + T - 1) % T)
    can_right, can_left = z < T - 1, z > 0

    def each(s, copies):
        if isinstance(s, int):
            copies(CUT if s == SL - 1 else S)
        else:
            pl.when(s < SL - 1)(lambda: copies(S))
            pl.when(s == SL - 1)(lambda: copies(CUT))

    def shard(s, n):
        return PK.at[s, 0:n, :]

    def block(s, t, i, n):
        return W_.at[s, t, pl.ds(pl.multiple_of(i * S, S), n), :]

    def send_z(s, n):
        return (
            (can_right, remote(shard(s, n), block(s, z, dp, n), zs.at[s, 0], zr.at[s, z], right)),
            (can_left, remote(shard(s, n), block(s, z, dp, n), zs.at[s, 1], zr.at[s, z], left)),
        )

    def pass_z(s, t, n):
        here = block(s, t, dp, n)
        return (
            (can_right & (t < z), remote(here, here, zf.at[s, t], zr.at[s, t], right)),
            (can_left & (t > z), remote(here, here, zf.at[s, t], zr.at[s, t], left)),
        )

    def push_z(s):
        for able, copy in send_z(s, CUT if s == SL - 1 else S):
            pl.when(able)(copy.start)

    def send_block(s, d, src, n):
        t = source(d)
        remote(src, block(s, t, dp, n), os_.at[0, s, d], xr.at[s, d], (dpx, z)).start()
        remote(src, block(s, t, dp, n), os_.at[1, s, d], yr.at[s, d], (dpy, z)).start()
        remote(src, block(s, t, dp, n), os_.at[2, s, d], cr.at[0, s, d], (dpc, z)).start()

    def pass_core(kind, s, d, i, n):
        here = block(s, source(d), i, n)
        remote(here, here, ks.at[kind - 1, s, d], cr.at[kind, s, d], (dpc, z)).start()

    def take_z(s, d, n):
        t = source(d)
        remote(shard(s, n), block(s, t, dp, n), zs.at[s, 0], zr.at[s, t], right).wait_recv()
        for able, copy in pass_z(s, t, n):
            pl.when(able)(copy.start)
        send_block(s, d, block(s, t, dp, n), n)

    def take_xy(s, d, n):
        t = source(d)
        fromx, fromy = block(s, t, dpx, n), block(s, t, dpy, n)
        remote(shard(s, n), fromx, os_.at[0, s, d], xr.at[s, d], (dpx, z)).wait_recv()

        @pl.when(d < T // 2)
        def _():
            remote(fromx, fromx, fs.at[s, d], dr.at[s, d], (dpy, z)).start()

        pass_core(1, s, d, dpx, n)
        remote(shard(s, n), fromy, os_.at[1, s, d], yr.at[s, d], (dpy, z)).wait_recv()

        @pl.when(d >= T // 2)
        def _():
            remote(fromy, fromy, fs.at[s, d], dr.at[s, d], (dpx, z)).start()

        pass_core(2, s, d, dpy, n)

    def take_diag(s, d, n):
        remote(shard(s, n), block(s, source(d), dpxy, n), fs.at[s, d], dr.at[s, d], (dpx, z)).wait_recv()
        pass_core(3, s, d, dpxy, n)

    def late_to(way, i, who):
        src = PK.at[SL - 1, CUT:S, :] if way < 2 else late(z, i)
        return remote(src, late(z, i), us.at[way], ur.at[way], who)

    chips = (dp, dpx, dpy, dpxy)

    def bundle(t, send, recv, who):
        return [remote(late(t, i), late(t, i), us.at[send], ur.at[recv], who) for i in chips]

    def whole(t, send, recv, who):
        every = W_.at[SL - 1, t, 0:4 * CUT, :]
        return remote(every, every, us.at[send], ur.at[recv], who)

    def late_core(t):
        for copy in bundle(t, 5 + T + t, 3 + T + t, (dpc, z)):
            copy.start()

    def late_start():
        late_to(0, dp, (dpx, z)).start()
        late_to(1, dp, (dpy, z)).start()

    def late_turn():
        late_to(0, dpx, (dpx, z)).wait_recv()
        late_to(2, dpx, (dpy, z)).start()

    def late_along():
        late_to(1, dpy, (dpy, z)).wait_recv()
        late_to(2, dpxy, (dpy, z)).wait_recv()
        for able, send, who in ((can_right, 3, right), (can_left, 4, left)):
            @pl.when(able)
            def _():
                for copy in bundle(z, send, 3 + z, who):
                    copy.start()
        late_core(z)

    def late_pass(t):
        whole(t, 3, 3 + t, right).wait_recv()
        for able, who in ((can_right & (t < z), right), (can_left & (t > z), left)):
            @pl.when(able)
            def _():
                for copy in bundle(t, 5 + t, 3 + t, who):
                    copy.start()
        late_core(t)

    def late_sent():
        for way, who in ((0, dpx), (1, dpy), (2, dpy)):
            late_to(way, dp, (who, z)).wait_send()
        pl.when(can_right)(whole(z, 3, 3, right).wait_send)
        pl.when(can_left)(whole(z, 4, 3, left).wait_send)
        for t in range(T):
            pl.when((can_right & (t < z)) | (can_left & (t > z)))(whole(t, 5 + t, 3, right).wait_send)
            whole(t, 5 + T + t, 3, (dpc, z)).wait_send()

    PIECES = SL * T
    XL, DL = 2, 4
    STEPS = PIECES + DL
    first_steps = DL

    def gather_step(n):
        n = jnp.int32(n)

        def piece(lag, what):
            @pl.when((n >= lag) & (n < PIECES + lag))
            def _():
                s, d = (n - lag) // T, (n - lag) % T
                each(s, lambda size: what(s, d, size))

        def arrive(s, d, size):
            pl.when(d > 0)(lambda: take_z(s, d, size))
            pl.when(d == 0)(lambda: send_block(s, d, shard(s, size), size))

        piece(0, arrive)
        for when, act in LATE:
            pl.when(n == when)(act)
        piece(XL, take_xy)
        piece(DL, take_diag)

    LATE = (
        (0, late_start), (2, late_turn), (4, late_along),
        (7, lambda: late_pass(source(1))), (9, lambda: late_pass(source(2))), (11, lambda: late_pass(source(3))),
    )

    def gathered(s, d):
        n = CUT if s == SL - 1 else S
        for kind, i in enumerate((dpc, dpx + flip, dpy + flip, dpxy + flip)):
            remote(shard(s, n), block(s, source(d), i, n), os_.at[2, s, d], cr.at[kind, s, d], (dpc, z)).wait_recv()
        if s == SL - 1:
            whole(source(d), 3, 3 + T + source(d), (dpc, z)).wait_recv()

    for s in range(SL):
        push_z(s)
    seq = pl.ds(pl.multiple_of((z % 2) * L, L), L)
    mine = pl.ds(pl.multiple_of((z % 2) * L + own, M), M)
    other = pl.ds(pl.multiple_of((z % 2) * L + oth, M), M)
    tok_out = remote(TOK.at[seq], X, ts.at[0], tr.at[0], (dpc, z))
    cot_out = remote(COT.at[other], CO, ts.at[1], tr.at[1], (dpc, z))
    doc_out = remote(SG.at[0], SG.at[1], ts.at[2], tr.at[2], (dpc, z))
    tok_in = pltpu.make_async_copy(TOK.at[seq], X, loc.at[0])
    cot_in = pltpu.make_async_copy(COT.at[mine], CO, loc.at[1])

    @pl.when(core == home)
    def _():
        for copy in (tok_out, cot_out, doc_out, tok_in, cot_in):
            copy.start()

    for d in range(1, T):
        remote(BP, BI.at[z], bs.at[d - 1], br.at[d - 1], (dp, (z + d) % T)).start()
    for s in range(SL):
        W_[s, z, pl.ds(pl.multiple_of(dp * S, S), S), :] = PK[s]
    BI[z] = BP[...]
    SM[...] = jnp.zeros_like(SM)

    @pl.loop(0, 2)
    def _(n):
        gather_step(n)

    @pl.when(core == home)
    def _():
        tok_in.wait()
        cot_in.wait()
        for copy in (tok_out, cot_out, doc_out):
            copy.wait_send()

    @pl.when(core != home)
    def _():
        for copy in (tok_out, cot_out, doc_out):
            copy.wait_recv()

    for d in range(1, T):
        remote(BP, BI.at[(z - d + T) % T], bs.at[d - 1], br.at[d - 1], (dp, (z + 1) % T)).wait_recv()

    docs = jnp.where(core == home, SG[0], SG[1])
    SG[0] = docs
    key_doc = jnp.broadcast_to(docs[0:1, :], (128, L)).T
    for i in range(M // 128):
        query_doc = SG[0, 0:1, pl.ds(pl.multiple_of(own + i * 128, 128), 128)]
        bias[:, i * 128:(i + 1) * 128] = jnp.where(key_doc == query_doc, 0.0, NEG)

    @pl.loop(2, first_steps)
    def _(n):
        gather_step(n)

    @pl.loop(0, T)
    def _(d):
        gather_step(first_steps + d)
        gathered(0, d)
        t = source(d)
        mine_qkv = nn(X[ownhalf, :], W_[0, t, :, 0:3 * W])
        q[t, :, 0:W] = ((mine_qkv[:, 0:W] + BI[t, 1:2, 0:W]).astype(BF) * BF(scale)).astype(BF)
        k[t, ownhalf, 0:W] = mine_qkv[:, W:2 * W].astype(BF)
        v[t, ownhalf, 0:W] = (mine_qkv[:, 2 * W:3 * W] + BI[t, 2:3, 0:W]).astype(BF)
        their_kv = nn(X[othhalf, :], W_[0, t, :, W:3 * W])
        k[t, othhalf, 0:W] = their_kv[:, 0:W].astype(BF)
        v[t, othhalf, 0:W] = (their_kv[:, W:2 * W] + BI[t, 2:3, 0:W]).astype(BF)

    lane = lax.broadcasted_iota(jnp.int32, (1, 128), 1)

    def head(ref, t, rr, j):
        if j % 2 == 0 and j == NH - 1:
            return ref[t, rr, j * HD:(j + 1) * HD]
        p = j // 2
        return ref[t, rr, p * 128:(p + 1) * 128]

    def only(part, j):
        if part.shape[1] == HD:
            return part
        keep = (lane < HD) if j % 2 == 0 else (lane >= HD)
        return jnp.where(keep, part, jnp.zeros_like(part))

    everything = slice(None)

    @pl.loop(0, T)
    def _(t):
        vT[...] = v[t, :, 0:W].T

        for j in range(NH):
            s = nt(head(k, t, everything, j), only(head(q, t, everything, j), j)) + bias[...]
            m = jnp.max(s, axis=0, keepdims=True)
            p = jnp.exp(s - m)
            l = jnp.sum(p, axis=0, keepdims=True)
            lse[t * 4 + j] = jnp.broadcast_to(m + jnp.log(l), (8, M))
            o = nn(vT[j * HD:(j + 1) * HD, :], p.astype(BF))
            oT[j * HD:(j + 1) * HD, :] = o * (1.0 / l)

        mixed[t, :, 0:W] = oT[...].T.astype(BF)
        gather_step(first_steps + T + t)

    @pl.loop(0, M // RB)
    def _(r):
        zz = X[ownrows(r), :].astype(F32) + NP[0:1, :]
        for t in range(T):
            zz = zz + nt(mixed[t, rows(r), 0:W], W_[0, t, :, 3 * W:4 * W])
        cen = zz - mean_last(zz)
        rs = lax.rsqrt(mean_last(cen * cen) + EPS)
        n = cen * rs
        n1[rows(r), :] = n
        r1[rows(r), :] = jnp.broadcast_to(rs, (RB, 128))
        flow[rows(r), :] = (n * NP[1:2, :] + NP[2:3, :]).astype(BF)

    @pl.loop(0, T)
    def _(d):
        gather_step(first_steps + 2 * T + d)
        gathered(1, d)
        t = source(d)
        inner = nn(flow[...], W_[1, t]) + BI[t, 0:1, :]
        phi = 0.5 * (1.0 + lax.erf(inner * (2.0 ** -0.5)))
        hid[t] = (inner * phi).astype(BF)
        gp[t] = (phi + inner * (jnp.exp(-0.5 * inner * inner) * 0.3989422804014327)).astype(BF)

    gz[...] = n1[...] * NP[1:2, :] + NP[2:3, :] + NP[3:4, :]

    @pl.loop(0, T)
    def _(d):
        gathered(2, d)
        t = source(d)
        gz[...] += nt(hid[t], W_[2, t])

    @pl.loop(0, M // RB)
    def _(r):
        rr = rows(r)
        zz = gz[rr, :]
        cen = zz - mean_last(zz)
        rs = lax.rsqrt(mean_last(cen * cen) + EPS)
        n = cen * rs
        ct = CO[rr, :].astype(F32)
        CO[rr, :] = (n * NP[4:5, :] + NP[5:6, :]).astype(BF)
        g = ct * NP[4:5, :]
        g2 = rs * (g - mean_last(g) - n * mean_last(g * n))
        SM[16:17, :] += colsum(ct * n)
        SM[17:18, :] += colsum(ct)
        SM[13:14, :] += colsum(g2)
        gz[rr, :] = g2
        low[rr, :] = g2.astype(BF)

    dest = dp - core + home

    PARTS = 2
    PR = M // PARTS

    def spotrows(b, cc, part):
        return pl.ds(pl.multiple_of(((b % 2) * 2 + cc) * M + part * PR, PR), PR)

    def spotsem(b, cc, part):
        return ((b % 2) * 2 + cc) * PARTS + part

    def pushes(src, full, sems, recv):
        return [
            (able, remote(src.at[pl.ds(part * PR, PR)], full.at[spotrows(z, core, part)],
                          sems.at[i * PARTS + part], recv.at[spotsem(z, core, part)], chip))
            for part in range(PARTS)
            for i, (able, chip) in enumerate((
                (can_right, (dest, (z + 1) % T)), (can_left, (dest, (z + T - 1) % T)), (core != home, (dpc, z))))
        ]

    def here(src, full, slot):
        rows_ = pl.ds(pl.multiple_of(((z % 2) * 2 + core) * M, M), M)
        return pltpu.make_async_copy(src, full.at[rows_], slot)

    def push(src, full, sems, recv, slot):
        for able, copy in pushes(src, full, sems, recv):
            pl.when(able)(copy.start)
        pl.when(core == home)(here(src, full, slot).start)

    def pushed(src, full, sems, recv, slot):
        for able, copy in pushes(src, full, sems, recv):
            pl.when(able)(copy.wait_send)
        pl.when(core == home)(here(src, full, slot).wait)

    ahead = 1 - 2 * core

    def moves(hop):
        if hop == 0:
            return (z == 1) | (z == 2)
        return z == 2 - core

    def got(src, full, recv, b, cc, part):
        remote(src.at[0:PR], full.at[spotrows(b, cc, part)], gs, recv.at[spotsem(b, cc, part)], (dpx, z)).wait_recv()

    def handing(full, recv, base, hop, cc, part):
        b = z - ahead * (hop + 1)
        spot_ = full.at[spotrows(b, cc, part)]
        return remote(spot_, spot_, fwd.at[base + (2 * hop + cc) * PARTS + part],
                      recv.at[spotsem(b, cc, part)], (dp, (z + ahead) % T))

    def hand_on(src, full, recv, base, hop, part):
        @pl.when(moves(hop))
        def _():
            for cc in range(2):
                got(src, full, recv, z - ahead * (hop + 1), cc, part)
                handing(full, recv, base, hop, cc, part).start()

    def settle(src, full, recv, base):
        for kk in range(2):
            for cc in range(2):
                b = core * 2 + kk
                gone = (moves(0) & (b == z - ahead)) | (moves(1) & (b == z - 2 * ahead))

                @pl.when(jnp.logical_not((b == z) & (core == cc)) & jnp.logical_not(gone))
                def _():
                    for part in range(PARTS):
                        got(src, full, recv, b, cc, part)

        for hop in range(2):
            @pl.when(moves(hop))
            def _():
                for cc in range(2):
                    for part in range(PARTS):
                        handing(full, recv, base, hop, cc, part).wait_send()

    push(CO, OF, osem, orcv, osl)

    for s in range(SL):
        n = CUT if s == SL - 1 else S
        for able, copy in send_z(s, n):
            pl.when(able)(copy.wait_send)
        for t in range(T):
            for able, copy in pass_z(s, t, n):
                pl.when(able)(copy.wait_send)
        for d in range(T):
            for kind in range(3):
                remote(shard(s, n), block(s, z, dp, n), os_.at[kind, s, d], xr.at[s, d], (dpx, z)).wait_send()
                remote(shard(s, n), block(s, z, dp, n), ks.at[kind, s, d], xr.at[s, d], (dpx, z)).wait_send()
            remote(shard(s, n), block(s, z, dp, n), fs.at[s, d], xr.at[s, d], (dpx, z)).wait_send()
    late_sent()
    for d in range(1, T):
        remote(BP, BI.at[z], bs.at[d - 1], br.at[d - 1], (dp, (z + d) % T)).wait_send()

    def grad(s):
        return W_.at[s]

    rel = (dp, dpx, dpy, dpxy)

    def rowsof(i):
        return pl.ds(pl.multiple_of(i * S, S), S)

    def core_copy(s, kk):
        return remote(grad(s).at[:, rowsof(rel[kk] + flip), :], rc.at[s, kk], cs.at[s, kk], crr.at[s, kk], (dpc, z))

    def turn(s, kk):
        src, dst, who = (
            (rc.at[s, 3, 0:2], ra.at[s, 0], (dpy, z)),
            (rc.at[s, 3, 2:4], ra.at[s, 1], (dpx, z)),
        )[kk]
        return remote(src, dst, s1.at[s, kk], q1.at[s, kk], who)

    def straight(s, kk):
        src, dst, who = (
            (rc.at[s, 1, 2:4], rb.at[s, 0, 2:4], (dpx, z)),
            (rc.at[s, 2, 0:2], rb.at[s, 1, 0:2], (dpy, z)),
            (rc.at[s, 1, 0:2], rb.at[s, 0, 0:2], (dpx, z)),
            (rc.at[s, 2, 2:4], rb.at[s, 1, 2:4], (dpy, z)),
        )[kk]
        return remote(src, dst, s2.at[s, kk], q2.at[s, kk], who)

    def along(s, t, sign):
        way = (1 - sign) // 2
        return remote(rc.at[s, 0, t], rz.at[s, way, t], s3.at[s, way, t], q3.at[s, way, t], (dp, (z + sign + T) % T))

    def add(dst, src):
        @pl.loop(0, dst.shape[0])
        def _(t):
            dst[t] = (dst[t].astype(F32) + src[t].astype(F32)).astype(BF)

    def sum_start(s):
        for kk in (3, 1, 2, 0):
            core_copy(s, kk).start()

    def sum_core(s):
        for kk in (3, 1, 2, 0):
            core_copy(s, kk).wait_recv()
            add(rc.at[s, kk], grad(s).at[:, rowsof(rel[kk]), :])
            if kk == 3:
                turn(s, 0).start()
                turn(s, 1).start()
            if kk == 1:
                straight(s, 0).start()
            if kk == 2:
                straight(s, 1).start()

    def sum_turn(s):
        turn(s, 0).wait_recv()
        add(rc.at[s, 1, 0:2], ra.at[s, 0])
        straight(s, 2).start()
        turn(s, 1).wait_recv()
        add(rc.at[s, 2, 2:4], ra.at[s, 1])
        straight(s, 3).start()

    def sum_straight(s):
        for kk in range(4):
            straight(s, kk).wait_recv()
        add(rc.at[s, 0], rb.at[s, 0])
        add(rc.at[s, 0], rb.at[s, 1])

    def sum_along(s):
        @pl.loop(0, 2)
        def _(i):
            sign = (1 - 2 * half) * (1 - 2 * i)
            way = (1 - sign) // 2
            behind = z - sign

            @pl.loop(0, T - 1)
            def _(j):
                t = (1 - way) * (T - 1 - j) + way * j

                @pl.when((t - z) * sign > 0)
                def _():
                    @pl.when((behind >= 0) & (behind < T))
                    def _():
                        along(s, t, sign).wait_recv()
                        rc[s, 0, t] = (rc[s, 0, t].astype(F32) + rz[s, way, t].astype(F32)).astype(BF)

                    along(s, t, sign).start()

    def sum_last(s):
        GR[s] = rc[s, 0, z].astype(F32)
        for sign in (1, -1):
            @pl.when((z - sign >= 0) & (z - sign < T))
            def _():
                along(s, z, sign).wait_recv()
                GR[s] += rz[s, (1 - sign) // 2, z].astype(F32)

    def sum_sent(s):
        for sign in (1, -1):
            for t in range(T):
                pl.when((t - z) * sign > 0)(along(s, t, sign).wait_send)

    xT[:, 0:M] = low[...].T
    xT[:, M:L] = flow[...].T

    @pl.loop(0, T)
    def _(t):
        gi = (nn(low[...], W_[2, t]) * gp[t].astype(F32)).astype(BF)
        gp[t] = gi
        SM[pl.ds(2 * T + t, 1), :] += colsum(gi.astype(F32))
        gz[...] += nt(gi, W_[1, t])
        W_[2, t] = nn(xT[:, 0:M], hid[t]).astype(BF)
        W_[1, t] = nn(xT[:, M:L], gi).astype(BF)

    hand_on(CO, OF, orcv, 0, 0, 0)
    sum_start(2)
    sum_start(1)

    @pl.loop(0, M // RB)
    def _(r):
        rr = rows(r)
        gf = gz[rr, :]
        n = n1[rr, :]
        g = gf * NP[1:2, :]
        g1 = r1[rr, 0:1] * (g - mean_last(g) - n * mean_last(g * n))
        SM[14:15, :] += colsum(gf * n)
        SM[15:16, :] += colsum(gf)
        SM[12:13, :] += colsum(g1)
        gz[rr, :] = g1
        low[rr, :] = g1.astype(BF)

    xT[:, 0:M] = low[...].T

    @pl.loop(0, T)
    def _(t):
        hid[t, :, 0:W] = nn(low[...], W_[0, t, :, 3 * W:4 * W]).astype(BF)

    @pl.loop(0, T)
    def _(t):
        @pl.when(t == 0)
        def _():
            hand_on(CO, OF, orcv, 0, 0, 1)
            sum_core(2)

        @pl.when(t == 1)
        def _():
            sum_core(1)

        @pl.when(t == 2)
        def _():
            sum_turn(2)
            hand_on(CO, OF, orcv, 0, 1, 0)

        @pl.when(t == 3)
        def _():
            sum_turn(1)
            hand_on(CO, OF, orcv, 0, 1, 1)

        vT[...] = k[t, :, 0:W].T
        for pair in range((NH + 1) // 2):
            heads = [j for j in (2 * pair, 2 * pair + 1) if j < NH]
            wide = HD * len(heads)
            dk = jnp.zeros((L, wide), F32)
            dv = jnp.zeros((L, wide), F32)
            for j in heads:
                for i in range(M // QC):
                    qs = slice(i * QC, (i + 1) * QC)
                    qm = only(head(q, t, qs, j), j)
                    om = only(head(hid, t, qs, j), j)
                    s = nt(head(k, t, everything, j), qm) + bias[:, qs]
                    p = jnp.exp(s - lse[t * 4 + j, 0:1, qs])
                    dpr = nt(head(v, t, everything, j), om)
                    cen = jnp.sum(p * dpr, axis=0, keepdims=True)
                    ds = (p * (dpr - cen)).astype(BF)
                    dv = dv + nn(p.astype(BF), om)
                    dk = dk + nn(ds, qm)
                    oT[j * HD:(j + 1) * HD, qs] = nn(vT[j * HD:(j + 1) * HD, :], ds) * scale
            lanes = slice(pair * 128, pair * 128 + wide)
            k[t, :, lanes] = dk.astype(BF)
            v[t, :, lanes] = dv.astype(BF)
        dq = oT[...].T.astype(BF)
        q[t, :, 0:W] = dq
        SM[pl.ds(t, 1), 0:W] += colsum(dq.astype(F32))
        SM[pl.ds(T + t, 1), 0:W] += colsum(v[t, :, 0:W].astype(F32))

    @pl.loop(0, M // RB)
    def _(r):
        acc = jnp.zeros((RB, D), F32)
        for t in range(T):
            acc = acc + nt(k[t, othrows(r), 0:W], W_[0, t, :, W:2 * W])
            acc = acc + nt(v[t, othrows(r), 0:W], W_[0, t, :, 2 * W:3 * W])
        flow[rows(r), :] = acc.astype(BF)

    part = remote(flow, rgt, gs, gr, (dpc, z))
    part.start()

    @pl.loop(0, M // RB)
    def _(r):
        acc = gz[rows(r), :]
        for t in range(T):
            acc = acc + nt(q[t, rows(r), 0:W], W_[0, t, :, 0:W])
            acc = acc + nt(k[t, ownrows(r), 0:W], W_[0, t, :, W:2 * W])
            acc = acc + nt(v[t, ownrows(r), 0:W], W_[0, t, :, 2 * W:3 * W])
        gz[rows(r), :] = acc

    part.wait_recv()
    low[...] = (gz[...] + rgt[...].astype(F32)).astype(BF)
    push(low, GF, gsem, grcv, gsl)

    pals = [(dpc, z), (dpx, z), (dpy, z), (dp, z + 1 - 2 * (z % 2)), (dp, (z + 2) % T)]

    def small(step):
        return remote(ssend.at[step], srecv.at[step], ms.at[step], mr.at[step], pals[step])

    def small_start(step):
        ssend[step] = SM[...]
        small(step).start()

    def small_end(step):
        small(step).wait_recv()
        SM[...] += srecv[step]

    small_start(0)

    @pl.loop(0, T)
    def _(t):
        W_[0, t, :, 3 * W:4 * W] = nn(xT[:, 0:M], mixed[t, :, 0:W]).astype(BF)

    xT[...] = X[...].T

    @pl.loop(0, T)
    def _(t):
        W_[0, t, :, 0:W] = nn(xT[:, pl.ds(pl.multiple_of(own, 128), M)], q[t, :, 0:W]).astype(BF)
        W_[0, t, :, W:2 * W] = nn(xT[...], k[t, :, 0:W]).astype(BF)
        W_[0, t, :, 2 * W:3 * W] = nn(xT[...], v[t, :, 0:W]).astype(BF)

    sum_start(0)
    hand_on(low, GF, grcv, 8, 0, 0)
    small_end(0)
    small_start(1)
    sum_core(0)
    hand_on(low, GF, grcv, 8, 0, 1)
    small_end(1)
    small_start(2)
    sum_straight(2)
    sum_turn(0)
    hand_on(low, GF, grcv, 8, 1, 0)
    sum_along(2)
    small_end(2)
    small_start(3)
    sum_straight(1)
    hand_on(low, GF, grcv, 8, 1, 1)
    sum_along(1)
    small_end(3)
    small_start(4)
    sum_straight(0)
    sum_along(0)
    small_end(4)
    for s in (2, 1, 0):
        sum_last(s)
    SMO[...] = SM[...]
    settle(CO, OF, orcv, 0)
    settle(low, GF, grcv, 8)
    pushed(CO, OF, osem, orcv, osl)
    pushed(low, GF, gsem, grcv, gsl)
    part.wait_send()
    for step in range(5):
        small(step).wait_send()
    for s in range(SL):
        for kk in range(4):
            core_copy(s, kk).wait_send()
            straight(s, kk).wait_send()
        turn(s, 0).wait_send()
        turn(s, 1).wait_send()
        sum_sent(s)


def layer_call(weights, vectors, lengths, tokens, cotangent, T):
    wq, w1 = weights[0], weights[4]
    S, W = wq.shape
    D = tokens.shape[1]
    F = w1.shape[1]
    L = tokens.shape[0] // lengths.shape[0]
    M = L // 2
    SL = 3
    WP = 256
    any_ = pl.BlockSpec(memory_space=pl.ANY)
    vm = pl.BlockSpec(memory_space=pltpu.VMEM)
    dma = pltpu.SemaphoreType.DMA
    f32 = lambda *s: jax.ShapeDtypeStruct(s, F32)
    V = pltpu.VMEM
    return pl.pallas_call(
        layer_kernel,
        in_specs=[vm] * (len(weights) + len(vectors)) + [pl.BlockSpec(memory_space=pltpu.SMEM), any_, any_],
        out_specs=[any_, any_, vm, vm],
        out_shape=[
            jax.ShapeDtypeStruct((4 * M, D), BF),
            jax.ShapeDtypeStruct((4 * M, D), BF),
            f32(SL, S, D), f32(24, D),
        ],
        scratch_shapes=[
            V((SL, S, D), BF),
            V((SL, T, D, F), BF),
            V((L, D), BF),
            V((M, D), BF),
            V((2, 8, L), F32),
            V((8, D), F32),
            V((8, D), F32),
            V((T, 8, D), F32),
            V((24, D), F32),
            V((T, M, WP), BF),
            V((T, L, WP), BF),
            V((T, L, WP), BF),
            V((T, M, WP), BF),
            V((W, L), BF),
            V((W, M), F32),
            V((T * 4, 8, M), F32),
            V((L, M), F32),
            V((M, D), F32),
            V((M, 128), F32),
            V((M, D), BF),
            V((T, M, F), BF),
            V((T, M, F), BF),
            V((M, D), F32),
            V((M, D), BF),
            V((D, L), BF),
            V((M, D), BF),
            V((SL, 4, T, S, D), BF),
            V((SL, 2, 2, S, D), BF),
            V((SL, 2, T, S, D), BF),
            V((SL, 2, T, S, D), BF),
            V((5, 24, D), F32),
            V((5, 24, D), F32),
            dma((2,)),
            dma((5 + 2 * T,)), dma((3 + 2 * T,)),
            dma((SL, 2)), dma((SL, T)), dma((SL, T)),
            dma((3, SL, T)), dma((SL, T)), dma((SL, T)), dma((4, SL, T)),
            dma((SL, T)), dma((SL, T)),
            dma((3, SL, T)),
            dma((T - 1,)), dma((T - 1,)),
            dma((3,)), dma((3,)),
            dma, dma,
            dma((6,)), dma((8,)), dma,
            dma((6,)), dma((8,)), dma,
            dma((16,)),
            dma((SL, 4)), dma((SL, 4)),
            dma((SL, 2)), dma((SL, 2)),
            dma((SL, 4)), dma((SL, 4)),
            dma((SL, 2, T)), dma((SL, 2, T)),
            dma((5,)), dma((5,)),
        ],
        compiler_params=pltpu.CompilerParams(
            collective_id=0, has_side_effects=True, vmem_limit_bytes=64 << 20
        ),
    )(*weights, *vectors, lengths, tokens, cotangent)


def finish_kernel(OF, GF, GR, SMO, OUT, GT, *rest):
    outs, (keep, gr, sm, *bufs, came, went, read, wrote) = rest[:15], rest[15:]
    z = lax.axis_index("tensor")
    T = lax.axis_size("tensor")
    W = bufs[0].shape[1]
    small = [pltpu.make_async_copy(GR, gr, read.at[0]), pltpu.make_async_copy(SMO, sm, read.at[1])]
    n, size = keep.shape[1:3]
    ins, backs = [], []
    for a, (src, dst) in enumerate(((GF, GT), (OF, OUT))):
        for i in range(n):
            part = pl.ds(i * size, size)
            ins.append(pltpu.make_async_copy(src.at[part], keep.at[a, i], came.at[a, i]))
            backs.append(pltpu.make_async_copy(keep.at[a, i], dst.at[part], went.at[a, i]))
    for copy in small + ins:
        copy.start()
    for copy in small:
        copy.wait()
    dq, dk, dv, do, bq, bv, b1 = bufs[:7]
    dq[...] = gr[0, :, 0:W]
    dk[...] = gr[0, :, W:2 * W]
    dv[...] = gr[0, :, 2 * W:3 * W]
    do[...] = gr[0, :, 3 * W:4 * W].T
    bq[...] = sm[pl.ds(z, 1), 0:W].reshape(W)
    bv[...] = sm[pl.ds(T + z, 1), 0:W].reshape(W)
    b1[...] = sm[pl.ds(2 * T + z, 1), :].reshape(b1.shape[0])
    for i, ref in zip((0, 2, 3, 1, 4, 5), bufs[7:]):
        ref[...] = sm[3 * T + i:3 * T + i + 1, :].reshape(ref.shape[0])
    sources = [dq, dk, dv, do, gr.at[1], gr.at[2], *bufs[4:]]
    writes = [pltpu.make_async_copy(src, dst, wrote.at[i]) for i, (src, dst) in enumerate(zip(sources, outs))]
    for copy in writes:
        copy.start()
    for a, b in zip(ins, backs):
        a.wait()
        b.start()
    for copy in backs + writes:
        copy.wait()


def finish_call(full, grads, gr, sm, T):
    SL, S, D = gr.shape
    W = D // T
    n = 4
    any_ = pl.BlockSpec(memory_space=pltpu.HBM)
    f32 = lambda *s: jax.ShapeDtypeStruct(s, F32)
    same = jax.ShapeDtypeStruct(full.shape, full.dtype)
    made = [(S, W), (S, W), (S, W), (W, S), (W,), (W,), (D,), (D,), (D,), (D,), (D,), (D,), (D,)]
    dma = pltpu.SemaphoreType.DMA
    return pl.pallas_call(
        finish_kernel,
        in_specs=[any_] * 4,
        out_specs=[any_] * 17,
        out_shape=[same, same] + [f32(*m) for m in made[:4]] + [f32(S, D), f32(S, D)] + [f32(*m) for m in made[4:]],
        scratch_shapes=[
            pltpu.VMEM((2, n, full.shape[0] // n, D), BF), pltpu.VMEM(gr.shape, F32), pltpu.VMEM(sm.shape, F32),
            *[pltpu.VMEM(m, F32) for m in made],
            dma((2, n)), dma((2, n)), dma((2,)), dma((15,)),
        ],
        compiler_params=pltpu.CompilerParams(vmem_limit_bytes=64 << 20),
    )(full, grads, gr, sm)


def doc_ids(lengths, count):
    ends = jnp.cumsum(lengths)
    places = jnp.arange(count, dtype=jnp.int32)
    return jnp.sum((places[:, None] >= ends[None, :]).astype(jnp.int32), axis=1)


def collect(wq, wk, wv, wo, w1, w2):
    return (
        lax.all_gather(wq, "dp", axis=0, tiled=True),
        lax.all_gather(wk, "dp", axis=0, tiled=True),
        lax.all_gather(wv, "dp", axis=0, tiled=True),
        lax.all_gather(wo, "dp", axis=1, tiled=True),
        lax.all_gather(w1, "dp", axis=0, tiled=True),
        lax.all_gather(w2, "dp", axis=1, tiled=True),
    )


def reduce_large(grads):
    return (
        lax.psum_scatter(grads[0], "dp", scatter_dimension=0, tiled=True),
        lax.psum_scatter(grads[1], "dp", scatter_dimension=0, tiled=True),
        lax.psum_scatter(grads[2], "dp", scatter_dimension=0, tiled=True),
        lax.psum_scatter(grads[3], "dp", scatter_dimension=1, tiled=True),
        lax.psum_scatter(grads[4], "dp", scatter_dimension=0, tiled=True),
        lax.psum_scatter(grads[5], "dp", scatter_dimension=1, tiled=True),
    )


def reduce_small(grads):
    return lax.psum(
        (grads[0], grads[1], grads[2], grads[3], grads[4], grads[5], grads[6], grads[7], grads[8]),
        "dp",
    )


def contract_rows(left, right):
    return lax.dot_general(
        left, right, (((0,), (0,)), ((), ())), preferred_element_type=jnp.float32
    )


def contract_cols(left, right):
    return lax.dot_general(
        left, right, (((1,), (1,)), ((), ())), preferred_element_type=jnp.float32
    )


def contract_mixed(left, right):
    return lax.dot_general(
        left, right, (((0,), (1,)), ((), ())), preferred_element_type=jnp.float32
    )


def norm_forward(total, gain, shift):
    centre = total - jnp.mean(total, axis=-1, keepdims=True)
    scaled = lax.rsqrt(jnp.mean(centre * centre, axis=-1, keepdims=True) + EPS)
    normed = centre * scaled
    return (normed * gain + shift, normed, scaled)


def norm_backward(grad_result, normed, scaled, gain):
    grad_normed = grad_result * gain
    mean_grad = jnp.mean(grad_normed, axis=-1, keepdims=True)
    mean_cross = jnp.mean(grad_normed * normed, axis=-1, keepdims=True)
    grad_total = scaled * (grad_normed - mean_grad - normed * mean_cross)
    return (grad_total, jnp.sum(grad_result * normed, axis=0), jnp.sum(grad_result, axis=0))


def block_scores(query_block, key_heads, seg_block, seg, scale):
    raw = (
        jnp.einsum("hdq,hdk->hqk", query_block, key_heads, preferred_element_type=jnp.float32)
        * scale
    )
    same_doc = seg_block[:, None] == seg[None, :]
    return jnp.where(same_doc[None], raw, NEG)


def general_body(
    tokens,
    doc_lengths,
    wq,
    bq,
    wk,
    wv,
    bv,
    wo,
    bo,
    gain1,
    shift1,
    w1,
    b1,
    w2,
    b2,
    gain2,
    shift2,
    cotangent,
):
    micro = doc_lengths.shape[0]
    seq_len = tokens.shape[0] // micro
    block = min(512, seq_len)
    scale = HD ** (-0.5)
    results = []
    grad_inputs = []
    large_total = None
    small_total = None
    for index in range(micro):
        full = collect(wq, wk, wv, wo, w1, w2)
        full_q, full_k, full_v, full_o, full_first, full_second = full
        width = full_q.shape[1]
        heads_here = width // HD
        rows_in = tokens[index * seq_len : (index + 1) * seq_len]
        inputs = rows_in.astype(jnp.float32)
        seg = doc_ids(doc_lengths[index], seq_len)
        queries = (
            lax.dot_general(
                full_q, rows_in, (((0,), (1,)), ((), ())), preferred_element_type=jnp.float32
            )
            + bq[:, None]
        ).astype(jnp.bfloat16)
        keys_low = lax.dot_general(
            full_k, rows_in, (((0,), (1,)), ((), ())), preferred_element_type=jnp.float32
        ).astype(jnp.bfloat16)
        values_low = (
            lax.dot_general(
                full_v, rows_in, (((0,), (1,)), ((), ())), preferred_element_type=jnp.float32
            )
            + bv[:, None]
        ).astype(jnp.bfloat16)
        query_heads = queries.reshape(heads_here, HD, seq_len)
        key_heads = keys_low.reshape(heads_here, HD, seq_len)
        value_heads = values_low.reshape(heads_here, HD, seq_len)
        pieces = []
        log_totals = []
        for offset in range(0, seq_len, block):
            scores = block_scores(
                query_heads[:, :, offset : offset + block],
                key_heads,
                seg[offset : offset + block],
                seg,
                scale,
            )
            highest = jnp.max(scores, axis=-1, keepdims=True)
            log_total = highest + jnp.log(
                jnp.sum(jnp.exp(scores - highest), axis=-1, keepdims=True)
            )
            probs_low = jnp.exp(scores - log_total).astype(jnp.bfloat16)
            pieces.append(
                jnp.einsum(
                    "hqk,hdk->hdq", probs_low, value_heads, preferred_element_type=jnp.float32
                )
            )
            log_totals.append(log_total)
        mixed_cols = jnp.concatenate(pieces, axis=2).reshape(width, seq_len).astype(jnp.bfloat16)
        attended = lax.psum(
            contract_rows(mixed_cols, full_o).astype(jnp.bfloat16), "tensor"
        ).astype(jnp.float32)
        first, normed_one, scaled_one = norm_forward(inputs + attended + bo, gain1, shift1)
        first_low = first.astype(jnp.bfloat16)
        inner = jnp.dot(first_low, full_first, preferred_element_type=jnp.float32) + b1
        hidden = jax.nn.gelu(inner, approximate=False).astype(jnp.bfloat16)
        second = lax.psum(
            jnp.dot(hidden, full_second, preferred_element_type=jnp.float32).astype(jnp.bfloat16),
            "tensor",
        ).astype(jnp.float32)
        result, normed_two, scaled_two = norm_forward(first + second + b2, gain2, shift2)
        results.append(result.astype(jnp.bfloat16))
        grad_result = cotangent[index * seq_len : (index + 1) * seq_len].astype(jnp.float32)
        grad_two, grad_gain2, grad_shift2 = norm_backward(
            grad_result, normed_two, scaled_two, gain2
        )
        grad_b2 = jnp.sum(grad_two, axis=0)
        full = collect(wq, wk, wv, wo, w1, w2)
        full_q, full_k, full_v, full_o, full_first, full_second = full
        two_low = grad_two.astype(jnp.bfloat16)
        grad_w2 = contract_rows(hidden, two_low)
        grad_hidden = contract_cols(two_low, full_second)
        grad_inner = jax.vjp(partial(jax.nn.gelu, approximate=False), inner)[1](grad_hidden)[
            0
        ].astype(jnp.bfloat16)
        grad_b1 = jnp.sum(grad_inner.astype(jnp.float32), axis=0)
        grad_w1 = contract_rows(first_low, grad_inner)
        grad_first = grad_two + lax.psum(
            contract_cols(grad_inner, full_first).astype(jnp.bfloat16), "tensor"
        ).astype(jnp.float32)
        grad_one, grad_gain1, grad_shift1 = norm_backward(grad_first, normed_one, scaled_one, gain1)
        grad_bo = jnp.sum(grad_one, axis=0)
        one_low = grad_one.astype(jnp.bfloat16)
        grad_wo = jnp.dot(mixed_cols, one_low, preferred_element_type=jnp.float32)
        grad_mixed = (
            contract_cols(full_o, one_low).astype(jnp.bfloat16).reshape(heads_here, HD, seq_len)
        )
        grad_key_heads = jnp.zeros((heads_here, HD, seq_len), jnp.float32)
        grad_value_heads = jnp.zeros((heads_here, HD, seq_len), jnp.float32)
        grad_query_pieces = []
        for number, offset in enumerate(range(0, seq_len, block)):
            query_block = query_heads[:, :, offset : offset + block]
            grad_block = grad_mixed[:, :, offset : offset + block]
            scores = block_scores(query_block, key_heads, seg[offset : offset + block], seg, scale)
            probs = jnp.exp(scores - log_totals[number])
            grad_probs = jnp.einsum(
                "hdq,hdk->hqk", grad_block, value_heads, preferred_element_type=jnp.float32
            )
            centre = jnp.sum(probs * grad_probs, axis=-1, keepdims=True)
            grad_scores = (probs * (grad_probs - centre)).astype(jnp.bfloat16)
            grad_query_pieces.append(
                jnp.einsum(
                    "hqk,hdk->hdq", grad_scores, key_heads, preferred_element_type=jnp.float32
                )
                * scale
            )
            grad_key_heads = (
                grad_key_heads
                + jnp.einsum(
                    "hqk,hdq->hdk", grad_scores, query_block, preferred_element_type=jnp.float32
                )
                * scale
            )
            grad_value_heads = grad_value_heads + jnp.einsum(
                "hqk,hdq->hdk",
                probs.astype(jnp.bfloat16),
                grad_block,
                preferred_element_type=jnp.float32,
            )
        grad_queries = (
            jnp.concatenate(grad_query_pieces, axis=2).reshape(width, seq_len).astype(jnp.bfloat16)
        )
        grad_keys = grad_key_heads.reshape(width, seq_len).astype(jnp.bfloat16)
        grad_values = grad_value_heads.reshape(width, seq_len).astype(jnp.bfloat16)
        grad_bq = jnp.sum(grad_queries.astype(jnp.float32), axis=1)
        grad_bv = jnp.sum(grad_values.astype(jnp.float32), axis=1)
        grad_wq = contract_cols(rows_in.T, grad_queries)
        grad_wk = contract_cols(rows_in.T, grad_keys)
        grad_wv = contract_cols(rows_in.T, grad_values)
        back_terms = (
            contract_mixed(grad_queries, full_q)
            + contract_mixed(grad_keys, full_k)
            + contract_mixed(grad_values, full_v)
        )
        grad_rows = grad_one + lax.psum(back_terms.astype(jnp.bfloat16), "tensor").astype(
            jnp.float32
        )
        grad_inputs.append(grad_rows.astype(jnp.bfloat16))
        large_local = (grad_wq, grad_wk, grad_wv, grad_wo, grad_w1, grad_w2)
        small_local = (
            grad_bq,
            grad_bv,
            grad_b1,
            grad_bo,
            grad_b2,
            grad_gain1,
            grad_shift1,
            grad_gain2,
            grad_shift2,
        )
        large_local = reduce_large(large_local)
        small_local = reduce_small(small_local)
        if large_total is None:
            large_total = large_local
            small_total = small_local
        else:
            large_total = jax.tree.map(jnp.add, large_total, large_local)
            small_total = jax.tree.map(jnp.add, small_total, small_local)
    grad_wq, grad_wk, grad_wv, grad_wo, grad_w1, grad_w2 = large_total
    (
        grad_bq,
        grad_bv,
        grad_b1,
        grad_bo,
        grad_b2,
        grad_gain1,
        grad_shift1,
        grad_gain2,
        grad_shift2,
    ) = small_total
    return (
        jnp.concatenate(results, axis=0),
        jnp.concatenate(grad_inputs, axis=0),
        grad_wq,
        grad_bq,
        grad_wk,
        grad_wv,
        grad_bv,
        grad_wo,
        grad_bo,
        grad_gain1,
        grad_shift1,
        grad_w1,
        grad_b1,
        grad_w2,
        grad_b2,
        grad_gain2,
        grad_shift2,
    )


def split_body(T, tokens, doc_lengths, wq, bq, wk, wv, bv, wo, bo, gain1, shift1, w1, b1, w2, b2,
               gain2, shift2, cotangent):
    weights = (wq, wk, wv, wo, w1, w2.T)
    vectors = (bo, gain1, shift1, b2, gain2, shift2, b1, bq, bv)
    (full, grads, dq, dk, dv, do, d1, d2, gbq, gbv, gb1, gbo, gg1, gs1, gb2, gg2, gs2) = finish_call(
        *layer_call(weights, vectors, doc_lengths, tokens, cotangent, T), T)
    return full, grads, dq, gbq, dk, dv, gbv, do, gbo, gg1, gs1, d1, gb1, d2.T, gb2, gg2, gs2


def solution(mesh):
    placed = (
        P("dp", None),
        P("dp", None),
        P("dp", "tensor"),
        P("tensor"),
        P("dp", "tensor"),
        P("dp", "tensor"),
        P("tensor"),
        P("tensor", "dp"),
        P(),
        P(),
        P(),
        P("dp", "tensor"),
        P("tensor"),
        P("tensor", "dp"),
        P(),
        P(),
        P(),
        P("dp", None),
    )
    if mesh.shape["dp"] == 8 and mesh.shape["tensor"] == 4:
        body = partial(split_body, mesh.shape["tensor"])
    else:
        body = general_body
    return jax.shard_map(
        body,
        mesh=mesh,
        in_specs=placed,
        out_specs=(
            P("dp", None),
            P("dp", None),
            P("dp", "tensor"),
            P("tensor"),
            P("dp", "tensor"),
            P("dp", "tensor"),
            P("tensor"),
            P("tensor", "dp"),
            P(),
            P(),
            P(),
            P("dp", "tensor"),
            P("tensor"),
            P("tensor", "dp"),
            P(),
            P(),
            P(),
        ),
        check_vma=False,
    )
```

```python
from functools import partial
import jax
import jax.numpy as jnp
from jax import lax
from jax.experimental import pallas as pl
from jax.experimental.pallas import tpu as pltpu

from jax.sharding import PartitionSpec as P

BF = jnp.bfloat16
F32 = jnp.float32
EPS = 1e-12
HD = 64
NEG = -1e30
RB = 256


def nn(a, b):
    return jnp.dot(a, b, preferred_element_type=F32)


def nt(a, b):
    return lax.dot_general(a, b, (((1,), (1,)), ((), ())), preferred_element_type=F32)


def rows(r, n=RB):
    return pl.ds(pl.multiple_of(r * n, n), n)


def mean_last(x):
    return jnp.mean(x, axis=-1, keepdims=True)


def colsum(x):
    return jnp.sum(x, axis=0, keepdims=True)


MESH = pl.DeviceIdType.MESH


def remote(src, dst, send, recv, device):
    return pltpu.make_async_remote_copy(
        src_ref=src, dst_ref=dst, send_sem=send, recv_sem=recv, device_id=device, device_id_type=MESH
    )


def layer_kernel(
    WQ, WK, WV, WO, W1, W2T, BO_, GAIN1, SHIFT1, B2_, GAIN2, SHIFT2, B1_, BQ_, BV_, LEN, TOK, COT,
    OF, GF, GR, SMO,
    PK, W_, X, CO, SG, NP, BP, BI, SM,
    q, k, v, mixed, vT, oT, lse, bias, n1, r1, flow, hid, gp, gz, low, xT,
    rgt, rc, ra, rb, rz, ssend, srecv,
    loc, us, ur, zs, zf, zr, os_, xr, yr, cr, fs, dr, ks, bs, br, ts, tr,
    gs, gr, osem, orcv, osl, gsem, grcv, gsl, fwd, cs, crr, s1, q1, s2, q2, s3, q3, ms, mr,
):
    SL, S, D = PK.shape
    T = W_.shape[1]
    L = X.shape[0]
    M = L // 2
    W = D // T
    NH = W // HD
    scale = HD ** (-0.5)
    QC = M

    dp = lax.axis_index("dp")
    z = lax.axis_index("tensor")
    core = dp % 2
    dpc = dp + 1 - 2 * core
    dpx = dp + 2 - 4 * ((dp // 2) % 2)
    dpy = dp + 4 - 8 * ((dp // 4) % 2)
    dpxy = dpx + dpy - dp
    flip = dpc - dp
    home = z // 2
    own = core * M
    oth = (1 - core) * M

    def ownrows(r):
        return pl.ds(pl.multiple_of(own + r * RB, RB), RB)

    def othrows(r):
        return pl.ds(pl.multiple_of(oth + r * RB, RB), RB)

    ownhalf = pl.ds(pl.multiple_of(own, M), M)
    othhalf = pl.ds(pl.multiple_of(oth, M), M)

    PK[0, :, 0:W] = WQ[...]
    PK[0, :, W:2 * W] = WK[...]
    PK[0, :, 2 * W:3 * W] = WV[...]
    PK[0, :, 3 * W:4 * W] = WO[...].T
    PK[1] = W1[...]
    PK[2] = W2T[...]
    for i, ref in enumerate((BO_, GAIN1, SHIFT1, B2_, GAIN2, SHIFT2)):
        NP[i:i + 1, :] = ref[...].reshape(1, D)
    BP[0:1, :] = B1_[...].reshape(1, D)
    BP[1:2, 0:W] = BQ_[...].reshape(1, W)
    BP[2:3, 0:W] = BV_[...].reshape(1, W)

    spot = lax.broadcasted_iota(jnp.int32, (8, L), 1)
    doc = jnp.zeros((8, L), F32)
    end = jnp.int32(0)
    for j in range(LEN.shape[1]):
        end = end + LEN[z % 2, j]
        doc = doc + jnp.where(spot >= end, 1.0, 0.0)
    SG[0] = doc

    barrier = pltpu.get_barrier_semaphore()
    friends = [(dp, (z + d) % T) for d in range(1, T)] + [(dpc, (z + d) % T) for d in range(T)] + [
        (dpx, z), (dpy, z)]
    for friend in friends:
        pl.semaphore_signal(barrier, inc=1, device_id=friend, device_id_type=MESH)
    pl.semaphore_wait(barrier, len(friends))

    CUT = S // 2

    def late(t, i):
        return W_.at[SL - 1, t, pl.ds(pl.multiple_of(i * S + CUT, CUT), CUT), :]

    half = z // 2

    def source(d):
        edge = z + half * (3 - 2 * z)
        swap = edge * (1 - d // 2)
        t = swap * (1 - d) + (1 - swap) * d
        return t + half * (3 - 2 * t)

    right, left = (dp, (z + 1) % T), (dp, (z + T - 1) % T)
    can_right, can_left = z < T - 1, z > 0

    def each(s, copies):
        if isinstance(s, int):
            copies(CUT if s == SL - 1 else S)
        else:
            pl.when(s < SL - 1)(lambda: copies(S))
            pl.when(s == SL - 1)(lambda: copies(CUT))

    def shard(s, n):
        return PK.at[s, 0:n, :]

    def block(s, t, i, n):
        return W_.at[s, t, pl.ds(pl.multiple_of(i * S, S), n), :]

    def send_z(s, n):
        return (
            (can_right, remote(shard(s, n), block(s, z, dp, n), zs.at[s, 0], zr.at[s, z], right)),
            (can_left, remote(shard(s, n), block(s, z, dp, n), zs.at[s, 1], zr.at[s, z], left)),
        )

    def pass_z(s, t, n):
        here = block(s, t, dp, n)
        return (
            (can_right & (t < z), remote(here, here, zf.at[s, t], zr.at[s, t], right)),
            (can_left & (t > z), remote(here, here, zf.at[s, t], zr.at[s, t], left)),
        )

    def push_z(s):
        for able, copy in send_z(s, CUT if s == SL - 1 else S):
            pl.when(able)(copy.start)

    def send_block(s, d, src, n):
        t = source(d)
        remote(src, block(s, t, dp, n), os_.at[0, s], xr.at[s, d], (dpx, z)).start()
        remote(src, block(s, t, dp, n), os_.at[1, s], yr.at[s, d], (dpy, z)).start()
        remote(src, block(s, t, dp, n), os_.at[2, s], cr.at[s, d], (dpc, z)).start()

    def pass_core(kind, s, d, i, n):
        here = block(s, source(d), i, n)
        remote(here, here, ks.at[kind - 1, s], cr.at[s, d], (dpc, z)).start()

    def take_z(s, d, n):
        t = source(d)
        remote(shard(s, n), block(s, t, dp, n), zs.at[s, 0], zr.at[s, t], right).wait_recv()
        for able, copy in pass_z(s, t, n):
            pl.when(able)(copy.start)
        send_block(s, d, block(s, t, dp, n), n)

    def take_xy(s, d, n):
        t = source(d)
        fromx, fromy = block(s, t, dpx, n), block(s, t, dpy, n)
        remote(shard(s, n), fromx, os_.at[0, s], xr.at[s, d], (dpx, z)).wait_recv()

        @pl.when(d < T // 2)
        def _():
            remote(fromx, fromx, fs.at[s], dr.at[s, d], (dpy, z)).start()

        pass_core(1, s, d, dpx, n)
        remote(shard(s, n), fromy, os_.at[1, s], yr.at[s, d], (dpy, z)).wait_recv()

        @pl.when(d >= T // 2)
        def _():
            remote(fromy, fromy, fs.at[s], dr.at[s, d], (dpx, z)).start()

        pass_core(2, s, d, dpy, n)

    def take_diag(s, d, n):
        remote(shard(s, n), block(s, source(d), dpxy, n), fs.at[s], dr.at[s, d], (dpx, z)).wait_recv()
        pass_core(3, s, d, dpxy, n)

    def late_to(way, i, who):
        src = PK.at[SL - 1, CUT:S, :] if way < 2 else late(z, i)
        return remote(src, late(z, i), us.at[way], ur.at[way], who)

    chips = (dp, dpx, dpy, dpxy)

    def bundle(t, send, recv, who):
        return [remote(late(t, i), late(t, i), us.at[send], ur.at[recv], who) for i in chips]

    def whole(t, send, recv, who):
        every = W_.at[SL - 1, t, 0:4 * CUT, :]
        return remote(every, every, us.at[send], ur.at[recv], who)

    def late_core(t):
        for copy in bundle(t, 5 + T + t, 3 + T + t, (dpc, z)):
            copy.start()

    def late_start():
        late_to(0, dp, (dpx, z)).start()
        late_to(1, dp, (dpy, z)).start()

    def late_turn():
        late_to(0, dpx, (dpx, z)).wait_recv()
        late_to(2, dpx, (dpy, z)).start()

    def late_along():
        late_to(1, dpy, (dpy, z)).wait_recv()
        late_to(2, dpxy, (dpy, z)).wait_recv()
        for able, send, who in ((can_right, 3, right), (can_left, 4, left)):
            @pl.when(able)
            def _():
                for copy in bundle(z, send, 3 + z, who):
                    copy.start()
        late_core(z)

    def late_pass(t):
        whole(t, 3, 3 + t, right).wait_recv()
        for able, who in ((can_right & (t < z), right), (can_left & (t > z), left)):
            @pl.when(able)
            def _():
                for copy in bundle(t, 5 + t, 3 + t, who):
                    copy.start()
        late_core(t)

    def late_sent():
        for way, who in ((0, dpx), (1, dpy), (2, dpy)):
            late_to(way, dp, (who, z)).wait_send()
        pl.when(can_right)(whole(z, 3, 3, right).wait_send)
        pl.when(can_left)(whole(z, 4, 3, left).wait_send)
        for t in range(T):
            pl.when((can_right & (t < z)) | (can_left & (t > z)))(whole(t, 5 + t, 3, right).wait_send)
            whole(t, 5 + T + t, 3, (dpc, z)).wait_send()

    PIECES = SL * T
    XL, DL = 2, 4
    STEPS = PIECES + DL
    first_steps = DL

    def gather_step(n):
        n = jnp.int32(n)

        def piece(lag, what):
            @pl.when((n >= lag) & (n < PIECES + lag))
            def _():
                s, d = (n - lag) // T, (n - lag) % T
                each(s, lambda size: what(s, d, size))

        def arrive(s, d, size):
            pl.when(d > 0)(lambda: take_z(s, d, size))
            pl.when(d == 0)(lambda: send_block(s, d, shard(s, size), size))

        piece(0, arrive)
        for when, act in LATE:
            pl.when(n == when)(act)
        piece(XL, take_xy)
        piece(DL, take_diag)

    LATE = (
        (0, late_start), (1, late_turn), (3, late_along),
        (6, lambda: late_pass(source(1))), (8, lambda: late_pass(source(2))), (10, lambda: late_pass(source(3))),
    )

    def gathered(s, d):
        n = CUT if s == SL - 1 else S
        four = W_.at[s, source(d), 0:4 * n, :]
        remote(four, four, os_.at[2, s], cr.at[s, d], (dpc, z)).wait_recv()
        if s == SL - 1:
            whole(source(d), 3, 3 + T + source(d), (dpc, z)).wait_recv()

    for s in range(SL):
        push_z(s)
    seq = pl.ds(pl.multiple_of((z % 2) * L, L), L)
    mine = pl.ds(pl.multiple_of((z % 2) * L + own, M), M)
    other = pl.ds(pl.multiple_of((z % 2) * L + oth, M), M)
    tok_out = remote(TOK.at[seq], X, ts.at[0], tr.at[0], (dpc, z))
    cot_out = remote(COT.at[other], CO, ts.at[1], tr.at[1], (dpc, z))
    doc_out = remote(SG.at[0], SG.at[1], ts.at[2], tr.at[2], (dpc, z))
    tok_in = pltpu.make_async_copy(TOK.at[seq], X, loc.at[0])
    cot_in = pltpu.make_async_copy(COT.at[mine], CO, loc.at[1])

    @pl.when(core == home)
    def _():
        for copy in (tok_out, cot_out, doc_out, tok_in, cot_in):
            copy.start()

    for d in range(1, T):
        remote(BP, BI.at[z], bs.at[d - 1], br.at[d - 1], (dp, (z + d) % T)).start()
    for s in range(SL):
        W_[s, z, pl.ds(pl.multiple_of(dp * S, S), S), :] = PK[s]
    BI[z] = BP[...]
    SM[...] = jnp.zeros_like(SM)

    @pl.loop(0, 2)
    def _(n):
        gather_step(n)

    @pl.when(core == home)
    def _():
        tok_in.wait()
        cot_in.wait()
        for copy in (tok_out, cot_out, doc_out):
            copy.wait_send()

    @pl.when(core != home)
    def _():
        for copy in (tok_out, cot_out, doc_out):
            copy.wait_recv()

    for d in range(1, T):
        remote(BP, BI.at[(z - d + T) % T], bs.at[d - 1], br.at[d - 1], (dp, (z + 1) % T)).wait_recv()

    docs = jnp.where(core == home, SG[0], SG[1])
    SG[0] = docs
    key_doc = jnp.broadcast_to(docs[0:1, :], (128, L)).T
    for i in range(M // 128):
        query_doc = SG[0, 0:1, pl.ds(pl.multiple_of(own + i * 128, 128), 128)]
        bias[:, i * 128:(i + 1) * 128] = jnp.where(key_doc == query_doc, 0.0, NEG)

    @pl.loop(2, first_steps)
    def _(n):
        gather_step(n)

    @pl.loop(0, T)
    def _(d):
        gather_step(first_steps + d)
        gathered(0, d)
        t = source(d)
        mine_qkv = nn(X[ownhalf, :], W_[0, t, :, 0:3 * W])
        q[t, :, 0:W] = ((mine_qkv[:, 0:W] + BI[t, 1:2, 0:W]).astype(BF) * BF(scale)).astype(BF)
        k[t, ownhalf, 0:W] = mine_qkv[:, W:2 * W].astype(BF)
        v[t, ownhalf, 0:W] = (mine_qkv[:, 2 * W:3 * W] + BI[t, 2:3, 0:W]).astype(BF)
        their_kv = nn(X[othhalf, :], W_[0, t, :, W:3 * W])
        k[t, othhalf, 0:W] = their_kv[:, 0:W].astype(BF)
        v[t, othhalf, 0:W] = (their_kv[:, W:2 * W] + BI[t, 2:3, 0:W]).astype(BF)

    lane = lax.broadcasted_iota(jnp.int32, (1, 128), 1)

    def head(ref, t, rr, j):
        if j % 2 == 0 and j == NH - 1:
            return ref[t, rr, j * HD:(j + 1) * HD]
        p = j // 2
        return ref[t, rr, p * 128:(p + 1) * 128]

    def only(part, j):
        if part.shape[1] == HD:
            return part
        keep = (lane < HD) if j % 2 == 0 else (lane >= HD)
        return jnp.where(keep, part, jnp.zeros_like(part))

    everything = slice(None)

    @pl.loop(0, T)
    def _(t):
        vT[...] = v[t, :, 0:W].T

        for j in range(NH):
            s = nt(head(k, t, everything, j), only(head(q, t, everything, j), j)) + bias[...]
            m = jnp.max(s, axis=0, keepdims=True)
            p = jnp.exp(s - m)
            l = jnp.sum(p, axis=0, keepdims=True)
            lse[t * 4 + j] = jnp.broadcast_to(m + jnp.log(l), (8, M))
            o = nn(vT[j * HD:(j + 1) * HD, :], p.astype(BF))
            oT[j * HD:(j + 1) * HD, :] = o * (1.0 / l)

        mixed[t, :, 0:W] = oT[...].T.astype(BF)
        gather_step(first_steps + T + t)

    @pl.loop(0, M // RB)
    def _(r):
        zz = X[ownrows(r), :].astype(F32) + NP[0:1, :]
        for t in range(T):
            zz = zz + nt(mixed[t, rows(r), 0:W], W_[0, t, :, 3 * W:4 * W])
        cen = zz - mean_last(zz)
        rs = lax.rsqrt(mean_last(cen * cen) + EPS)
        n = cen * rs
        n1[rows(r), :] = n
        r1[rows(r), :] = jnp.broadcast_to(rs, (RB, 128))
        flow[rows(r), :] = (n * NP[1:2, :] + NP[2:3, :]).astype(BF)

    @pl.loop(0, T)
    def _(d):
        gather_step(first_steps + 2 * T + d)
        gathered(1, d)
        t = source(d)
        inner = nn(flow[...], W_[1, t]) + BI[t, 0:1, :]
        phi = 0.5 * (1.0 + lax.erf(inner * (2.0 ** -0.5)))
        hid[t] = (inner * phi).astype(BF)
        gp[t] = (phi + inner * (jnp.exp(-0.5 * inner * inner) * 0.3989422804014327)).astype(BF)

    gz[...] = n1[...] * NP[1:2, :] + NP[2:3, :] + NP[3:4, :]

    @pl.loop(0, T)
    def _(d):
        gathered(2, d)
        t = source(d)
        gz[...] += nt(hid[t], W_[2, t])

    @pl.loop(0, M // RB)
    def _(r):
        rr = rows(r)
        zz = gz[rr, :]
        cen = zz - mean_last(zz)
        rs = lax.rsqrt(mean_last(cen * cen) + EPS)
        n = cen * rs
        ct = CO[rr, :].astype(F32)
        CO[rr, :] = (n * NP[4:5, :] + NP[5:6, :]).astype(BF)
        g = ct * NP[4:5, :]
        g2 = rs * (g - mean_last(g) - n * mean_last(g * n))
        SM[16:17, :] += colsum(ct * n)
        SM[17:18, :] += colsum(ct)
        SM[13:14, :] += colsum(g2)
        gz[rr, :] = g2
        low[rr, :] = g2.astype(BF)

    dest = dp - core + home

    PARTS = 2
    PR = M // PARTS

    def spotrows(b, cc, part):
        return pl.ds(pl.multiple_of(((b % 2) * 2 + cc) * M + part * PR, PR), PR)

    def spotsem(b, cc, part):
        return ((b % 2) * 2 + cc) * PARTS + part

    def pushes(src, full, sems, recv):
        return [
            (able, remote(src.at[pl.ds(part * PR, PR)], full.at[spotrows(z, core, part)],
                          sems.at[i * PARTS + part], recv.at[spotsem(z, core, part)], chip))
            for part in range(PARTS)
            for i, (able, chip) in enumerate((
                (can_right, (dest, (z + 1) % T)), (can_left, (dest, (z + T - 1) % T)), (core != home, (dpc, z))))
        ]

    def here(src, full, slot):
        rows_ = pl.ds(pl.multiple_of(((z % 2) * 2 + core) * M, M), M)
        return pltpu.make_async_copy(src, full.at[rows_], slot)

    def push(src, full, sems, recv, slot):
        for able, copy in pushes(src, full, sems, recv):
            pl.when(able)(copy.start)
        pl.when(core == home)(here(src, full, slot).start)

    def pushed(src, full, sems, recv, slot):
        for able, copy in pushes(src, full, sems, recv):
            pl.when(able)(copy.wait_send)
        pl.when(core == home)(here(src, full, slot).wait)

    ahead = 1 - 2 * core

    def moves(hop):
        if hop == 0:
            return (z == 1) | (z == 2)
        return z == 2 - core

    def got(src, full, recv, b, cc, part):
        remote(src.at[0:PR], full.at[spotrows(b, cc, part)], gs, recv.at[spotsem(b, cc, part)], (dpx, z)).wait_recv()

    def handing(full, recv, base, hop, cc, part):
        b = z - ahead * (hop + 1)
        spot_ = full.at[spotrows(b, cc, part)]
        return remote(spot_, spot_, fwd.at[base + (2 * hop + cc) * PARTS + part],
                      recv.at[spotsem(b, cc, part)], (dp, (z + ahead) % T))

    def hand_on(src, full, recv, base, hop, part):
        @pl.when(moves(hop))
        def _():
            for cc in range(2):
                got(src, full, recv, z - ahead * (hop + 1), cc, part)
                handing(full, recv, base, hop, cc, part).start()

    def settle(src, full, recv, base):
        for kk in range(2):
            for cc in range(2):
                b = core * 2 + kk
                gone = (moves(0) & (b == z - ahead)) | (moves(1) & (b == z - 2 * ahead))

                @pl.when(jnp.logical_not((b == z) & (core == cc)) & jnp.logical_not(gone))
                def _():
                    for part in range(PARTS):
                        got(src, full, recv, b, cc, part)

        for hop in range(2):
            @pl.when(moves(hop))
            def _():
                for cc in range(2):
                    for part in range(PARTS):
                        handing(full, recv, base, hop, cc, part).wait_send()

    push(CO, OF, osem, orcv, osl)

    for s in range(SL):
        n = CUT if s == SL - 1 else S
        for able, copy in send_z(s, n):
            pl.when(able)(copy.wait_send)
        for t in range(T):
            for able, copy in pass_z(s, t, n):
                pl.when(able)(copy.wait_send)
        four = W_.at[s, z, 0:4 * n, :]
        for kind in range(3):
            remote(four, four, os_.at[kind, s], xr.at[s, 0], (dpx, z)).wait_send()
            remote(four, four, ks.at[kind, s], xr.at[s, 0], (dpx, z)).wait_send()
        remote(four, four, fs.at[s], xr.at[s, 0], (dpx, z)).wait_send()
    late_sent()
    for d in range(1, T):
        remote(BP, BI.at[z], bs.at[d - 1], br.at[d - 1], (dp, (z + d) % T)).wait_send()

    def grad(s):
        return W_.at[s]

    rel = (dp, dpx, dpy, dpxy)

    def rowsof(i):
        return pl.ds(pl.multiple_of(i * S, S), S)

    def core_copy(s, kk):
        return remote(grad(s).at[:, rowsof(rel[kk] + flip), :], rc.at[s, kk], cs.at[s], crr.at[s, kk], (dpc, z))

    def turn(s, kk):
        src, dst, who = (
            (rc.at[s, 3, 0:2], ra.at[s, 0], (dpy, z)),
            (rc.at[s, 3, 2:4], ra.at[s, 1], (dpx, z)),
        )[kk]
        return remote(src, dst, s1.at[s, kk], q1.at[s, kk], who)

    def straight(s, kk):
        src, dst, who = (
            (rc.at[s, 1, 2:4], rb.at[s, 0, 2:4], (dpx, z)),
            (rc.at[s, 2, 0:2], rb.at[s, 1, 0:2], (dpy, z)),
            (rc.at[s, 1, 0:2], rb.at[s, 0, 0:2], (dpx, z)),
            (rc.at[s, 2, 2:4], rb.at[s, 1, 2:4], (dpy, z)),
        )[kk]
        return remote(src, dst, s2.at[s, kk], q2.at[s, kk], who)

    def along(s, t, sign):
        way = (1 - sign) // 2
        return remote(rc.at[s, 0, t], rz.at[s, way, t], s3.at[s, way, t], q3.at[s, way, t], (dp, (z + sign + T) % T))

    def add(dst, src):
        @pl.loop(0, dst.shape[0])
        def _(t):
            dst[t] = (dst[t].astype(F32) + src[t].astype(F32)).astype(BF)

    def sum_start(s):
        for kk in (3, 1, 2, 0):
            core_copy(s, kk).start()

    def sum_core(s):
        for kk in (3, 1, 2, 0):
            core_copy(s, kk).wait_recv()
            add(rc.at[s, kk], grad(s).at[:, rowsof(rel[kk]), :])
            if kk == 3:
                turn(s, 0).start()
                turn(s, 1).start()
            if kk == 1:
                straight(s, 0).start()
            if kk == 2:
                straight(s, 1).start()

    def sum_turn(s):
        turn(s, 0).wait_recv()
        add(rc.at[s, 1, 0:2], ra.at[s, 0])
        straight(s, 2).start()
        turn(s, 1).wait_recv()
        add(rc.at[s, 2, 2:4], ra.at[s, 1])
        straight(s, 3).start()

    def sum_straight(s):
        for kk in range(4):
            straight(s, kk).wait_recv()
        add(rc.at[s, 0], rb.at[s, 0])
        add(rc.at[s, 0], rb.at[s, 1])

    def sum_along(s):
        @pl.loop(0, 2)
        def _(i):
            sign = (1 - 2 * half) * (1 - 2 * i)
            way = (1 - sign) // 2
            behind = z - sign

            @pl.loop(0, T - 1)
            def _(j):
                t = (1 - way) * (T - 1 - j) + way * j

                @pl.when((t - z) * sign > 0)
                def _():
                    @pl.when((behind >= 0) & (behind < T))
                    def _():
                        along(s, t, sign).wait_recv()
                        rc[s, 0, t] = (rc[s, 0, t].astype(F32) + rz[s, way, t].astype(F32)).astype(BF)

                    along(s, t, sign).start()

    def sum_last(s):
        GR[s] = rc[s, 0, z].astype(F32)
        for sign in (1, -1):
            @pl.when((z - sign >= 0) & (z - sign < T))
            def _():
                along(s, z, sign).wait_recv()
                GR[s] += rz[s, (1 - sign) // 2, z].astype(F32)

    def sum_sent(s):
        for sign in (1, -1):
            for t in range(T):
                pl.when((t - z) * sign > 0)(along(s, t, sign).wait_send)

    xT[:, 0:M] = low[...].T
    xT[:, M:L] = flow[...].T

    @pl.loop(0, T)
    def _(t):
        gi = (nn(low[...], W_[2, t]) * gp[t].astype(F32)).astype(BF)
        gp[t] = gi
        SM[pl.ds(2 * T + t, 1), :] += colsum(gi.astype(F32))
        gz[...] += nt(gi, W_[1, t])
        W_[2, t] = nn(xT[:, 0:M], hid[t]).astype(BF)
        W_[1, t] = nn(xT[:, M:L], gi).astype(BF)

    hand_on(CO, OF, orcv, 0, 0, 0)
    sum_start(2)
    sum_start(1)

    @pl.loop(0, M // RB)
    def _(r):
        rr = rows(r)
        gf = gz[rr, :]
        n = n1[rr, :]
        g = gf * NP[1:2, :]
        g1 = r1[rr, 0:1] * (g - mean_last(g) - n * mean_last(g * n))
        SM[14:15, :] += colsum(gf * n)
        SM[15:16, :] += colsum(gf)
        SM[12:13, :] += colsum(g1)
        gz[rr, :] = g1
        low[rr, :] = g1.astype(BF)

    xT[:, 0:M] = low[...].T

    @pl.loop(0, T)
    def _(t):
        hid[t, :, 0:W] = nn(low[...], W_[0, t, :, 3 * W:4 * W]).astype(BF)

    @pl.loop(0, T)
    def _(t):
        @pl.when(t == 0)
        def _():
            sum_core(2)
            hand_on(CO, OF, orcv, 0, 0, 1)

        @pl.when(t == 1)
        def _():
            sum_core(1)

        @pl.when(t == 2)
        def _():
            sum_turn(2)
            hand_on(CO, OF, orcv, 0, 1, 0)

        @pl.when(t == 3)
        def _():
            sum_turn(1)
            hand_on(CO, OF, orcv, 0, 1, 1)

        vT[...] = k[t, :, 0:W].T
        for pair in range((NH + 1) // 2):
            heads = [j for j in (2 * pair, 2 * pair + 1) if j < NH]
            wide = HD * len(heads)
            dk = jnp.zeros((L, wide), F32)
            dv = jnp.zeros((L, wide), F32)
            for j in heads:
                for i in range(M // QC):
                    qs = slice(i * QC, (i + 1) * QC)
                    qm = only(head(q, t, qs, j), j)
                    om = only(head(hid, t, qs, j), j)
                    s = nt(head(k, t, everything, j), qm) + bias[:, qs]
                    p = jnp.exp(s - lse[t * 4 + j, 0:1, qs])
                    dpr = nt(head(v, t, everything, j), om)
                    cen = jnp.sum(p * dpr, axis=0, keepdims=True)
                    ds = (p * (dpr - cen)).astype(BF)
                    dv = dv + nn(p.astype(BF), om)
                    dk = dk + nn(ds, qm)
                    oT[j * HD:(j + 1) * HD, qs] = nn(vT[j * HD:(j + 1) * HD, :], ds) * scale
            lanes = slice(pair * 128, pair * 128 + wide)
            k[t, :, lanes] = dk.astype(BF)
            v[t, :, lanes] = dv.astype(BF)
        dq = oT[...].T.astype(BF)
        q[t, :, 0:W] = dq
        SM[pl.ds(t, 1), 0:W] += colsum(dq.astype(F32))
        SM[pl.ds(T + t, 1), 0:W] += colsum(v[t, :, 0:W].astype(F32))

    @pl.loop(0, M // RB)
    def _(r):
        acc = jnp.zeros((RB, D), F32)
        for t in range(T):
            acc = acc + nt(k[t, othrows(r), 0:W], W_[0, t, :, W:2 * W])
            acc = acc + nt(v[t, othrows(r), 0:W], W_[0, t, :, 2 * W:3 * W])
        flow[rows(r), :] = acc.astype(BF)

    part = remote(flow, rgt, gs, gr, (dpc, z))
    part.start()

    @pl.loop(0, M // RB)
    def _(r):
        acc = gz[rows(r), :]
        for t in range(T):
            acc = acc + nt(q[t, rows(r), 0:W], W_[0, t, :, 0:W])
            acc = acc + nt(k[t, ownrows(r), 0:W], W_[0, t, :, W:2 * W])
            acc = acc + nt(v[t, ownrows(r), 0:W], W_[0, t, :, 2 * W:3 * W])
        gz[rows(r), :] = acc

    part.wait_recv()
    low[...] = (gz[...] + rgt[...].astype(F32)).astype(BF)
    push(low, GF, gsem, grcv, gsl)

    pals = [(dpc, z), (dpx, z), (dpy, z), (dp, z + 1 - 2 * (z % 2)), (dp, (z + 2) % T)]

    def small(step):
        return remote(ssend.at[step], srecv.at[step], ms.at[step], mr.at[step], pals[step])

    def small_start(step):
        ssend[step] = SM[...]
        small(step).start()

    def small_end(step):
        small(step).wait_recv()
        SM[...] += srecv[step]

    small_start(0)

    @pl.loop(0, T)
    def _(t):
        W_[0, t, :, 3 * W:4 * W] = nn(xT[:, 0:M], mixed[t, :, 0:W]).astype(BF)

    xT[...] = X[...].T

    @pl.loop(0, T)
    def _(t):
        W_[0, t, :, 0:W] = nn(xT[:, pl.ds(pl.multiple_of(own, 128), M)], q[t, :, 0:W]).astype(BF)
        W_[0, t, :, W:2 * W] = nn(xT[...], k[t, :, 0:W]).astype(BF)
        W_[0, t, :, 2 * W:3 * W] = nn(xT[...], v[t, :, 0:W]).astype(BF)

    sum_start(0)
    hand_on(low, GF, grcv, 8, 0, 0)
    small_end(0)
    small_start(1)
    sum_core(0)
    hand_on(low, GF, grcv, 8, 0, 1)
    small_end(1)
    small_start(2)
    sum_straight(2)
    sum_turn(0)
    hand_on(low, GF, grcv, 8, 1, 0)
    sum_along(2)
    small_end(2)
    small_start(3)
    sum_straight(1)
    hand_on(low, GF, grcv, 8, 1, 1)
    sum_along(1)
    small_end(3)
    small_start(4)
    sum_straight(0)
    sum_along(0)
    small_end(4)
    for s in (2, 1, 0):
        sum_last(s)
    SMO[...] = SM[...]
    settle(CO, OF, orcv, 0)
    settle(low, GF, grcv, 8)
    pushed(CO, OF, osem, orcv, osl)
    pushed(low, GF, gsem, grcv, gsl)
    part.wait_send()
    for step in range(5):
        small(step).wait_send()
    for s in range(SL):
        for kk in range(4):
            straight(s, kk).wait_send()
        remote(rc.at[s], rc.at[s], cs.at[s], crr.at[s, 0], (dpc, z)).wait_send()
        turn(s, 0).wait_send()
        turn(s, 1).wait_send()
        sum_sent(s)


def layer_call(weights, vectors, lengths, tokens, cotangent, T):
    wq, w1 = weights[0], weights[4]
    S, W = wq.shape
    D = tokens.shape[1]
    F = w1.shape[1]
    L = tokens.shape[0] // lengths.shape[0]
    M = L // 2
    SL = 3
    WP = 256
    any_ = pl.BlockSpec(memory_space=pl.ANY)
    vm = pl.BlockSpec(memory_space=pltpu.VMEM)
    dma = pltpu.SemaphoreType.DMA
    f32 = lambda *s: jax.ShapeDtypeStruct(s, F32)
    V = pltpu.VMEM
    return pl.pallas_call(
        layer_kernel,
        in_specs=[vm] * (len(weights) + len(vectors)) + [pl.BlockSpec(memory_space=pltpu.SMEM), any_, any_],
        out_specs=[any_, any_, vm, vm],
        out_shape=[
            jax.ShapeDtypeStruct((4 * M, D), BF),
            jax.ShapeDtypeStruct((4 * M, D), BF),
            f32(SL, S, D), f32(24, D),
        ],
        scratch_shapes=[
            V((SL, S, D), BF),
            V((SL, T, D, F), BF),
            V((L, D), BF),
            V((M, D), BF),
            V((2, 8, L), F32),
            V((8, D), F32),
            V((8, D), F32),
            V((T, 8, D), F32),
            V((24, D), F32),
            V((T, M, WP), BF),
            V((T, L, WP), BF),
            V((T, L, WP), BF),
            V((T, M, WP), BF),
            V((W, L), BF),
            V((W, M), F32),
            V((T * 4, 8, M), F32),
            V((L, M), F32),
            V((M, D), F32),
            V((M, 128), F32),
            V((M, D), BF),
            V((T, M, F), BF),
            V((T, M, F), BF),
            V((M, D), F32),
            V((M, D), BF),
            V((D, L), BF),
            V((M, D), BF),
            V((SL, 4, T, S, D), BF),
            V((SL, 2, 2, S, D), BF),
            V((SL, 2, T, S, D), BF),
            V((SL, 2, T, S, D), BF),
            V((5, 24, D), F32),
            V((5, 24, D), F32),
            dma((2,)),
            dma((5 + 2 * T,)), dma((3 + 2 * T,)),
            dma((SL, 2)), dma((SL, T)), dma((SL, T)),
            dma((3, SL)), dma((SL, T)), dma((SL, T)), dma((SL, T)),
            dma((SL,)), dma((SL, T)),
            dma((3, SL)),
            dma((T - 1,)), dma((T - 1,)),
            dma((3,)), dma((3,)),
            dma, dma,
            dma((6,)), dma((8,)), dma,
            dma((6,)), dma((8,)), dma,
            dma((16,)),
            dma((SL,)), dma((SL, 4)),
            dma((SL, 2)), dma((SL, 2)),
            dma((SL, 4)), dma((SL, 4)),
            dma((SL, 2, T)), dma((SL, 2, T)),
            dma((5,)), dma((5,)),
        ],
        compiler_params=pltpu.CompilerParams(
            collective_id=0, has_side_effects=True, vmem_limit_bytes=64 << 20
        ),
    )(*weights, *vectors, lengths, tokens, cotangent)


def finish_kernel(OF, GF, GR, SMO, OUT, GT, *rest):
    outs, (keep, gr, sm, *bufs, came, went, read, wrote) = rest[:15], rest[15:]
    z = lax.axis_index("tensor")
    T = lax.axis_size("tensor")
    W = bufs[0].shape[1]
    small = [pltpu.make_async_copy(GR, gr, read.at[0]), pltpu.make_async_copy(SMO, sm, read.at[1])]
    n, size = keep.shape[1:3]
    ins, backs = [], []
    for a, (src, dst) in enumerate(((GF, GT), (OF, OUT))):
        for i in range(n):
            part = pl.ds(i * size, size)
            ins.append(pltpu.make_async_copy(src.at[part], keep.at[a, i], came.at[a, i]))
            backs.append(pltpu.make_async_copy(keep.at[a, i], dst.at[part], went.at[a, i]))
    for copy in small + ins:
        copy.start()
    for copy in small:
        copy.wait()
    dq, dk, dv, do, bq, bv, b1 = bufs[:7]
    dq[...] = gr[0, :, 0:W]
    dk[...] = gr[0, :, W:2 * W]
    dv[...] = gr[0, :, 2 * W:3 * W]
    do[...] = gr[0, :, 3 * W:4 * W].T
    bq[...] = sm[pl.ds(z, 1), 0:W].reshape(W)
    bv[...] = sm[pl.ds(T + z, 1), 0:W].reshape(W)
    b1[...] = sm[pl.ds(2 * T + z, 1), :].reshape(b1.shape[0])
    for i, ref in zip((0, 2, 3, 1, 4, 5), bufs[7:]):
        ref[...] = sm[3 * T + i:3 * T + i + 1, :].reshape(ref.shape[0])
    sources = [dq, dk, dv, do, gr.at[1], gr.at[2], *bufs[4:]]
    writes = [pltpu.make_async_copy(src, dst, wrote.at[i]) for i, (src, dst) in enumerate(zip(sources, outs))]
    for copy in writes:
        copy.start()
    for a, b in zip(ins, backs):
        a.wait()
        b.start()
    for copy in backs + writes:
        copy.wait()


def finish_call(full, grads, gr, sm, T):
    SL, S, D = gr.shape
    W = D // T
    n = 4
    any_ = pl.BlockSpec(memory_space=pltpu.HBM)
    f32 = lambda *s: jax.ShapeDtypeStruct(s, F32)
    same = jax.ShapeDtypeStruct(full.shape, full.dtype)
    made = [(S, W), (S, W), (S, W), (W, S), (W,), (W,), (D,), (D,), (D,), (D,), (D,), (D,), (D,)]
    dma = pltpu.SemaphoreType.DMA
    return pl.pallas_call(
        finish_kernel,
        in_specs=[any_] * 4,
        out_specs=[any_] * 17,
        out_shape=[same, same] + [f32(*m) for m in made[:4]] + [f32(S, D), f32(S, D)] + [f32(*m) for m in made[4:]],
        scratch_shapes=[
            pltpu.VMEM((2, n, full.shape[0] // n, D), BF), pltpu.VMEM(gr.shape, F32), pltpu.VMEM(sm.shape, F32),
            *[pltpu.VMEM(m, F32) for m in made],
            dma((2, n)), dma((2, n)), dma((2,)), dma((15,)),
        ],
        compiler_params=pltpu.CompilerParams(vmem_limit_bytes=64 << 20),
    )(full, grads, gr, sm)


def doc_ids(lengths, count):
    ends = jnp.cumsum(lengths)
    places = jnp.arange(count, dtype=jnp.int32)
    return jnp.sum((places[:, None] >= ends[None, :]).astype(jnp.int32), axis=1)


def collect(wq, wk, wv, wo, w1, w2):
    return (
        lax.all_gather(wq, "dp", axis=0, tiled=True),
        lax.all_gather(wk, "dp", axis=0, tiled=True),
        lax.all_gather(wv, "dp", axis=0, tiled=True),
        lax.all_gather(wo, "dp", axis=1, tiled=True),
        lax.all_gather(w1, "dp", axis=0, tiled=True),
        lax.all_gather(w2, "dp", axis=1, tiled=True),
    )


def reduce_large(grads):
    return (
        lax.psum_scatter(grads[0], "dp", scatter_dimension=0, tiled=True),
        lax.psum_scatter(grads[1], "dp", scatter_dimension=0, tiled=True),
        lax.psum_scatter(grads[2], "dp", scatter_dimension=0, tiled=True),
        lax.psum_scatter(grads[3], "dp", scatter_dimension=1, tiled=True),
        lax.psum_scatter(grads[4], "dp", scatter_dimension=0, tiled=True),
        lax.psum_scatter(grads[5], "dp", scatter_dimension=1, tiled=True),
    )


def reduce_small(grads):
    return lax.psum(
        (grads[0], grads[1], grads[2], grads[3], grads[4], grads[5], grads[6], grads[7], grads[8]),
        "dp",
    )


def contract_rows(left, right):
    return lax.dot_general(
        left, right, (((0,), (0,)), ((), ())), preferred_element_type=jnp.float32
    )


def contract_cols(left, right):
    return lax.dot_general(
        left, right, (((1,), (1,)), ((), ())), preferred_element_type=jnp.float32
    )


def contract_mixed(left, right):
    return lax.dot_general(
        left, right, (((0,), (1,)), ((), ())), preferred_element_type=jnp.float32
    )


def norm_forward(total, gain, shift):
    centre = total - jnp.mean(total, axis=-1, keepdims=True)
    scaled = lax.rsqrt(jnp.mean(centre * centre, axis=-1, keepdims=True) + EPS)
    normed = centre * scaled
    return (normed * gain + shift, normed, scaled)


def norm_backward(grad_result, normed, scaled, gain):
    grad_normed = grad_result * gain
    mean_grad = jnp.mean(grad_normed, axis=-1, keepdims=True)
    mean_cross = jnp.mean(grad_normed * normed, axis=-1, keepdims=True)
    grad_total = scaled * (grad_normed - mean_grad - normed * mean_cross)
    return (grad_total, jnp.sum(grad_result * normed, axis=0), jnp.sum(grad_result, axis=0))


def block_scores(query_block, key_heads, seg_block, seg, scale):
    raw = (
        jnp.einsum("hdq,hdk->hqk", query_block, key_heads, preferred_element_type=jnp.float32)
        * scale
    )
    same_doc = seg_block[:, None] == seg[None, :]
    return jnp.where(same_doc[None], raw, NEG)


def general_body(
    tokens,
    doc_lengths,
    wq,
    bq,
    wk,
    wv,
    bv,
    wo,
    bo,
    gain1,
    shift1,
    w1,
    b1,
    w2,
    b2,
    gain2,
    shift2,
    cotangent,
):
    micro = doc_lengths.shape[0]
    seq_len = tokens.shape[0] // micro
    block = min(512, seq_len)
    scale = HD ** (-0.5)
    results = []
    grad_inputs = []
    large_total = None
    small_total = None
    for index in range(micro):
        full = collect(wq, wk, wv, wo, w1, w2)
        full_q, full_k, full_v, full_o, full_first, full_second = full
        width = full_q.shape[1]
        heads_here = width // HD
        rows_in = tokens[index * seq_len : (index + 1) * seq_len]
        inputs = rows_in.astype(jnp.float32)
        seg = doc_ids(doc_lengths[index], seq_len)
        queries = (
            lax.dot_general(
                full_q, rows_in, (((0,), (1,)), ((), ())), preferred_element_type=jnp.float32
            )
            + bq[:, None]
        ).astype(jnp.bfloat16)
        keys_low = lax.dot_general(
            full_k, rows_in, (((0,), (1,)), ((), ())), preferred_element_type=jnp.float32
        ).astype(jnp.bfloat16)
        values_low = (
            lax.dot_general(
                full_v, rows_in, (((0,), (1,)), ((), ())), preferred_element_type=jnp.float32
            )
            + bv[:, None]
        ).astype(jnp.bfloat16)
        query_heads = queries.reshape(heads_here, HD, seq_len)
        key_heads = keys_low.reshape(heads_here, HD, seq_len)
        value_heads = values_low.reshape(heads_here, HD, seq_len)
        pieces = []
        log_totals = []
        for offset in range(0, seq_len, block):
            scores = block_scores(
                query_heads[:, :, offset : offset + block],
                key_heads,
                seg[offset : offset + block],
                seg,
                scale,
            )
            highest = jnp.max(scores, axis=-1, keepdims=True)
            log_total = highest + jnp.log(
                jnp.sum(jnp.exp(scores - highest), axis=-1, keepdims=True)
            )
            probs_low = jnp.exp(scores - log_total).astype(jnp.bfloat16)
            pieces.append(
                jnp.einsum(
                    "hqk,hdk->hdq", probs_low, value_heads, preferred_element_type=jnp.float32
                )
            )
            log_totals.append(log_total)
        mixed_cols = jnp.concatenate(pieces, axis=2).reshape(width, seq_len).astype(jnp.bfloat16)
        attended = lax.psum(
            contract_rows(mixed_cols, full_o).astype(jnp.bfloat16), "tensor"
        ).astype(jnp.float32)
        first, normed_one, scaled_one = norm_forward(inputs + attended + bo, gain1, shift1)
        first_low = first.astype(jnp.bfloat16)
        inner = jnp.dot(first_low, full_first, preferred_element_type=jnp.float32) + b1
        hidden = jax.nn.gelu(inner, approximate=False).astype(jnp.bfloat16)
        second = lax.psum(
            jnp.dot(hidden, full_second, preferred_element_type=jnp.float32).astype(jnp.bfloat16),
            "tensor",
        ).astype(jnp.float32)
        result, normed_two, scaled_two = norm_forward(first + second + b2, gain2, shift2)
        results.append(result.astype(jnp.bfloat16))
        grad_result = cotangent[index * seq_len : (index + 1) * seq_len].astype(jnp.float32)
        grad_two, grad_gain2, grad_shift2 = norm_backward(
            grad_result, normed_two, scaled_two, gain2
        )
        grad_b2 = jnp.sum(grad_two, axis=0)
        full = collect(wq, wk, wv, wo, w1, w2)
        full_q, full_k, full_v, full_o, full_first, full_second = full
        two_low = grad_two.astype(jnp.bfloat16)
        grad_w2 = contract_rows(hidden, two_low)
        grad_hidden = contract_cols(two_low, full_second)
        grad_inner = jax.vjp(partial(jax.nn.gelu, approximate=False), inner)[1](grad_hidden)[
            0
        ].astype(jnp.bfloat16)
        grad_b1 = jnp.sum(grad_inner.astype(jnp.float32), axis=0)
        grad_w1 = contract_rows(first_low, grad_inner)
        grad_first = grad_two + lax.psum(
            contract_cols(grad_inner, full_first).astype(jnp.bfloat16), "tensor"
        ).astype(jnp.float32)
        grad_one, grad_gain1, grad_shift1 = norm_backward(grad_first, normed_one, scaled_one, gain1)
        grad_bo = jnp.sum(grad_one, axis=0)
        one_low = grad_one.astype(jnp.bfloat16)
        grad_wo = jnp.dot(mixed_cols, one_low, preferred_element_type=jnp.float32)
        grad_mixed = (
            contract_cols(full_o, one_low).astype(jnp.bfloat16).reshape(heads_here, HD, seq_len)
        )
        grad_key_heads = jnp.zeros((heads_here, HD, seq_len), jnp.float32)
        grad_value_heads = jnp.zeros((heads_here, HD, seq_len), jnp.float32)
        grad_query_pieces = []
        for number, offset in enumerate(range(0, seq_len, block)):
            query_block = query_heads[:, :, offset : offset + block]
            grad_block = grad_mixed[:, :, offset : offset + block]
            scores = block_scores(query_block, key_heads, seg[offset : offset + block], seg, scale)
            probs = jnp.exp(scores - log_totals[number])
            grad_probs = jnp.einsum(
                "hdq,hdk->hqk", grad_block, value_heads, preferred_element_type=jnp.float32
            )
            centre = jnp.sum(probs * grad_probs, axis=-1, keepdims=True)
            grad_scores = (probs * (grad_probs - centre)).astype(jnp.bfloat16)
            grad_query_pieces.append(
                jnp.einsum(
                    "hqk,hdk->hdq", grad_scores, key_heads, preferred_element_type=jnp.float32
                )
                * scale
            )
            grad_key_heads = (
                grad_key_heads
                + jnp.einsum(
                    "hqk,hdq->hdk", grad_scores, query_block, preferred_element_type=jnp.float32
                )
                * scale
            )
            grad_value_heads = grad_value_heads + jnp.einsum(
                "hqk,hdq->hdk",
                probs.astype(jnp.bfloat16),
                grad_block,
                preferred_element_type=jnp.float32,
            )
        grad_queries = (
            jnp.concatenate(grad_query_pieces, axis=2).reshape(width, seq_len).astype(jnp.bfloat16)
        )
        grad_keys = grad_key_heads.reshape(width, seq_len).astype(jnp.bfloat16)
        grad_values = grad_value_heads.reshape(width, seq_len).astype(jnp.bfloat16)
        grad_bq = jnp.sum(grad_queries.astype(jnp.float32), axis=1)
        grad_bv = jnp.sum(grad_values.astype(jnp.float32), axis=1)
        grad_wq = contract_cols(rows_in.T, grad_queries)
        grad_wk = contract_cols(rows_in.T, grad_keys)
        grad_wv = contract_cols(rows_in.T, grad_values)
        back_terms = (
            contract_mixed(grad_queries, full_q)
            + contract_mixed(grad_keys, full_k)
            + contract_mixed(grad_values, full_v)
        )
        grad_rows = grad_one + lax.psum(back_terms.astype(jnp.bfloat16), "tensor").astype(
            jnp.float32
        )
        grad_inputs.append(grad_rows.astype(jnp.bfloat16))
        large_local = (grad_wq, grad_wk, grad_wv, grad_wo, grad_w1, grad_w2)
        small_local = (
            grad_bq,
            grad_bv,
            grad_b1,
            grad_bo,
            grad_b2,
            grad_gain1,
            grad_shift1,
            grad_gain2,
            grad_shift2,
        )
        large_local = reduce_large(large_local)
        small_local = reduce_small(small_local)
        if large_total is None:
            large_total = large_local
            small_total = small_local
        else:
            large_total = jax.tree.map(jnp.add, large_total, large_local)
            small_total = jax.tree.map(jnp.add, small_total, small_local)
    grad_wq, grad_wk, grad_wv, grad_wo, grad_w1, grad_w2 = large_total
    (
        grad_bq,
        grad_bv,
        grad_b1,
        grad_bo,
        grad_b2,
        grad_gain1,
        grad_shift1,
        grad_gain2,
        grad_shift2,
    ) = small_total
    return (
        jnp.concatenate(results, axis=0),
        jnp.concatenate(grad_inputs, axis=0),
        grad_wq,
        grad_bq,
        grad_wk,
        grad_wv,
        grad_bv,
        grad_wo,
        grad_bo,
        grad_gain1,
        grad_shift1,
        grad_w1,
        grad_b1,
        grad_w2,
        grad_b2,
        grad_gain2,
        grad_shift2,
    )


def split_body(T, tokens, doc_lengths, wq, bq, wk, wv, bv, wo, bo, gain1, shift1, w1, b1, w2, b2,
               gain2, shift2, cotangent):
    weights = (wq, wk, wv, wo, w1, w2.T)
    vectors = (bo, gain1, shift1, b2, gain2, shift2, b1, bq, bv)
    (full, grads, dq, dk, dv, do, d1, d2, gbq, gbv, gb1, gbo, gg1, gs1, gb2, gg2, gs2) = finish_call(
        *layer_call(weights, vectors, doc_lengths, tokens, cotangent, T), T)
    return full, grads, dq, gbq, dk, dv, gbv, do, gbo, gg1, gs1, d1, gb1, d2.T, gb2, gg2, gs2


def solution(mesh):
    placed = (
        P("dp", None),
        P("dp", None),
        P("dp", "tensor"),
        P("tensor"),
        P("dp", "tensor"),
        P("dp", "tensor"),
        P("tensor"),
        P("tensor", "dp"),
        P(),
        P(),
        P(),
        P("dp", "tensor"),
        P("tensor"),
        P("tensor", "dp"),
        P(),
        P(),
        P(),
        P("dp", None),
    )
    if mesh.shape["dp"] == 8 and mesh.shape["tensor"] == 4:
        body = partial(split_body, mesh.shape["tensor"])
    else:
        body = general_body
    return jax.shard_map(
        body,
        mesh=mesh,
        in_specs=placed,
        out_specs=(
            P("dp", None),
            P("dp", None),
            P("dp", "tensor"),
            P("tensor"),
            P("dp", "tensor"),
            P("dp", "tensor"),
            P("tensor"),
            P("tensor", "dp"),
            P(),
            P(),
            P(),
            P("dp", "tensor"),
            P("tensor"),
            P("tensor", "dp"),
            P(),
            P(),
            P(),
        ),
        check_vma=False,
    )
```

```python
from functools import partial
import jax
import jax.numpy as jnp
from jax import lax
from jax.experimental import pallas as pl
from jax.experimental.pallas import tpu as pltpu

from jax.sharding import PartitionSpec as P

BF = jnp.bfloat16
F32 = jnp.float32
EPS = 1e-12
HD = 64
NEG = -1e30
RB = 256


def nn(a, b):
    return jnp.dot(a, b, preferred_element_type=F32)


def nt(a, b):
    return lax.dot_general(a, b, (((1,), (1,)), ((), ())), preferred_element_type=F32)


def rows(r, n=RB):
    return pl.ds(pl.multiple_of(r * n, n), n)


def mean_last(x):
    return jnp.mean(x, axis=-1, keepdims=True)


def colsum(x):
    return jnp.sum(x, axis=0, keepdims=True)


MESH = pl.DeviceIdType.MESH


def remote(src, dst, send, recv, device):
    return pltpu.make_async_remote_copy(
        src_ref=src, dst_ref=dst, send_sem=send, recv_sem=recv, device_id=device, device_id_type=MESH
    )


def layer_kernel(
    WQ, WK, WV, WO, W1, W2T, BO_, GAIN1, SHIFT1, B2_, GAIN2, SHIFT2, B1_, BQ_, BV_, LEN, TOK, COT,
    OF, GF, GR, SMO,
    PK, W_, X, CO, SG, NP, BP, BI, SM,
    q, k, v, mixed, vT, oT, lse, bias, n1, r1, flow, hid, gp, gz, low, xT,
    rgt, rc, ra, rb, rz, ssend, srecv,
    loc, us, ur, zs, zf, zr, os_, xr, yr, cr, fs, dr, ks, bs, br, ts, tr,
    gs, gr, osem, orcv, osl, gsem, grcv, gsl, fwd, cs, crr, s1, q1, s2, q2, s3, q3, ms, mr,
):
    SL, S, D = PK.shape
    T = W_.shape[1]
    L = X.shape[0]
    M = L // 2
    W = D // T
    NH = W // HD
    scale = HD ** (-0.5)
    QC = M

    dp = lax.axis_index("dp")
    z = lax.axis_index("tensor")
    core = dp % 2
    dpc = dp + 1 - 2 * core
    dpx = dp + 2 - 4 * ((dp // 2) % 2)
    dpy = dp + 4 - 8 * ((dp // 4) % 2)
    dpxy = dpx + dpy - dp
    flip = dpc - dp
    home = z // 2
    own = core * M
    oth = (1 - core) * M

    def ownrows(r):
        return pl.ds(pl.multiple_of(own + r * RB, RB), RB)

    def othrows(r):
        return pl.ds(pl.multiple_of(oth + r * RB, RB), RB)

    ownhalf = pl.ds(pl.multiple_of(own, M), M)
    othhalf = pl.ds(pl.multiple_of(oth, M), M)

    PK[0, :, 0:W] = WQ[...]
    PK[0, :, W:2 * W] = WK[...]
    PK[0, :, 2 * W:3 * W] = WV[...]
    PK[0, :, 3 * W:4 * W] = WO[...].T
    PK[1] = W1[...]
    PK[2] = W2T[...]
    for i, ref in enumerate((BO_, GAIN1, SHIFT1, B2_, GAIN2, SHIFT2)):
        NP[i:i + 1, :] = ref[...].reshape(1, D)
    BP[0:1, :] = B1_[...].reshape(1, D)
    BP[1:2, 0:W] = BQ_[...].reshape(1, W)
    BP[2:3, 0:W] = BV_[...].reshape(1, W)

    spot = lax.broadcasted_iota(jnp.int32, (8, L), 1)
    doc = jnp.zeros((8, L), F32)
    end = jnp.int32(0)
    for j in range(LEN.shape[1]):
        end = end + LEN[z % 2, j]
        doc = doc + jnp.where(spot >= end, 1.0, 0.0)
    SG[0] = doc

    barrier = pltpu.get_barrier_semaphore()
    friends = [(dp, (z + d) % T) for d in range(1, T)] + [(dpc, (z + d) % T) for d in range(T)] + [
        (dpx, z), (dpy, z)]
    for friend in friends:
        pl.semaphore_signal(barrier, inc=1, device_id=friend, device_id_type=MESH)
    pl.semaphore_wait(barrier, len(friends))

    CUT = S // 2

    def late(t, i):
        return W_.at[SL - 1, t, pl.ds(pl.multiple_of(i * S + CUT, CUT), CUT), :]

    half = z // 2

    def source(d):
        edge = z + half * (3 - 2 * z)
        swap = edge * (1 - d // 2)
        t = swap * (1 - d) + (1 - swap) * d
        return t + half * (3 - 2 * t)

    right, left = (dp, (z + 1) % T), (dp, (z + T - 1) % T)
    can_right, can_left = z < T - 1, z > 0

    def each(s, copies):
        if isinstance(s, int):
            copies(CUT if s == SL - 1 else S)
        else:
            pl.when(s < SL - 1)(lambda: copies(S))
            pl.when(s == SL - 1)(lambda: copies(CUT))

    def shard(s, n):
        return PK.at[s, 0:n, :]

    def block(s, t, i, n):
        return W_.at[s, t, pl.ds(pl.multiple_of(i * S, S), n), :]

    def send_z(s, n):
        return (
            (can_right, remote(shard(s, n), block(s, z, dp, n), zs.at[s, 0], zr.at[s, z], right)),
            (can_left, remote(shard(s, n), block(s, z, dp, n), zs.at[s, 1], zr.at[s, z], left)),
        )

    def pass_z(s, t, n):
        here = block(s, t, dp, n)
        return (
            (can_right & (t < z), remote(here, here, zf.at[s, t], zr.at[s, t], right)),
            (can_left & (t > z), remote(here, here, zf.at[s, t], zr.at[s, t], left)),
        )

    def push_z(s):
        for able, copy in send_z(s, CUT if s == SL - 1 else S):
            pl.when(able)(copy.start)

    def send_block(s, d, src, n):
        t = source(d)
        remote(src, block(s, t, dp, n), os_.at[0, s], xr.at[s, d], (dpx, z)).start()
        remote(src, block(s, t, dp, n), os_.at[1, s], yr.at[s, d], (dpy, z)).start()
        remote(src, block(s, t, dp, n), os_.at[2, s], cr.at[s, d], (dpc, z)).start()

    def pass_core(kind, s, d, i, n):
        here = block(s, source(d), i, n)
        remote(here, here, ks.at[kind - 1, s], cr.at[s, d], (dpc, z)).start()

    def take_z(s, d, n):
        t = source(d)
        remote(shard(s, n), block(s, t, dp, n), zs.at[s, 0], zr.at[s, t], right).wait_recv()
        for able, copy in pass_z(s, t, n):
            pl.when(able)(copy.start)
        send_block(s, d, block(s, t, dp, n), n)

    def take_xy(s, d, n):
        t = source(d)
        fromx, fromy = block(s, t, dpx, n), block(s, t, dpy, n)
        remote(shard(s, n), fromx, os_.at[0, s], xr.at[s, d], (dpx, z)).wait_recv()

        @pl.when(d < T // 2)
        def _():
            remote(fromx, fromx, fs.at[s], dr.at[s, d], (dpy, z)).start()

        pass_core(1, s, d, dpx, n)
        remote(shard(s, n), fromy, os_.at[1, s], yr.at[s, d], (dpy, z)).wait_recv()

        @pl.when(d >= T // 2)
        def _():
            remote(fromy, fromy, fs.at[s], dr.at[s, d], (dpx, z)).start()

        pass_core(2, s, d, dpy, n)

    def take_diag(s, d, n):
        remote(shard(s, n), block(s, source(d), dpxy, n), fs.at[s], dr.at[s, d], (dpx, z)).wait_recv()
        pass_core(3, s, d, dpxy, n)

    def late_to(way, i, who):
        src = PK.at[SL - 1, CUT:S, :] if way < 2 else late(z, i)
        return remote(src, late(z, i), us.at[way], ur.at[way], who)

    chips = (dp, dpx, dpy, dpxy)

    def bundle(t, send, recv, who):
        return [remote(late(t, i), late(t, i), us.at[send], ur.at[recv], who) for i in chips]

    def whole(t, send, recv, who):
        every = W_.at[SL - 1, t, 0:4 * CUT, :]
        return remote(every, every, us.at[send], ur.at[recv], who)

    def late_core(t):
        for copy in bundle(t, 5 + T + t, 3 + T + t, (dpc, z)):
            copy.start()

    def late_start():
        late_to(0, dp, (dpx, z)).start()
        late_to(1, dp, (dpy, z)).start()

    def late_turn():
        late_to(0, dpx, (dpx, z)).wait_recv()
        late_to(2, dpx, (dpy, z)).start()

    def late_along():
        late_to(1, dpy, (dpy, z)).wait_recv()
        late_to(2, dpxy, (dpy, z)).wait_recv()
        for able, send, who in ((can_right, 3, right), (can_left, 4, left)):
            @pl.when(able)
            def _():
                for copy in bundle(z, send, 3 + z, who):
                    copy.start()
        late_core(z)

    def late_pass(t):
        whole(t, 3, 3 + t, right).wait_recv()
        for able, who in ((can_right & (t < z), right), (can_left & (t > z), left)):
            @pl.when(able)
            def _():
                for copy in bundle(t, 5 + t, 3 + t, who):
                    copy.start()
        late_core(t)

    def late_sent():
        for way, who in ((0, dpx), (1, dpy), (2, dpy)):
            late_to(way, dp, (who, z)).wait_send()
        pl.when(can_right)(whole(z, 3, 3, right).wait_send)
        pl.when(can_left)(whole(z, 4, 3, left).wait_send)
        for t in range(T):
            pl.when((can_right & (t < z)) | (can_left & (t > z)))(whole(t, 5 + t, 3, right).wait_send)
            whole(t, 5 + T + t, 3, (dpc, z)).wait_send()

    PIECES = SL * T
    XL, DL = 2, 4
    STEPS = PIECES + DL
    first_steps = DL

    def gather_step(n):
        n = jnp.int32(n)

        def piece(lag, what):
            @pl.when((n >= lag) & (n < PIECES + lag))
            def _():
                s, d = (n - lag) // T, (n - lag) % T
                each(s, lambda size: what(s, d, size))

        def arrive(s, d, size):
            pl.when(d > 0)(lambda: take_z(s, d, size))
            pl.when(d == 0)(lambda: send_block(s, d, shard(s, size), size))

        piece(0, arrive)
        for when, act in LATE:
            pl.when(n == when)(act)
        piece(XL, take_xy)
        piece(DL, take_diag)

    LATE = (
        (0, late_start), (1, late_turn), (3, late_along),
        (6, lambda: late_pass(source(1))), (8, lambda: late_pass(source(2))), (10, lambda: late_pass(source(3))),
    )

    def gathered(s, d):
        n = CUT if s == SL - 1 else S
        four = W_.at[s, source(d), 0:4 * n, :]
        remote(four, four, os_.at[2, s], cr.at[s, d], (dpc, z)).wait_recv()
        if s == SL - 1:
            whole(source(d), 3, 3 + T + source(d), (dpc, z)).wait_recv()

    for s in range(SL):
        push_z(s)
    seq = pl.ds(pl.multiple_of((z % 2) * L, L), L)
    mine = pl.ds(pl.multiple_of((z % 2) * L + own, M), M)
    other = pl.ds(pl.multiple_of((z % 2) * L + oth, M), M)
    tok_out = remote(TOK.at[seq], X, ts.at[0], tr.at[0], (dpc, z))
    cot_out = remote(COT.at[other], CO, ts.at[1], tr.at[1], (dpc, z))
    doc_out = remote(SG.at[0], SG.at[1], ts.at[2], tr.at[2], (dpc, z))
    tok_in = pltpu.make_async_copy(TOK.at[seq], X, loc.at[0])
    cot_in = pltpu.make_async_copy(COT.at[mine], CO, loc.at[1])

    @pl.when(core == home)
    def _():
        for copy in (tok_out, cot_out, doc_out, tok_in, cot_in):
            copy.start()

    for d in range(1, T):
        remote(BP, BI.at[z], bs.at[d - 1], br.at[d - 1], (dp, (z + d) % T)).start()
    for s in range(SL):
        W_[s, z, pl.ds(pl.multiple_of(dp * S, S), S), :] = PK[s]
    BI[z] = BP[...]
    SM[...] = jnp.zeros_like(SM)

    @pl.loop(0, 2)
    def _(n):
        gather_step(n)

    @pl.when(core == home)
    def _():
        tok_in.wait()
        cot_in.wait()
        for copy in (tok_out, cot_out, doc_out):
            copy.wait_send()

    @pl.when(core != home)
    def _():
        for copy in (tok_out, cot_out, doc_out):
            copy.wait_recv()

    for d in range(1, T):
        remote(BP, BI.at[(z - d + T) % T], bs.at[d - 1], br.at[d - 1], (dp, (z + 1) % T)).wait_recv()

    docs = jnp.where(core == home, SG[0], SG[1])
    SG[0] = docs
    key_doc = jnp.broadcast_to(docs[0:1, :], (128, L)).T
    for i in range(M // 128):
        query_doc = SG[0, 0:1, pl.ds(pl.multiple_of(own + i * 128, 128), 128)]
        bias[:, i * 128:(i + 1) * 128] = jnp.where(key_doc == query_doc, 0.0, NEG)

    @pl.loop(2, first_steps)
    def _(n):
        gather_step(n)

    @pl.loop(0, T)
    def _(d):
        gather_step(first_steps + d)
        gathered(0, d)
        t = source(d)
        mine_qkv = nn(X[ownhalf, :], W_[0, t, :, 0:3 * W])
        q[t, :, 0:W] = ((mine_qkv[:, 0:W] + BI[t, 1:2, 0:W]).astype(BF) * BF(scale)).astype(BF)
        k[t, ownhalf, 0:W] = mine_qkv[:, W:2 * W].astype(BF)
        v[t, ownhalf, 0:W] = (mine_qkv[:, 2 * W:3 * W] + BI[t, 2:3, 0:W]).astype(BF)
        their_kv = nn(X[othhalf, :], W_[0, t, :, W:3 * W])
        k[t, othhalf, 0:W] = their_kv[:, 0:W].astype(BF)
        v[t, othhalf, 0:W] = (their_kv[:, W:2 * W] + BI[t, 2:3, 0:W]).astype(BF)

    lane = lax.broadcasted_iota(jnp.int32, (1, 128), 1)

    def head(ref, t, rr, j):
        if j % 2 == 0 and j == NH - 1:
            return ref[t, rr, j * HD:(j + 1) * HD]
        p = j // 2
        return ref[t, rr, p * 128:(p + 1) * 128]

    def only(part, j):
        if part.shape[1] == HD:
            return part
        keep = (lane < HD) if j % 2 == 0 else (lane >= HD)
        return jnp.where(keep, part, jnp.zeros_like(part))

    everything = slice(None)

    @pl.loop(0, T)
    def _(t):
        vT[...] = v[t, :, 0:W].T

        for j in range(NH):
            s = nt(head(k, t, everything, j), only(head(q, t, everything, j), j)) + bias[...]
            m = jnp.max(s, axis=0, keepdims=True)
            p = jnp.exp(s - m)
            l = jnp.sum(p, axis=0, keepdims=True)
            lse[t * 4 + j] = jnp.broadcast_to(m + jnp.log(l), (8, M))
            o = nn(vT[j * HD:(j + 1) * HD, :], p.astype(BF))
            oT[j * HD:(j + 1) * HD, :] = o * (1.0 / l)

        mixed[t, :, 0:W] = oT[...].T.astype(BF)
        gather_step(first_steps + T + t)

    @pl.loop(0, M // RB)
    def _(r):
        zz = X[ownrows(r), :].astype(F32) + NP[0:1, :]
        for t in range(T):
            zz = zz + nt(mixed[t, rows(r), 0:W], W_[0, t, :, 3 * W:4 * W])
        cen = zz - mean_last(zz)
        rs = lax.rsqrt(mean_last(cen * cen) + EPS)
        n = cen * rs
        n1[rows(r), :] = n
        r1[rows(r), :] = jnp.broadcast_to(rs, (RB, 128))
        flow[rows(r), :] = (n * NP[1:2, :] + NP[2:3, :]).astype(BF)

    @pl.loop(0, T)
    def _(d):
        gather_step(first_steps + 2 * T + d)
        gathered(1, d)
        t = source(d)
        inner = nn(flow[...], W_[1, t]) + BI[t, 0:1, :]
        phi = 0.5 * (1.0 + lax.erf(inner * (2.0 ** -0.5)))
        hid[t] = (inner * phi).astype(BF)
        gp[t] = (phi + inner * (jnp.exp(-0.5 * inner * inner) * 0.3989422804014327)).astype(BF)

    gz[...] = n1[...] * NP[1:2, :] + NP[2:3, :] + NP[3:4, :]

    @pl.loop(0, T)
    def _(d):
        gathered(2, d)
        t = source(d)
        gz[...] += nt(hid[t], W_[2, t])

    @pl.loop(0, M // RB)
    def _(r):
        rr = rows(r)
        zz = gz[rr, :]
        cen = zz - mean_last(zz)
        rs = lax.rsqrt(mean_last(cen * cen) + EPS)
        n = cen * rs
        ct = CO[rr, :].astype(F32)
        CO[rr, :] = (n * NP[4:5, :] + NP[5:6, :]).astype(BF)
        g = ct * NP[4:5, :]
        g2 = rs * (g - mean_last(g) - n * mean_last(g * n))
        SM[16:17, :] += colsum(ct * n)
        SM[17:18, :] += colsum(ct)
        SM[13:14, :] += colsum(g2)
        gz[rr, :] = g2
        low[rr, :] = g2.astype(BF)

    dest = dp - core + home

    PARTS = 2
    PR = M // PARTS

    def spotrows(b, cc, part):
        return pl.ds(pl.multiple_of(((b % 2) * 2 + cc) * M + part * PR, PR), PR)

    def spotsem(b, cc, part):
        return ((b % 2) * 2 + cc) * PARTS + part

    def pushes(src, full, sems, recv, parts=range(2)):
        return [
            (able, remote(src.at[pl.ds(part * PR, PR)], full.at[spotrows(z, core, part)],
                          sems.at[i * PARTS + part], recv.at[spotsem(z, core, part)], chip))
            for part in parts
            for i, (able, chip) in enumerate((
                (can_right, (dest, (z + 1) % T)), (can_left, (dest, (z + T - 1) % T)), (core != home, (dpc, z))))
        ]

    def here(src, full, slot):
        rows_ = pl.ds(pl.multiple_of(((z % 2) * 2 + core) * M, M), M)
        return pltpu.make_async_copy(src, full.at[rows_], slot)

    def push(src, full, sems, recv, slot):
        for able, copy in pushes(src, full, sems, recv):
            pl.when(able)(copy.start)
        pl.when(core == home)(here(src, full, slot).start)

    def pushed(src, full, sems, recv, slot):
        for able, copy in pushes(src, full, sems, recv):
            pl.when(able)(copy.wait_send)
        pl.when(core == home)(here(src, full, slot).wait)

    ahead = 1 - 2 * core

    def moves(hop):
        if hop == 0:
            return (z == 1) | (z == 2)
        return z == 2 - core

    def got(src, full, recv, b, cc, part):
        remote(src.at[0:PR], full.at[spotrows(b, cc, part)], gs.at[0], recv.at[spotsem(b, cc, part)], (dpx, z)).wait_recv()

    def handing(full, recv, base, hop, cc, part):
        b = z - ahead * (hop + 1)
        spot_ = full.at[spotrows(b, cc, part)]
        return remote(spot_, spot_, fwd.at[base + (2 * hop + cc) * PARTS + part],
                      recv.at[spotsem(b, cc, part)], (dp, (z + ahead) % T))

    def hand_on(src, full, recv, base, hop, part):
        @pl.when(moves(hop))
        def _():
            for cc in range(2):
                got(src, full, recv, z - ahead * (hop + 1), cc, part)
                handing(full, recv, base, hop, cc, part).start()

    def settle(src, full, recv, base):
        for kk in range(2):
            for cc in range(2):
                b = core * 2 + kk
                gone = (moves(0) & (b == z - ahead)) | (moves(1) & (b == z - 2 * ahead))

                @pl.when(jnp.logical_not((b == z) & (core == cc)) & jnp.logical_not(gone))
                def _():
                    for part in range(PARTS):
                        got(src, full, recv, b, cc, part)

        for hop in range(2):
            @pl.when(moves(hop))
            def _():
                for cc in range(2):
                    for part in range(PARTS):
                        handing(full, recv, base, hop, cc, part).wait_send()

    push(CO, OF, osem, orcv, osl)

    for s in range(SL):
        n = CUT if s == SL - 1 else S
        for able, copy in send_z(s, n):
            pl.when(able)(copy.wait_send)
        for t in range(T):
            for able, copy in pass_z(s, t, n):
                pl.when(able)(copy.wait_send)
        four = W_.at[s, z, 0:4 * n, :]
        for kind in range(3):
            remote(four, four, os_.at[kind, s], xr.at[s, 0], (dpx, z)).wait_send()
            remote(four, four, ks.at[kind, s], xr.at[s, 0], (dpx, z)).wait_send()
        remote(four, four, fs.at[s], xr.at[s, 0], (dpx, z)).wait_send()
    late_sent()
    for d in range(1, T):
        remote(BP, BI.at[z], bs.at[d - 1], br.at[d - 1], (dp, (z + d) % T)).wait_send()

    def grad(s):
        return W_.at[s]

    rel = (dp, dpx, dpy, dpxy)

    def rowsof(i):
        return pl.ds(pl.multiple_of(i * S, S), S)

    def core_copy(s, kk):
        return remote(grad(s).at[:, rowsof(rel[kk] + flip), :], rc.at[s, kk], cs.at[s], crr.at[s, kk], (dpc, z))

    def turn(s, kk):
        src, dst, who = (
            (rc.at[s, 3, 0:2], ra.at[s, 0], (dpy, z)),
            (rc.at[s, 3, 2:4], ra.at[s, 1], (dpx, z)),
        )[kk]
        return remote(src, dst, s1.at[s, kk], q1.at[s, kk], who)

    def straight(s, kk):
        src, dst, who = (
            (rc.at[s, 1, 2:4], rb.at[s, 0, 2:4], (dpx, z)),
            (rc.at[s, 2, 0:2], rb.at[s, 1, 0:2], (dpy, z)),
            (rc.at[s, 1, 0:2], rb.at[s, 0, 0:2], (dpx, z)),
            (rc.at[s, 2, 2:4], rb.at[s, 1, 2:4], (dpy, z)),
        )[kk]
        return remote(src, dst, s2.at[s, kk], q2.at[s, kk], who)

    def along(s, t, sign):
        way = (1 - sign) // 2
        return remote(rc.at[s, 0, t], rz.at[s, way, t], s3.at[s, way, t], q3.at[s, way, t], (dp, (z + sign + T) % T))

    def add(dst, src):
        @pl.loop(0, dst.shape[0])
        def _(t):
            dst[t] = (dst[t].astype(F32) + src[t].astype(F32)).astype(BF)

    def sum_start(s):
        for kk in (3, 1, 2, 0):
            core_copy(s, kk).start()

    def sum_core(s):
        for kk in (3, 1, 2, 0):
            core_copy(s, kk).wait_recv()
            add(rc.at[s, kk], grad(s).at[:, rowsof(rel[kk]), :])
            if kk == 3:
                turn(s, 0).start()
                turn(s, 1).start()
            if kk == 1:
                straight(s, 0).start()
            if kk == 2:
                straight(s, 1).start()

    def sum_turn(s):
        turn(s, 0).wait_recv()
        add(rc.at[s, 1, 0:2], ra.at[s, 0])
        straight(s, 2).start()
        turn(s, 1).wait_recv()
        add(rc.at[s, 2, 2:4], ra.at[s, 1])
        straight(s, 3).start()

    def sum_straight(s):
        for kk in range(4):
            straight(s, kk).wait_recv()
        add(rc.at[s, 0], rb.at[s, 0])
        add(rc.at[s, 0], rb.at[s, 1])

    def sum_along(s):
        @pl.loop(0, 2)
        def _(i):
            sign = (1 - 2 * half) * (1 - 2 * i)
            way = (1 - sign) // 2
            behind = z - sign

            @pl.loop(0, T - 1)
            def _(j):
                t = (1 - way) * (T - 1 - j) + way * j

                @pl.when((t - z) * sign > 0)
                def _():
                    @pl.when((behind >= 0) & (behind < T))
                    def _():
                        along(s, t, sign).wait_recv()
                        rc[s, 0, t] = (rc[s, 0, t].astype(F32) + rz[s, way, t].astype(F32)).astype(BF)

                    along(s, t, sign).start()

    def sum_last(s):
        GR[s] = rc[s, 0, z].astype(F32)
        for sign in (1, -1):
            @pl.when((z - sign >= 0) & (z - sign < T))
            def _():
                along(s, z, sign).wait_recv()
                GR[s] += rz[s, (1 - sign) // 2, z].astype(F32)

    def sum_sent(s):
        for sign in (1, -1):
            for t in range(T):
                pl.when((t - z) * sign > 0)(along(s, t, sign).wait_send)

    xT[:, 0:M] = low[...].T
    xT[:, M:L] = flow[...].T

    @pl.loop(0, T)
    def _(t):
        gi = (nn(low[...], W_[2, t]) * gp[t].astype(F32)).astype(BF)
        gp[t] = gi
        SM[pl.ds(2 * T + t, 1), :] += colsum(gi.astype(F32))
        gz[...] += nt(gi, W_[1, t])
        W_[2, t] = nn(xT[:, 0:M], hid[t]).astype(BF)
        W_[1, t] = nn(xT[:, M:L], gi).astype(BF)

    hand_on(CO, OF, orcv, 0, 0, 0)
    sum_start(2)
    sum_start(1)

    @pl.loop(0, M // RB)
    def _(r):
        rr = rows(r)
        gf = gz[rr, :]
        n = n1[rr, :]
        g = gf * NP[1:2, :]
        g1 = r1[rr, 0:1] * (g - mean_last(g) - n * mean_last(g * n))
        SM[14:15, :] += colsum(gf * n)
        SM[15:16, :] += colsum(gf)
        SM[12:13, :] += colsum(g1)
        gz[rr, :] = g1
        low[rr, :] = g1.astype(BF)

    xT[:, 0:M] = low[...].T

    @pl.loop(0, T)
    def _(t):
        hid[t, :, 0:W] = nn(low[...], W_[0, t, :, 3 * W:4 * W]).astype(BF)

    @pl.loop(0, T)
    def _(t):
        @pl.when(t == 0)
        def _():
            sum_core(2)
            hand_on(CO, OF, orcv, 0, 0, 1)

        @pl.when(t == 1)
        def _():
            sum_core(1)

        @pl.when(t == 2)
        def _():
            sum_turn(2)
            hand_on(CO, OF, orcv, 0, 1, 0)

        @pl.when(t == 3)
        def _():
            sum_turn(1)
            hand_on(CO, OF, orcv, 0, 1, 1)

        vT[...] = k[t, :, 0:W].T
        for pair in range((NH + 1) // 2):
            heads = [j for j in (2 * pair, 2 * pair + 1) if j < NH]
            wide = HD * len(heads)
            dk = jnp.zeros((L, wide), F32)
            dv = jnp.zeros((L, wide), F32)
            for j in heads:
                for i in range(M // QC):
                    qs = slice(i * QC, (i + 1) * QC)
                    qm = only(head(q, t, qs, j), j)
                    om = only(head(hid, t, qs, j), j)
                    s = nt(head(k, t, everything, j), qm) + bias[:, qs]
                    p = jnp.exp(s - lse[t * 4 + j, 0:1, qs])
                    dpr = nt(head(v, t, everything, j), om)
                    cen = jnp.sum(p * dpr, axis=0, keepdims=True)
                    ds = (p * (dpr - cen)).astype(BF)
                    dv = dv + nn(p.astype(BF), om)
                    dk = dk + nn(ds, qm)
                    oT[j * HD:(j + 1) * HD, qs] = nn(vT[j * HD:(j + 1) * HD, :], ds) * scale
            lanes = slice(pair * 128, pair * 128 + wide)
            k[t, :, lanes] = dk.astype(BF)
            v[t, :, lanes] = dv.astype(BF)
        dq = oT[...].T.astype(BF)
        q[t, :, 0:W] = dq
        SM[pl.ds(t, 1), 0:W] += colsum(dq.astype(F32))
        SM[pl.ds(T + t, 1), 0:W] += colsum(v[t, :, 0:W].astype(F32))

    def share(r):
        return remote(flow.at[rows(r)], rgt.at[rows(r)], gs.at[r], gr.at[r], (dpc, z))

    @pl.loop(0, M // RB)
    def _(r):
        acc = jnp.zeros((RB, D), F32)
        for t in range(T):
            acc = acc + nt(k[t, othrows(r), 0:W], W_[0, t, :, W:2 * W])
            acc = acc + nt(v[t, othrows(r), 0:W], W_[0, t, :, 2 * W:3 * W])
        flow[rows(r), :] = acc.astype(BF)
        share(r).start()


    @pl.loop(0, M // RB)
    def _(r):
        acc = gz[rows(r), :]
        for t in range(T):
            acc = acc + nt(q[t, rows(r), 0:W], W_[0, t, :, 0:W])
            acc = acc + nt(k[t, ownrows(r), 0:W], W_[0, t, :, W:2 * W])
            acc = acc + nt(v[t, ownrows(r), 0:W], W_[0, t, :, 2 * W:3 * W])
        share(r).wait_recv()
        low[rows(r), :] = (acc + rgt[rows(r), :].astype(F32)).astype(BF)
        for part in range(PARTS):
            @pl.when(r == part)
            def _():
                for able, copy in pushes(low, GF, gsem, grcv, (part,)):
                    pl.when(able)(copy.start)

    pl.when(core == home)(here(low, GF, gsl).start)

    pals = [(dpc, z), (dpx, z), (dpy, z), (dp, z + 1 - 2 * (z % 2)), (dp, (z + 2) % T)]

    def small(step):
        return remote(ssend.at[step], srecv.at[step], ms.at[step], mr.at[step], pals[step])

    def small_start(step):
        ssend[step] = SM[...]
        small(step).start()

    def small_end(step):
        small(step).wait_recv()
        SM[...] += srecv[step]

    small_start(0)

    @pl.loop(0, T)
    def _(t):
        W_[0, t, :, 3 * W:4 * W] = nn(xT[:, 0:M], mixed[t, :, 0:W]).astype(BF)

    xT[...] = X[...].T

    @pl.loop(0, T)
    def _(t):
        W_[0, t, :, 0:W] = nn(xT[:, pl.ds(pl.multiple_of(own, 128), M)], q[t, :, 0:W]).astype(BF)
        W_[0, t, :, W:2 * W] = nn(xT[...], k[t, :, 0:W]).astype(BF)
        W_[0, t, :, 2 * W:3 * W] = nn(xT[...], v[t, :, 0:W]).astype(BF)

    sum_start(0)
    hand_on(low, GF, grcv, 8, 0, 0)
    small_end(0)
    small_start(1)
    sum_core(0)
    hand_on(low, GF, grcv, 8, 0, 1)
    small_end(1)
    small_start(2)
    sum_straight(2)
    sum_turn(0)
    hand_on(low, GF, grcv, 8, 1, 0)
    sum_along(2)
    small_end(2)
    small_start(3)
    sum_straight(1)
    hand_on(low, GF, grcv, 8, 1, 1)
    sum_along(1)
    small_end(3)
    small_start(4)
    sum_straight(0)
    sum_along(0)
    small_end(4)
    for s in (2, 1, 0):
        sum_last(s)
    SMO[...] = SM[...]
    settle(CO, OF, orcv, 0)
    settle(low, GF, grcv, 8)
    pushed(CO, OF, osem, orcv, osl)
    pushed(low, GF, gsem, grcv, gsl)
    share(0).wait_send()
    share(1).wait_send()
    for step in range(5):
        small(step).wait_send()
    for s in range(SL):
        for kk in range(4):
            straight(s, kk).wait_send()
        remote(rc.at[s], rc.at[s], cs.at[s], crr.at[s, 0], (dpc, z)).wait_send()
        turn(s, 0).wait_send()
        turn(s, 1).wait_send()
        sum_sent(s)


def layer_call(weights, vectors, lengths, tokens, cotangent, T):
    wq, w1 = weights[0], weights[4]
    S, W = wq.shape
    D = tokens.shape[1]
    F = w1.shape[1]
    L = tokens.shape[0] // lengths.shape[0]
    M = L // 2
    SL = 3
    WP = 256
    any_ = pl.BlockSpec(memory_space=pl.ANY)
    vm = pl.BlockSpec(memory_space=pltpu.VMEM)
    dma = pltpu.SemaphoreType.DMA
    f32 = lambda *s: jax.ShapeDtypeStruct(s, F32)
    V = pltpu.VMEM
    return pl.pallas_call(
        layer_kernel,
        in_specs=[vm] * (len(weights) + len(vectors)) + [pl.BlockSpec(memory_space=pltpu.SMEM), any_, any_],
        out_specs=[any_, any_, vm, vm],
        out_shape=[
            jax.ShapeDtypeStruct((4 * M, D), BF),
            jax.ShapeDtypeStruct((4 * M, D), BF),
            f32(SL, S, D), f32(24, D),
        ],
        scratch_shapes=[
            V((SL, S, D), BF),
            V((SL, T, D, F), BF),
            V((L, D), BF),
            V((M, D), BF),
            V((2, 8, L), F32),
            V((8, D), F32),
            V((8, D), F32),
            V((T, 8, D), F32),
            V((24, D), F32),
            V((T, M, WP), BF),
            V((T, L, WP), BF),
            V((T, L, WP), BF),
            V((T, M, WP), BF),
            V((W, L), BF),
            V((W, M), F32),
            V((T * 4, 8, M), F32),
            V((L, M), F32),
            V((M, D), F32),
            V((M, 128), F32),
            V((M, D), BF),
            V((T, M, F), BF),
            V((T, M, F), BF),
            V((M, D), F32),
            V((M, D), BF),
            V((D, L), BF),
            V((M, D), BF),
            V((SL, 4, T, S, D), BF),
            V((SL, 2, 2, S, D), BF),
            V((SL, 2, T, S, D), BF),
            V((SL, 2, T, S, D), BF),
            V((5, 24, D), F32),
            V((5, 24, D), F32),
            dma((2,)),
            dma((5 + 2 * T,)), dma((3 + 2 * T,)),
            dma((SL, 2)), dma((SL, T)), dma((SL, T)),
            dma((3, SL)), dma((SL, T)), dma((SL, T)), dma((SL, T)),
            dma((SL,)), dma((SL, T)),
            dma((3, SL)),
            dma((T - 1,)), dma((T - 1,)),
            dma((3,)), dma((3,)),
            dma((2,)), dma((2,)),
            dma((6,)), dma((8,)), dma,
            dma((6,)), dma((8,)), dma,
            dma((16,)),
            dma((SL,)), dma((SL, 4)),
            dma((SL, 2)), dma((SL, 2)),
            dma((SL, 4)), dma((SL, 4)),
            dma((SL, 2, T)), dma((SL, 2, T)),
            dma((5,)), dma((5,)),
        ],
        compiler_params=pltpu.CompilerParams(
            collective_id=0, has_side_effects=True, vmem_limit_bytes=64 << 20
        ),
    )(*weights, *vectors, lengths, tokens, cotangent)


def finish_kernel(OF, GF, GR, SMO, OUT, GT, *rest):
    outs, (keep, gr, sm, *bufs, came, went, read, wrote) = rest[:15], rest[15:]
    z = lax.axis_index("tensor")
    T = lax.axis_size("tensor")
    W = bufs[0].shape[1]
    small = [pltpu.make_async_copy(GR, gr, read.at[0]), pltpu.make_async_copy(SMO, sm, read.at[1])]
    n, size = keep.shape[1:3]
    ins, backs = [], []
    for a, (src, dst) in enumerate(((GF, GT), (OF, OUT))):
        for i in range(n):
            part = pl.ds(i * size, size)
            ins.append(pltpu.make_async_copy(src.at[part], keep.at[a, i], came.at[a, i]))
            backs.append(pltpu.make_async_copy(keep.at[a, i], dst.at[part], went.at[a, i]))
    for copy in small + ins:
        copy.start()
    for copy in small:
        copy.wait()
    dq, dk, dv, do, bq, bv, b1 = bufs[:7]
    dq[...] = gr[0, :, 0:W]
    dk[...] = gr[0, :, W:2 * W]
    dv[...] = gr[0, :, 2 * W:3 * W]
    do[...] = gr[0, :, 3 * W:4 * W].T
    bq[...] = sm[pl.ds(z, 1), 0:W].reshape(W)
    bv[...] = sm[pl.ds(T + z, 1), 0:W].reshape(W)
    b1[...] = sm[pl.ds(2 * T + z, 1), :].reshape(b1.shape[0])
    for i, ref in zip((0, 2, 3, 1, 4, 5), bufs[7:]):
        ref[...] = sm[3 * T + i:3 * T + i + 1, :].reshape(ref.shape[0])
    sources = [dq, dk, dv, do, gr.at[1], gr.at[2], *bufs[4:]]
    writes = [pltpu.make_async_copy(src, dst, wrote.at[i]) for i, (src, dst) in enumerate(zip(sources, outs))]
    for copy in writes:
        copy.start()
    for a, b in zip(ins, backs):
        a.wait()
        b.start()
    for copy in backs + writes:
        copy.wait()


def finish_call(full, grads, gr, sm, T):
    SL, S, D = gr.shape
    W = D // T
    n = 4
    any_ = pl.BlockSpec(memory_space=pltpu.HBM)
    f32 = lambda *s: jax.ShapeDtypeStruct(s, F32)
    same = jax.ShapeDtypeStruct(full.shape, full.dtype)
    made = [(S, W), (S, W), (S, W), (W, S), (W,), (W,), (D,), (D,), (D,), (D,), (D,), (D,), (D,)]
    dma = pltpu.SemaphoreType.DMA
    return pl.pallas_call(
        finish_kernel,
        in_specs=[any_] * 4,
        out_specs=[any_] * 17,
        out_shape=[same, same] + [f32(*m) for m in made[:4]] + [f32(S, D), f32(S, D)] + [f32(*m) for m in made[4:]],
        scratch_shapes=[
            pltpu.VMEM((2, n, full.shape[0] // n, D), BF), pltpu.VMEM(gr.shape, F32), pltpu.VMEM(sm.shape, F32),
            *[pltpu.VMEM(m, F32) for m in made],
            dma((2, n)), dma((2, n)), dma((2,)), dma((15,)),
        ],
        compiler_params=pltpu.CompilerParams(vmem_limit_bytes=64 << 20),
    )(full, grads, gr, sm)


def doc_ids(lengths, count):
    ends = jnp.cumsum(lengths)
    places = jnp.arange(count, dtype=jnp.int32)
    return jnp.sum((places[:, None] >= ends[None, :]).astype(jnp.int32), axis=1)


def collect(wq, wk, wv, wo, w1, w2):
    return (
        lax.all_gather(wq, "dp", axis=0, tiled=True),
        lax.all_gather(wk, "dp", axis=0, tiled=True),
        lax.all_gather(wv, "dp", axis=0, tiled=True),
        lax.all_gather(wo, "dp", axis=1, tiled=True),
        lax.all_gather(w1, "dp", axis=0, tiled=True),
        lax.all_gather(w2, "dp", axis=1, tiled=True),
    )


def reduce_large(grads):
    return (
        lax.psum_scatter(grads[0], "dp", scatter_dimension=0, tiled=True),
        lax.psum_scatter(grads[1], "dp", scatter_dimension=0, tiled=True),
        lax.psum_scatter(grads[2], "dp", scatter_dimension=0, tiled=True),
        lax.psum_scatter(grads[3], "dp", scatter_dimension=1, tiled=True),
        lax.psum_scatter(grads[4], "dp", scatter_dimension=0, tiled=True),
        lax.psum_scatter(grads[5], "dp", scatter_dimension=1, tiled=True),
    )


def reduce_small(grads):
    return lax.psum(
        (grads[0], grads[1], grads[2], grads[3], grads[4], grads[5], grads[6], grads[7], grads[8]),
        "dp",
    )


def contract_rows(left, right):
    return lax.dot_general(
        left, right, (((0,), (0,)), ((), ())), preferred_element_type=jnp.float32
    )


def contract_cols(left, right):
    return lax.dot_general(
        left, right, (((1,), (1,)), ((), ())), preferred_element_type=jnp.float32
    )


def contract_mixed(left, right):
    return lax.dot_general(
        left, right, (((0,), (1,)), ((), ())), preferred_element_type=jnp.float32
    )


def norm_forward(total, gain, shift):
    centre = total - jnp.mean(total, axis=-1, keepdims=True)
    scaled = lax.rsqrt(jnp.mean(centre * centre, axis=-1, keepdims=True) + EPS)
    normed = centre * scaled
    return (normed * gain + shift, normed, scaled)


def norm_backward(grad_result, normed, scaled, gain):
    grad_normed = grad_result * gain
    mean_grad = jnp.mean(grad_normed, axis=-1, keepdims=True)
    mean_cross = jnp.mean(grad_normed * normed, axis=-1, keepdims=True)
    grad_total = scaled * (grad_normed - mean_grad - normed * mean_cross)
    return (grad_total, jnp.sum(grad_result * normed, axis=0), jnp.sum(grad_result, axis=0))


def block_scores(query_block, key_heads, seg_block, seg, scale):
    raw = (
        jnp.einsum("hdq,hdk->hqk", query_block, key_heads, preferred_element_type=jnp.float32)
        * scale
    )
    same_doc = seg_block[:, None] == seg[None, :]
    return jnp.where(same_doc[None], raw, NEG)


def general_body(
    tokens,
    doc_lengths,
    wq,
    bq,
    wk,
    wv,
    bv,
    wo,
    bo,
    gain1,
    shift1,
    w1,
    b1,
    w2,
    b2,
    gain2,
    shift2,
    cotangent,
):
    micro = doc_lengths.shape[0]
    seq_len = tokens.shape[0] // micro
    block = min(512, seq_len)
    scale = HD ** (-0.5)
    results = []
    grad_inputs = []
    large_total = None
    small_total = None
    for index in range(micro):
        full = collect(wq, wk, wv, wo, w1, w2)
        full_q, full_k, full_v, full_o, full_first, full_second = full
        width = full_q.shape[1]
        heads_here = width // HD
        rows_in = tokens[index * seq_len : (index + 1) * seq_len]
        inputs = rows_in.astype(jnp.float32)
        seg = doc_ids(doc_lengths[index], seq_len)
        queries = (
            lax.dot_general(
                full_q, rows_in, (((0,), (1,)), ((), ())), preferred_element_type=jnp.float32
            )
            + bq[:, None]
        ).astype(jnp.bfloat16)
        keys_low = lax.dot_general(
            full_k, rows_in, (((0,), (1,)), ((), ())), preferred_element_type=jnp.float32
        ).astype(jnp.bfloat16)
        values_low = (
            lax.dot_general(
                full_v, rows_in, (((0,), (1,)), ((), ())), preferred_element_type=jnp.float32
            )
            + bv[:, None]
        ).astype(jnp.bfloat16)
        query_heads = queries.reshape(heads_here, HD, seq_len)
        key_heads = keys_low.reshape(heads_here, HD, seq_len)
        value_heads = values_low.reshape(heads_here, HD, seq_len)
        pieces = []
        log_totals = []
        for offset in range(0, seq_len, block):
            scores = block_scores(
                query_heads[:, :, offset : offset + block],
                key_heads,
                seg[offset : offset + block],
                seg,
                scale,
            )
            highest = jnp.max(scores, axis=-1, keepdims=True)
            log_total = highest + jnp.log(
                jnp.sum(jnp.exp(scores - highest), axis=-1, keepdims=True)
            )
            probs_low = jnp.exp(scores - log_total).astype(jnp.bfloat16)
            pieces.append(
                jnp.einsum(
                    "hqk,hdk->hdq", probs_low, value_heads, preferred_element_type=jnp.float32
                )
            )
            log_totals.append(log_total)
        mixed_cols = jnp.concatenate(pieces, axis=2).reshape(width, seq_len).astype(jnp.bfloat16)
        attended = lax.psum(
            contract_rows(mixed_cols, full_o).astype(jnp.bfloat16), "tensor"
        ).astype(jnp.float32)
        first, normed_one, scaled_one = norm_forward(inputs + attended + bo, gain1, shift1)
        first_low = first.astype(jnp.bfloat16)
        inner = jnp.dot(first_low, full_first, preferred_element_type=jnp.float32) + b1
        hidden = jax.nn.gelu(inner, approximate=False).astype(jnp.bfloat16)
        second = lax.psum(
            jnp.dot(hidden, full_second, preferred_element_type=jnp.float32).astype(jnp.bfloat16),
            "tensor",
        ).astype(jnp.float32)
        result, normed_two, scaled_two = norm_forward(first + second + b2, gain2, shift2)
        results.append(result.astype(jnp.bfloat16))
        grad_result = cotangent[index * seq_len : (index + 1) * seq_len].astype(jnp.float32)
        grad_two, grad_gain2, grad_shift2 = norm_backward(
            grad_result, normed_two, scaled_two, gain2
        )
        grad_b2 = jnp.sum(grad_two, axis=0)
        full = collect(wq, wk, wv, wo, w1, w2)
        full_q, full_k, full_v, full_o, full_first, full_second = full
        two_low = grad_two.astype(jnp.bfloat16)
        grad_w2 = contract_rows(hidden, two_low)
        grad_hidden = contract_cols(two_low, full_second)
        grad_inner = jax.vjp(partial(jax.nn.gelu, approximate=False), inner)[1](grad_hidden)[
            0
        ].astype(jnp.bfloat16)
        grad_b1 = jnp.sum(grad_inner.astype(jnp.float32), axis=0)
        grad_w1 = contract_rows(first_low, grad_inner)
        grad_first = grad_two + lax.psum(
            contract_cols(grad_inner, full_first).astype(jnp.bfloat16), "tensor"
        ).astype(jnp.float32)
        grad_one, grad_gain1, grad_shift1 = norm_backward(grad_first, normed_one, scaled_one, gain1)
        grad_bo = jnp.sum(grad_one, axis=0)
        one_low = grad_one.astype(jnp.bfloat16)
        grad_wo = jnp.dot(mixed_cols, one_low, preferred_element_type=jnp.float32)
        grad_mixed = (
            contract_cols(full_o, one_low).astype(jnp.bfloat16).reshape(heads_here, HD, seq_len)
        )
        grad_key_heads = jnp.zeros((heads_here, HD, seq_len), jnp.float32)
        grad_value_heads = jnp.zeros((heads_here, HD, seq_len), jnp.float32)
        grad_query_pieces = []
        for number, offset in enumerate(range(0, seq_len, block)):
            query_block = query_heads[:, :, offset : offset + block]
            grad_block = grad_mixed[:, :, offset : offset + block]
            scores = block_scores(query_block, key_heads, seg[offset : offset + block], seg, scale)
            probs = jnp.exp(scores - log_totals[number])
            grad_probs = jnp.einsum(
                "hdq,hdk->hqk", grad_block, value_heads, preferred_element_type=jnp.float32
            )
            centre = jnp.sum(probs * grad_probs, axis=-1, keepdims=True)
            grad_scores = (probs * (grad_probs - centre)).astype(jnp.bfloat16)
            grad_query_pieces.append(
                jnp.einsum(
                    "hqk,hdk->hdq", grad_scores, key_heads, preferred_element_type=jnp.float32
                )
                * scale
            )
            grad_key_heads = (
                grad_key_heads
                + jnp.einsum(
                    "hqk,hdq->hdk", grad_scores, query_block, preferred_element_type=jnp.float32
                )
                * scale
            )
            grad_value_heads = grad_value_heads + jnp.einsum(
                "hqk,hdq->hdk",
                probs.astype(jnp.bfloat16),
                grad_block,
                preferred_element_type=jnp.float32,
            )
        grad_queries = (
            jnp.concatenate(grad_query_pieces, axis=2).reshape(width, seq_len).astype(jnp.bfloat16)
        )
        grad_keys = grad_key_heads.reshape(width, seq_len).astype(jnp.bfloat16)
        grad_values = grad_value_heads.reshape(width, seq_len).astype(jnp.bfloat16)
        grad_bq = jnp.sum(grad_queries.astype(jnp.float32), axis=1)
        grad_bv = jnp.sum(grad_values.astype(jnp.float32), axis=1)
        grad_wq = contract_cols(rows_in.T, grad_queries)
        grad_wk = contract_cols(rows_in.T, grad_keys)
        grad_wv = contract_cols(rows_in.T, grad_values)
        back_terms = (
            contract_mixed(grad_queries, full_q)
            + contract_mixed(grad_keys, full_k)
            + contract_mixed(grad_values, full_v)
        )
        grad_rows = grad_one + lax.psum(back_terms.astype(jnp.bfloat16), "tensor").astype(
            jnp.float32
        )
        grad_inputs.append(grad_rows.astype(jnp.bfloat16))
        large_local = (grad_wq, grad_wk, grad_wv, grad_wo, grad_w1, grad_w2)
        small_local = (
            grad_bq,
            grad_bv,
            grad_b1,
            grad_bo,
            grad_b2,
            grad_gain1,
            grad_shift1,
            grad_gain2,
            grad_shift2,
        )
        large_local = reduce_large(large_local)
        small_local = reduce_small(small_local)
        if large_total is None:
            large_total = large_local
            small_total = small_local
        else:
            large_total = jax.tree.map(jnp.add, large_total, large_local)
            small_total = jax.tree.map(jnp.add, small_total, small_local)
    grad_wq, grad_wk, grad_wv, grad_wo, grad_w1, grad_w2 = large_total
    (
        grad_bq,
        grad_bv,
        grad_b1,
        grad_bo,
        grad_b2,
        grad_gain1,
        grad_shift1,
        grad_gain2,
        grad_shift2,
    ) = small_total
    return (
        jnp.concatenate(results, axis=0),
        jnp.concatenate(grad_inputs, axis=0),
        grad_wq,
        grad_bq,
        grad_wk,
        grad_wv,
        grad_bv,
        grad_wo,
        grad_bo,
        grad_gain1,
        grad_shift1,
        grad_w1,
        grad_b1,
        grad_w2,
        grad_b2,
        grad_gain2,
        grad_shift2,
    )


def split_body(T, tokens, doc_lengths, wq, bq, wk, wv, bv, wo, bo, gain1, shift1, w1, b1, w2, b2,
               gain2, shift2, cotangent):
    weights = (wq, wk, wv, wo, w1, w2.T)
    vectors = (bo, gain1, shift1, b2, gain2, shift2, b1, bq, bv)
    (full, grads, dq, dk, dv, do, d1, d2, gbq, gbv, gb1, gbo, gg1, gs1, gb2, gg2, gs2) = finish_call(
        *layer_call(weights, vectors, doc_lengths, tokens, cotangent, T), T)
    return full, grads, dq, gbq, dk, dv, gbv, do, gbo, gg1, gs1, d1, gb1, d2.T, gb2, gg2, gs2


def solution(mesh):
    placed = (
        P("dp", None),
        P("dp", None),
        P("dp", "tensor"),
        P("tensor"),
        P("dp", "tensor"),
        P("dp", "tensor"),
        P("tensor"),
        P("tensor", "dp"),
        P(),
        P(),
        P(),
        P("dp", "tensor"),
        P("tensor"),
        P("tensor", "dp"),
        P(),
        P(),
        P(),
        P("dp", None),
    )
    if mesh.shape["dp"] == 8 and mesh.shape["tensor"] == 4:
        body = partial(split_body, mesh.shape["tensor"])
    else:
        body = general_body
    return jax.shard_map(
        body,
        mesh=mesh,
        in_specs=placed,
        out_specs=(
            P("dp", None),
            P("dp", None),
            P("dp", "tensor"),
            P("tensor"),
            P("dp", "tensor"),
            P("dp", "tensor"),
            P("tensor"),
            P("tensor", "dp"),
            P(),
            P(),
            P(),
            P("dp", "tensor"),
            P("tensor"),
            P("tensor", "dp"),
            P(),
            P(),
            P(),
        ),
        check_vma=False,
    )
```
